32 devices in a mesh: fsdp: 4 (over y, x), ctx: 2 (over core), tp: 4 (over z).
Axes of the slice: x: 2, y: 2, z: 4, core: 2. Of those that a mesh axis runs over, the one named last changes fastest.
Arguments:
- hidden_in: bfloat16 [2, 4, 1024, 768], P(None, 'fsdp', 'ctx'), may hold values from -2.5 to 2.5
- cond_vec: bfloat16 [2, 4, 128], P(None, 'fsdp'), may hold values from -2.5 to 2.5
- segment_ids: int32 [2, 4, 1024], P(None, 'fsdp'), may hold values from 0 to 17, as said below
- pad_mask: int32 [2, 4, 1024], P(None, 'fsdp'), may hold values from 0 to 1, as said below
- out_cot: bfloat16 [2, 4, 1024, 768], P(None, 'fsdp', 'ctx'), may hold values from -8 to 8
- qkv_weight: bfloat16 [3, 768, 768], P(None, ('fsdp', 'ctx'), 'tp'), may hold values from -0.21875 to 0.21875
- attn_weight: bfloat16 [768, 768], P('tp', ('fsdp', 'ctx')), may hold values from -1.5 to 1.5
- up_weight: bfloat16 [768, 3072], P(('fsdp', 'ctx'), 'tp'), may hold values from -0.21875 to 0.21875
- up_bias: bfloat16 [3072], P(('tp', 'fsdp', 'ctx')), may hold values from -1.25 to 1.25
- down_weight: bfloat16 [3072, 768], P('tp', ('fsdp', 'ctx')), may hold values from -0.109375 to 0.109375
- down_bias: bfloat16 [768], P(('fsdp', 'ctx')), may hold values from -0.75 to 0.75
- ada_weight: bfloat16 [128, 4608], P(None, ('fsdp', 'ctx')), may hold values from -0.099609375 to 0.099609375
- ada_bias: bfloat16 [4608], P(('fsdp', 'ctx')), may hold values from -0.75 to 0.75
- attn_norm: bfloat16 [768], P(('fsdp', 'ctx')), may hold values from 0.5 to 1.5
- mlp_norm: bfloat16 [768], P(('fsdp', 'ctx')), may hold values from 0.5 to 1.5
Outputs:
- block_out: bfloat16 [2, 4, 1024, 768], P(None, 'fsdp', 'ctx')
- hidden_grad: float32 [2, 4, 1024, 768], P(None, 'fsdp', 'ctx')
- cond_grad: float32 [2, 4, 128], P(None, 'fsdp')
- grad_qkv: float32 [3, 768, 768], P(None, ('fsdp', 'ctx'), 'tp')
- grad_attn: float32 [768, 768], P('tp', ('fsdp', 'ctx'))
- grad_up: float32 [768, 3072], P(('fsdp', 'ctx'), 'tp')
- grad_upbias: float32 [3072], P(('tp', 'fsdp', 'ctx'))
- grad_down: float32 [3072, 768], P('tp', ('fsdp', 'ctx'))
- grad_downbias: float32 [768], P(('fsdp', 'ctx'))
- grad_ada: float32 [128, 4608], P(None, ('fsdp', 'ctx'))
- grad_adabias: float32 [4608], P(('fsdp', 'ctx'))
- grad_attnnorm: float32 [768], P(('fsdp', 'ctx'))
- grad_mlpnorm: float32 [768], P(('fsdp', 'ctx'))
The draws below stay inside these ranges and needn't reach their ends.
Inputs may be any that keep to these rules, and one draw needn't show every extreme that they name: `segment_ids`: within a sequence the numbers start at 0, rise by one at the start of each document and never fall; every document has 60 to 800 tokens; padding, where a sequence has some, is its last segment. In every micro-batch some sequence reaches the largest number, 17. `pad_mask`: 0 exactly on the padding tokens that end a sequence, 1 elsewhere.
All inputs are finite; a program needn't handle non-finite values.
Results may differ from the reference program's by a relative error of at most 0.012.
The reference program's roundings to bfloat16 on the way count: a program that leaves them out, or rounds other values in their place, can miss the bound.
Values may be sent and summed in bfloat16 or wider, within the bound.
No kernel may reach another device: no remote copies, remote signals or barrier semaphores. Data moves between devices by JAX's collectives and lax.ppermute only.
A program may use at most 128 MiB of HBM per device.

```python
import math
import jax
import jax.numpy as jnp
from jax import lax

D = 768
HEADS = 12
HEAD_DIM = 64
FF = 3072
CD = 128
SEQ = 1024
MB = 2
DOC_MIN = 60
DOC_MAX = 800
BATCH = 4


def document_layout(key):
    doc_count = SEQ // DOC_MIN + 1
    lengths = jax.random.randint(jax.random.fold_in(key, 11), (MB, BATCH, doc_count), DOC_MIN, DOC_MAX + 1, dtype=jnp.int32)
    first_row = (jnp.arange(BATCH, dtype=jnp.int32) == 0)[None, :, None]
    lengths = jnp.where(first_row, jnp.int32(DOC_MIN), lengths).astype(jnp.int32)
    doc_ends = jnp.cumsum(lengths, axis=-1)
    fitted = jnp.where(doc_ends <= SEQ, doc_ends, 0)
    last_end = jnp.max(fitted, axis=-1)
    places = jnp.arange(SEQ, dtype=jnp.int32)
    passed = (fitted[:, :, None, :] > 0) & (fitted[:, :, None, :] <= places[None, None, :, None])
    segments = jnp.sum(passed.astype(jnp.int32), axis=-1).astype(jnp.int32)
    padding = (places[None, None, :] < last_end[:, :, None]).astype(jnp.int32)
    return (segments, padding)


def draw_segment_ids(key, part):
    return document_layout(key)[0]


def draw_pad_mask(key, part):
    return document_layout(key)[1]


def spiked(array, rng, source, target, blocks, factor):
    owner, partner = [(jnp.arange(array.shape[position]) // (array.shape[position] // blocks)).reshape([-1 if axis == position else 1 for axis in range(array.ndim)]) for position in (source, target)]
    chosen = jax.random.permutation(rng, blocks)[partner]
    strong = (owner == chosen) | (owner == (partner + blocks // 2) % blocks)
    return jnp.where(strong, factor * array, array)


def shard_levels(stream_key, shape, cuts, least, high):
    loudness, own = 1.0, jax.random.fold_in(stream_key, 6)
    for position, blocks in cuts:
        steps = jnp.exp(jax.random.uniform(jax.random.fold_in(own, position), (blocks,), jnp.float32, least / len(cuts), high / len(cuts)))
        loudness = loudness * jnp.repeat(steps, shape[position] // blocks).reshape([-1 if axis == position else 1 for axis in range(len(shape))])
    return loudness


def centred(rng, dims, width, limit, cuts=(), held_as=jnp.bfloat16):
    loudness = shard_levels(rng, dims, cuts, -0.22, 0.18) if cuts else 1.0
    values = jax.random.normal(rng, dims, jnp.float32) * width * loudness
    return jnp.minimum(jnp.maximum(values, -limit), limit).astype(held_as)


def bell_draw_with(own_key, shape, scale, limit, cuts, heavy, held_as=jnp.bfloat16):
    drawn = scale * jax.random.normal(own_key, shape, jnp.float32)
    if cuts:
        drawn = drawn * shard_levels(own_key, shape, cuts, -0.22, 0.18)
    return jnp.clip(spiked(drawn, jax.random.fold_in(own_key, 3), *heavy), -limit, limit).astype(held_as)


def setup_inputs(seed: int = 0) -> dict:
    splits = jax.random.split(jax.random.key(seed), 16)
    return {
        "hidden_in": centred(splits[0], (MB, BATCH, SEQ, D), 1.0, 2.5, ((1, 4), (2, 2))),
        "cond_vec": centred(splits[1], (MB, BATCH, CD), 1.0, 2.5, ((1, 4),)),
        "segment_ids": draw_segment_ids(jax.random.fold_in(splits[15], 71), 0),
        "pad_mask": draw_pad_mask(jax.random.fold_in(splits[15], 71), 0),
        "out_cot": bell_draw_with(splits[4], (MB, BATCH, SEQ, D), 1.0, 8.0, ((1, 4), (2, 2)), (1, 3, 4, 2.0)),
        "qkv_weight": centred(splits[5], (3, D, D), D ** -0.5, 0.21875, ((1, 8), (2, 4))),
        "attn_weight": centred(splits[6], (D, D), 16 ** -0.5, 1.5, ((0, 4), (1, 8))),
        "up_weight": centred(splits[7], (D, FF), D ** -0.5, 0.21875, ((0, 8), (1, 4))),
        "up_bias": centred(splits[8], (FF,), 0.5, 1.25, ((0, 32),)),
        "down_weight": centred(splits[9], (FF, D), FF ** -0.5, 0.109375, ((0, 4), (1, 8))),
        "down_bias": centred(splits[10], (D,), 0.3, 0.75, ((0, 8),)),
        "ada_weight": centred(splits[11], (CD, 6 * D), 0.04, 0.099609375, ((1, 8),)),
        "ada_bias": centred(splits[12], (6 * D,), 0.3, 0.75, ((0, 8),)),
        "attn_norm": jnp.clip(1.0 + 0.1 * jax.random.normal(splits[13], (D,), jnp.float32), 0.5, 1.5).astype(jnp.bfloat16),
        "mlp_norm": jnp.clip(1.0 + 0.1 * jax.random.normal(splits[14], (D,), jnp.float32), 0.5, 1.5).astype(jnp.bfloat16),
    }


@jax.custom_vjp
def low(v):
    return lax.optimization_barrier(v.astype(jnp.bfloat16)).astype(jnp.float32)

@jax.custom_vjp
def low_back(v):
    return v

def low_keep(v):
    return (low(v), None)

def low_pass(kept, grad):
    return (grad,)

def back_keep(v):
    return (v, None)

def back_low(kept, grad):
    return (low(grad),)
low.defvjp(low_keep, low_pass)
low_back.defvjp(back_keep, back_low)
norm_eps = 1e-05

def matmul(left, right):
    return jnp.dot(left, right, precision=lax.Precision.HIGHEST, preferred_element_type=jnp.float32)

def modulate(hidden, norm_gain, shift_vec, scale_vec):
    row_mean = lax.optimization_barrier(jnp.mean(hidden, axis=-1, keepdims=True))
    centered = hidden - row_mean
    spread = lax.optimization_barrier(jnp.mean(centered * centered, axis=-1, keepdims=True))
    return centered * lax.rsqrt(spread + norm_eps) * norm_gain * (1.0 + scale_vec) + shift_vec

def rotary_tables(positions, head_count, head_width):
    freq_steps = jnp.arange(head_width // 2, dtype=jnp.float32)
    frequency = jnp.exp(freq_steps * (-2.0 * math.log(10000.0) / head_width))
    angles = positions.astype(jnp.float32)[:, None] * frequency[None, :]
    cosine_table = jnp.cos(angles)
    sine_table = jnp.sin(angles)
    cosine_table = jnp.tile(jnp.concatenate([cosine_table, cosine_table], axis=1), (1, head_count))
    sine_table = jnp.tile(jnp.concatenate([sine_table, sine_table], axis=1), (1, head_count))
    return (cosine_table, sine_table)

def turn_half(values, head_width):
    row_count = values.shape[0]
    halves = values.reshape(row_count, -1, 2, head_width // 2)
    return jnp.concatenate([-halves[:, :, 1:], halves[:, :, :1]], axis=2).reshape(row_count, -1)

def rotate(values, cosine_table, sine_table, head_width):
    return values * cosine_table + turn_half(values, head_width) * sine_table

def attend(queries, keys_full, values, segments):
    length = queries.shape[0]
    block_rows = min(512, length)
    query_blocks = queries.reshape(length // block_rows, block_rows, HEADS, HEAD_DIM)
    segment_blocks = segments.reshape(length // block_rows, block_rows)
    key_heads = keys_full.reshape(length, HEADS, HEAD_DIM)
    value_heads = values.reshape(length, HEADS, HEAD_DIM)

    def one_block(block_items):
        query_block, segment_block = block_items
        scores = jnp.einsum('qhd,khd->hqk', query_block, key_heads, precision=lax.Precision.HIGHEST) * HEAD_DIM ** (-0.5)
        scores = low_back(scores)
        allowed = segment_block[:, None] == segments[None, :]
        scores = jnp.where(allowed[None], scores, -1e+30)
        attn_probs = low(jax.nn.softmax(scores, axis=-1))
        return jnp.einsum('hqk,khd->qhd', attn_probs, value_heads, precision=lax.Precision.HIGHEST)
    mixed_heads = lax.map(jax.checkpoint(one_block), (query_blocks, segment_blocks))
    return mixed_heads.reshape(length, HEADS * HEAD_DIM)

def block_forward(weights, hidden, cond_row, segments):
    qkv_w, attn_w, up_w, up_b, down_w, down_b, ada_w, ada_b, norm_one, norm_two = weights
    length = hidden.shape[0]
    modulation = matmul(cond_row[None, :], ada_w)[0] + ada_b
    shift_one, scale_one, gate_one, shift_two, scale_two, gate_two = jnp.split(modulation, 6)
    normed_one = low(modulate(hidden, norm_one, shift_one, scale_one))
    cosine_table, sine_table = rotary_tables(jnp.arange(length, dtype=jnp.int32), HEADS, HEAD_DIM)
    queries = low(rotate(low_back(matmul(normed_one, qkv_w[0])), cosine_table, sine_table, HEAD_DIM))
    keys_full = low(rotate(low_back(matmul(normed_one, qkv_w[1])), cosine_table, sine_table, HEAD_DIM))
    values = low(low_back(matmul(normed_one, qkv_w[2])))
    mixed_heads = low(low_back(attend(queries, keys_full, values, segments)))
    branch = low_back(matmul(mixed_heads, attn_w))
    hidden_one = hidden + gate_one * branch
    normed_two = low(modulate(hidden_one, norm_two, shift_two, scale_two))
    upper_pre = low_back(matmul(normed_two, up_w) + up_b)
    active = low(jax.nn.gelu(upper_pre, approximate=True))
    down_part = low_back(matmul(active, down_w))
    return hidden_one + gate_two * (down_part + down_b)

def reference(hidden_in, cond_vec, segment_ids, pad_mask, out_cot, qkv_weight, attn_weight, up_weight, up_bias, down_weight, down_bias, ada_weight, ada_bias, attn_norm, mlp_norm):
    weights = tuple((weight.astype(jnp.float32) for weight in (qkv_weight, attn_weight, up_weight, up_bias, down_weight, down_bias, ada_weight, ada_bias, attn_norm, mlp_norm)))
    seq_count = MB * BATCH
    sequence_items = (hidden_in.reshape(seq_count, SEQ, D).astype(jnp.float32), cond_vec.reshape(seq_count, CD).astype(jnp.float32), segment_ids.reshape(seq_count, SEQ), pad_mask.reshape(seq_count, SEQ).astype(jnp.float32), out_cot.reshape(seq_count, SEQ, D).astype(jnp.float32))

    def one_sequence(running, seq_item):
        hidden, cond_row, segments, mask_row, cotangent = seq_item

        def forward(params, rows_in, vector):
            return block_forward(params, rows_in, vector, segments)
        result, pullback = jax.vjp(forward, weights, hidden, cond_row)
        param_grads, input_grad, vector_grad = pullback(cotangent * mask_row[:, None])
        updated = tuple((running_sum + addition for running_sum, addition in zip(running, param_grads)))
        return (updated, (result.astype(jnp.bfloat16), input_grad, vector_grad))
    zero_grads = tuple((jnp.zeros_like(weight) for weight in weights))
    totals, (outputs, hidden_grads, cond_grads) = lax.scan(one_sequence, zero_grads, sequence_items)
    return (outputs.reshape(MB, BATCH, SEQ, D), hidden_grads.reshape(MB, BATCH, SEQ, D), cond_grads.reshape(MB, BATCH, CD), totals[0], totals[1], totals[2], totals[3], totals[4], totals[5], totals[6], totals[7], totals[8], totals[9])
```

```python
import functools
import math

import jax
import jax.numpy as jnp
from jax import lax
from jax.experimental import pallas as pl
from jax.experimental.pallas import tpu as pltpu
from jax.sharding import PartitionSpec as P

HEAD_DIM = 64
HEADS_PER_BLOCK = 3
PAD = 256
NORM_EPS = 1e-05
GELU_C = math.sqrt(2.0 / math.pi)
bf16 = jnp.bfloat16
f32 = jnp.float32
FC = ("fsdp", "ctx")
SWAP = [(0, 1), (1, 0)]
MIB = 1 << 20


def dot_nn(a, b):
    return lax.dot_general(a, b, (((1,), (0,)), ((), ())), preferred_element_type=f32)


def dot_nt(a, b):
    return lax.dot_general(a, b, (((1,), (1,)), ((), ())), preferred_element_type=f32)


def params(limit, axes=1):
    return pltpu.CompilerParams(
        dimension_semantics=("arbitrary",) * axes, vmem_limit_bytes=limit * MIB
    )


def cost(flops, nbytes, trans=0):
    return pl.CostEstimate(flops=flops, bytes_accessed=nbytes, transcendentals=trans)


def whole(shape, **kw):
    return pl.BlockSpec(shape, lambda *_: (0,) * len(shape), **kw)


def turn(x, first):
    return jnp.where(first, pltpu.roll(x, 96, 1), pltpu.roll(x, 32, 1))


def qkv_kernel(x_ref, w_ref, cos_ref, sin_ref, q_ref, k_ref, v_ref):
    b = pl.program_id(1)
    x = x_ref[0]
    rows = x.shape[0]
    lane = lax.broadcasted_iota(jnp.int32, (rows, 128), 1)
    first = (lane % HEAD_DIM) < HEAD_DIM // 2
    low = lane < HEAD_DIM
    cos = cos_ref[0]
    sin = sin_ref[0]

    def rotated(y, scale):
        out = []
        for ch in range(2):
            z = y[:, 128 * ch : 128 * ch + 128]
            z = z * cos + turn(z, first) * sin
            if scale != 1.0:
                z = z.astype(bf16).astype(f32) * scale
            if ch == 1:
                z = jnp.where(low, z, 0.0)
            out.append(z.astype(bf16))
        return jnp.concatenate(out, axis=1)

    w = w_ref[0]

    @pl.when(b < 2)
    def _():
        q_ref[0] = rotated(dot_nn(x, w[:, 0:PAD]), HEAD_DIM ** (-0.5))

    k_ref[0] = rotated(dot_nn(x, w[:, PAD : 2 * PAD]), 1.0)
    v = dot_nn(x, w[:, 2 * PAD : 3 * PAD])
    v_ref[0] = jnp.concatenate(
        [v[:, :128].astype(bf16), jnp.where(low, v[:, 128:], 0.0).astype(bf16)], axis=1
    )


def qkv_call(x_all, w_attn, cos, sin):
    blocks, rows, width = x_all.shape
    tn = w_attn.shape[0]
    return pl.pallas_call(
        qkv_kernel,
        grid=(tn, blocks),
        in_specs=[
            pl.BlockSpec((1, rows, width), lambda t, b: (b, 0, 0)),
            pl.BlockSpec((1, width, 3 * PAD), lambda t, b: (t, 0, 0)),
            pl.BlockSpec((1, rows, 128), lambda t, b: (b // 2, 0, 0)),
            pl.BlockSpec((1, rows, 128), lambda t, b: (b // 2, 0, 0)),
        ],
        out_specs=[
            pl.BlockSpec((1, rows, PAD), lambda t, b: (jnp.minimum(b, 1), 0, t)),
            pl.BlockSpec((1, rows, PAD), lambda t, b: (b, 0, t)),
            pl.BlockSpec((1, rows, PAD), lambda t, b: (b, 0, t)),
        ],
        out_shape=[
            jax.ShapeDtypeStruct((2, rows, tn * PAD), bf16),
            jax.ShapeDtypeStruct((blocks, rows, tn * PAD), bf16),
            jax.ShapeDtypeStruct((blocks, rows, tn * PAD), bf16),
        ],
        compiler_params=params(24, 2),
        cost_estimate=cost(2 * blocks * rows * width * 640 * tn, 16 * MIB),
        name="qkv_rope",
    )(x_all, w_attn, cos, sin)


QB = 256


def head_lanes(x, h):
    if h == 2:
        return x
    lane = lax.broadcasted_iota(jnp.int32, x.shape, 1)
    keep = (lane < HEAD_DIM) if h == 0 else (lane >= HEAD_DIM)
    return jnp.where(keep, x, jnp.zeros_like(x))


def attn_fwd_kernel(q_ref, k_ref, v_ref, sq_ref, sk_ref, o_ref, lse_ref):
    rows = q_ref.shape[1]
    keys = 2 * rows
    k = k_ref[...].reshape(keys, PAD)
    v = v_ref[...].reshape(keys, PAD)
    sk = sk_ref[0]
    lse_ref[...] = jnp.zeros_like(lse_ref)
    low = lax.broadcasted_iota(jnp.int32, (QB, 128), 1) < HEAD_DIM
    for qb in range(rows // QB):
        span = pl.ds(qb * QB, QB)
        same = sq_ref[0, span, :] == sk
        outs = []
        for h in range(HEADS_PER_BLOCK):
            ch = slice(128 * (h // 2), 128 * (h // 2) + 128)
            qh = head_lanes(q_ref[0, span, ch], h)
            s = jnp.where(same, dot_nt(qh, k[:, ch]), -1e30)
            top = jnp.max(s, axis=1, keepdims=True)
            p = jnp.exp(s - top)
            total = jnp.sum(p, axis=1, keepdims=True)
            o = dot_nn(p.astype(bf16), v[:, ch]) / total
            outs.append(o)
            lse = jnp.broadcast_to(top + jnp.log(total), (QB, 128))
            lse_ref[0, 0, h : h + 1, span] = lse.T[0:1, :]
        pair = jnp.where(low, outs[0], outs[1]).astype(bf16)
        o_ref[0, span, :] = jnp.concatenate([pair, outs[2].astype(bf16)], axis=1)


def attn_fwd_call(q, k, v, seg_col, seg_row):
    _, rows, wide = q.shape
    tn = wide // PAD
    k4 = k.reshape(2, 2, rows, wide)
    v4 = v.reshape(2, 2, rows, wide)
    return pl.pallas_call(
        attn_fwd_kernel,
        grid=(2, tn),
        in_specs=[
            pl.BlockSpec((1, rows, PAD), lambda m, t: (m, 0, t)),
            pl.BlockSpec((2, 1, rows, PAD), lambda m, t: (0, m, 0, t)),
            pl.BlockSpec((2, 1, rows, PAD), lambda m, t: (0, m, 0, t)),
            pl.BlockSpec((1, rows, 1), lambda m, t: (m, 0, 0)),
            pl.BlockSpec((1, 1, 2 * rows), lambda m, t: (m, 0, 0)),
        ],
        out_specs=[
            pl.BlockSpec((1, rows, PAD), lambda m, t: (m, 0, t)),
            pl.BlockSpec((1, 1, 8, rows), lambda m, t: (m, t, 0, 0)),
        ],
        out_shape=[
            jax.ShapeDtypeStruct((2, rows, wide), bf16),
            jax.ShapeDtypeStruct((2, tn, 8, rows), f32),
        ],
        compiler_params=params(32, 2),
        cost_estimate=cost(
            2 * tn * 3 * 2 * 2 * rows * 2 * rows * 128 * 2, 12 * MIB, 2 * tn * 3 * rows * 2 * rows
        ),
        name="attn_fwd",
    )(q, k4, v4, seg_col, seg_row)


def attn_bwd_kernel(
    tl_ref,
    q_ref,
    k_ref,
    v_ref,
    g_ref,
    lse_ref,
    sq_ref,
    sk_ref,
    cq_ref,
    sinq_ref,
    ck_ref,
    sink_ref,
    dq_ref,
    own_ref,
    oth_ref,
):
    rows = q_ref.shape[1]
    keys = 2 * rows
    k = k_ref[...].reshape(keys, PAD)
    v = v_ref[...].reshape(keys, PAD)
    sk = sk_ref[0]
    low = lax.broadcasted_iota(jnp.int32, (QB, 128), 1) < HEAD_DIM

    def first_lanes(n):
        return (lax.broadcasted_iota(jnp.int32, (n, 128), 1) % HEAD_DIM) < HEAD_DIM // 2

    for chunk in range(2):
        ch = slice(128 * chunk, 128 * chunk + 128)
        kc = k[:, ch]
        vc = v[:, ch]
        kt = kc.T
        dk = jnp.zeros((keys, 128), f32)
        dv = jnp.zeros((keys, 128), f32)
        for qb in range(rows // QB):
            span = pl.ds(qb * QB, QB)
            same = sk == sq_ref[0, :, span]
            qc = q_ref[0, span, ch]
            gc = g_ref[0, span, ch]
            dqs = []
            for h in (0, 1) if chunk == 0 else (2,):
                qh = head_lanes(qc, h)
                gh = head_lanes(gc, h)
                s = dot_nt(kc, qh)
                p = jnp.exp(jnp.where(same, s - lse_ref[0, 0, h : h + 1, span], -1e30))
                dp = dot_nt(vc, gh)
                t = p * dp
                inner = jnp.sum(t, axis=0, keepdims=True)
                ds = (t - p * inner).astype(bf16)
                dv += dot_nn(p.astype(bf16), gh)
                dk += dot_nn(ds, qh)
                dqs.append(dot_nn(kt, ds).T * HEAD_DIM ** (-0.5))
            dq = jnp.where(low, dqs[0], dqs[1]) if chunk == 0 else jnp.where(low, dqs[0], 0.0)
            dq = dq * cq_ref[span, :] - turn(dq, first_lanes(QB)) * sinq_ref[span, :]
            dq_ref[0, 0, span, ch] = dq.astype(bf16)
        dk = dk * ck_ref[...] - turn(dk, first_lanes(keys)) * sink_ref[...]
        own_ref[0, 0, 0, :, ch] = dk[:rows]
        own_ref[0, 1, 0, :, ch] = dv[:rows]
        oth_ref[0, 0, 0, :, ch] = dk[rows:].astype(bf16)
        oth_ref[0, 1, 0, :, ch] = dv[rows:].astype(bf16)


def attn_bwd_call(tlist, q, k, v, g, lse, seg_row_q, seg_col_k, cos, sin):
    _, rows, wide = q.shape
    nt = tlist.shape[0]
    k4 = k.reshape(2, 2, rows, wide)
    v4 = v.reshape(2, 2, rows, wide)
    cos_all = cos.reshape(2 * rows, 128)
    sin_all = sin.reshape(2 * rows, 128)
    return pl.pallas_call(
        attn_bwd_kernel,
        grid_spec=pltpu.PrefetchScalarGridSpec(
            num_scalar_prefetch=1,
            grid=(nt, 2),
            in_specs=[
                pl.BlockSpec((1, rows, PAD), lambda i, m, tl: (m, 0, tl[i])),
                pl.BlockSpec((2, 1, rows, PAD), lambda i, m, tl: (0, m, 0, tl[i])),
                pl.BlockSpec((2, 1, rows, PAD), lambda i, m, tl: (0, m, 0, tl[i])),
                pl.BlockSpec((1, rows, PAD), lambda i, m, tl: (m, 0, tl[i])),
                pl.BlockSpec((1, 1, 8, rows), lambda i, m, tl: (m, tl[i], 0, 0)),
                pl.BlockSpec((1, 1, rows), lambda i, m, tl: (m, 0, 0)),
                pl.BlockSpec((1, 2 * rows, 1), lambda i, m, tl: (m, 0, 0)),
                whole((rows, 128)),
                whole((rows, 128)),
                whole((2 * rows, 128)),
                whole((2 * rows, 128)),
            ],
            out_specs=[
                pl.BlockSpec((1, 1, rows, PAD), lambda i, m, tl: (i, m, 0, 0)),
                pl.BlockSpec((1, 2, 1, rows, PAD), lambda i, m, tl: (i, 0, m, 0, 0)),
                pl.BlockSpec((1, 2, 1, rows, PAD), lambda i, m, tl: (i, 0, m, 0, 0)),
            ],
        ),
        out_shape=[
            jax.ShapeDtypeStruct((nt, 2, rows, PAD), bf16),
            jax.ShapeDtypeStruct((nt, 2, 2, rows, PAD), f32),
            jax.ShapeDtypeStruct((nt, 2, 2, rows, PAD), bf16),
        ],
        compiler_params=params(48, 2),
        cost_estimate=cost(
            2 * nt * 3 * 5 * 2 * rows * 2 * rows * 128, 5 * nt * MIB, 2 * nt * 3 * rows * 2 * rows
        ),
        name="attn_bwd",
    )(tlist, q, k4, v4, g, lse, seg_row_q, seg_col_k, cos_all[:rows], sin_all[:rows], cos_all, sin_all)


RB = 256


def normalise(h):
    mean = jnp.mean(h, axis=-1, keepdims=True)
    cent = h - mean
    var = jnp.mean(cent * cent, axis=-1, keepdims=True)
    rstd = lax.rsqrt(var + NORM_EPS)
    return cent * rstd, rstd


def outproj_kernel(mix_ref, w_ref, hid_ref, vec_ref, branch_ref, h1_ref, n2_ref):
    mix = mix_ref[0]
    acc = dot_nt(mix[:, 0:PAD], w_ref[0])
    for t in range(1, w_ref.shape[0]):
        acc += dot_nt(mix[:, t * PAD : (t + 1) * PAD], w_ref[t])
    branch_ref[0] = acc
    h1 = hid_ref[0].astype(f32) + vec_ref[0, 0:1, :] * acc
    h1_ref[0] = h1
    n, _ = normalise(h1)
    n2_ref[0] = (n * vec_ref[0, 1:2, :] + vec_ref[0, 2:3, :]).astype(bf16)


def outproj_call(mixed, w_out, hid, vec):
    _, rows, wide = mixed.shape
    width = hid.shape[-1]
    tn = w_out.shape[0]
    row = lambda w: pl.BlockSpec((1, RB, w), lambda m, i: (m, i, 0))
    return pl.pallas_call(
        outproj_kernel,
        grid=(2, rows // RB),
        in_specs=[
            row(wide),
            whole((tn, width, PAD)),
            row(width),
            pl.BlockSpec((1, 8, width), lambda m, i: (m, 0, 0)),
        ],
        out_specs=[row(width), row(width), row(width)],
        out_shape=[
            jax.ShapeDtypeStruct((2, rows, width), f32),
            jax.ShapeDtypeStruct((2, rows, width), f32),
            jax.ShapeDtypeStruct((2, rows, width), bf16),
        ],
        compiler_params=params(24, 2),
        cost_estimate=cost(2 * 2 * rows * wide * width, 12 * MIB),
        name="outproj_norm",
    )(mixed, w_out, hid, vec)


def mlp_kernel(own_ref, x_ref, g_ref, up_ref, dn_ref, ub_ref, down_ref, ng_ref, act_ref, ul_ref):
    j = pl.program_id(0)
    rows = x_ref.shape[0]
    bias = ub_ref[0]

    def step(i, carry):
        span = pl.ds(i * RB, RB)
        u = dot_nn(x_ref[span, :], up_ref[0]) + bias
        da = dot_nn(g_ref[span, :], dn_ref[0])
        u2 = u * u
        th = jnp.tanh(GELU_C * u * (1.0 + 0.044715 * u2))
        half = 0.5 * (1.0 + th)
        act = (u * half).astype(bf16)
        slope = half + (0.5 * GELU_C) * u * (1.0 - th * th) * (1.0 + (3 * 0.044715) * u2)
        ul = (da * slope).astype(bf16)
        d = dot_nt(act, dn_ref[0])
        n = dot_nt(ul, up_ref[0])

        @pl.when(j == 0)
        def _():
            down_ref[span, :] = d
            ng_ref[span, :] = n

        @pl.when(j > 0)
        def _():
            down_ref[span, :] += d
            ng_ref[span, :] += n

        @pl.when(j == own_ref[0])
        def _():
            act_ref[span, :] = act
            ul_ref[span, :] = ul

        return carry

    lax.fori_loop(0, rows // RB, step, 0)


def mlp_call(own, normed, down_low, w_up, w_down, up_bias):
    rows, width = normed.shape
    tn, _, ff = w_up.shape
    one = pl.Buffered(1)
    return pl.pallas_call(
        mlp_kernel,
        grid_spec=pltpu.PrefetchScalarGridSpec(
            num_scalar_prefetch=1,
            grid=(tn,),
            in_specs=[
                whole((rows, width), pipeline_mode=one),
                whole((rows, width), pipeline_mode=one),
                pl.BlockSpec((1, width, ff), lambda j, o: (j, 0, 0)),
                pl.BlockSpec((1, width, ff), lambda j, o: (j, 0, 0)),
                pl.BlockSpec((1, 1, ff), lambda j, o: (j, 0, 0)),
            ],
            out_specs=[
                whole((rows, width)),
                whole((rows, width)),
                whole((rows, ff)),
                whole((rows, ff)),
            ],
        ),
        out_shape=[
            jax.ShapeDtypeStruct((rows, width), f32),
            jax.ShapeDtypeStruct((rows, width), f32),
            jax.ShapeDtypeStruct((rows, ff), bf16),
            jax.ShapeDtypeStruct((rows, ff), bf16),
        ],
        compiler_params=params(44),
        cost_estimate=cost(4 * 2 * rows * width * ff * tn, 24 * MIB, rows * ff * tn),
        name="mlp_both",
    )(own, normed, down_low, w_up, w_down, up_bias)


def colsum(ref, row, value, first):
    total = jnp.sum(value, axis=0, keepdims=True)

    @pl.when(first)
    def _():
        ref[0, row : row + 1, :] = total

    @pl.when(jnp.logical_not(first))
    def _():
        ref[0, row : row + 1, :] += total


def middle_kernel(
    down_ref, ng_ref, h1_ref, br_ref, cot_ref, mask_ref, w_ref, vec_ref, out_ref, dh_ref, bl_ref, mg_ref, sum_ref
):
    first = pl.program_id(1) == 0
    gate1 = vec_ref[0, 0:1, :]
    gain2 = vec_ref[0, 1:2, :]
    gate2 = vec_ref[0, 3:4, :]
    dbias = vec_ref[0, 4:5, :]
    cot = cot_ref[0].astype(f32) * mask_ref[0]
    down = down_ref[0] + dbias
    h1 = h1_ref[0]
    out_ref[0] = (h1 + gate2 * down).astype(bf16)
    n, rstd = normalise(h1)
    g = ng_ref[0]
    gn = g * n
    e = g * gain2
    en = gn * gain2
    dh = cot + rstd * (
        e - jnp.mean(e, axis=-1, keepdims=True) - n * jnp.mean(en, axis=-1, keepdims=True)
    )
    dh_ref[0] = dh
    bl = (dh * gate1).astype(bf16)
    bl_ref[0] = bl
    for t in range(w_ref.shape[0]):
        mg_ref[0, :, t * PAD : (t + 1) * PAD] = dot_nn(bl, w_ref[t]).astype(bf16)

    @pl.when(first)
    def _():
        sum_ref[...] = jnp.zeros_like(sum_ref)

    parts = (cot * down, cot, g, gn, dh * br_ref[0])
    for i, part in enumerate(parts):
        sum_ref[0, i : i + 1, :] += jnp.sum(part, axis=0, keepdims=True)


def middle_call(down, ngrad, h1, branch, cot, mask_col, w_out, vec):
    _, rows, width = h1.shape
    tn = w_out.shape[0]
    row = lambda w: pl.BlockSpec((1, RB, w), lambda m, i: (m, i, 0))
    vecs = pl.BlockSpec((1, 8, width), lambda m, i: (m, 0, 0))
    return pl.pallas_call(
        middle_kernel,
        grid=(2, rows // RB),
        in_specs=[
            row(width),
            row(width),
            row(width),
            row(width),
            row(width),
            row(1),
            whole((tn, width, PAD)),
            vecs,
        ],
        out_specs=[row(width), row(width), row(width), row(tn * PAD), vecs],
        out_shape=[
            jax.ShapeDtypeStruct((2, rows, width), bf16),
            jax.ShapeDtypeStruct((2, rows, width), f32),
            jax.ShapeDtypeStruct((2, rows, width), bf16),
            jax.ShapeDtypeStruct((2, rows, tn * PAD), bf16),
            jax.ShapeDtypeStruct((2, 8, width), f32),
        ],
        compiler_params=params(32, 2),
        cost_estimate=cost(2 * 2 * rows * width * tn * PAD, 28 * MIB),
        name="middle_bwd",
    )(down, ngrad, h1, branch, cot, mask_col, w_out, vec)


def last_kernel(
    own_ref, dqo_ref, kvo_ref, rvo_ref, dqr_ref, kvr_ref, rvr_ref, w_ref, hid_ref, dh_ref, vec_ref, out_ref, sum_ref
):
    first = pl.program_id(1) == 0
    own = own_ref[0]
    tn = w_ref.shape[0]
    acc = jnp.zeros(dh_ref.shape[1:], f32)
    for t in range(tn):
        mine = own == t
        slot = jnp.minimum(lax.rem(t - own - 1 + 2 * tn, tn), tn - 2)
        dq = jnp.where(mine, dqo_ref[0, 0], dqr_ref[slot, 0])
        acc += dot_nt(dq, w_ref[t, :, 0:PAD])
        for j in range(2):
            d = jnp.where(
                mine,
                kvo_ref[0, j, 0] + rvo_ref[0, j, 0].astype(f32),
                kvr_ref[slot, j, 0] + rvr_ref[slot, j, 0].astype(f32),
            )
            acc += dot_nt(d.astype(bf16), w_ref[t, :, (j + 1) * PAD : (j + 2) * PAD])
    gain1 = vec_ref[0, 5:6, :]
    n, rstd = normalise(hid_ref[0].astype(f32))
    gn = acc * n
    e = acc * gain1
    en = gn * gain1
    out_ref[0] = dh_ref[0] + rstd * (
        e - jnp.mean(e, axis=-1, keepdims=True) - n * jnp.mean(en, axis=-1, keepdims=True)
    )

    @pl.when(first)
    def _():
        sum_ref[...] = jnp.zeros_like(sum_ref)

    sum_ref[0, 0:1, :] += jnp.sum(acc, axis=0, keepdims=True)
    sum_ref[0, 1:2, :] += jnp.sum(gn, axis=0, keepdims=True)


def last_call(own, dqo, kvo, rvo, dqr, kvr, rvr, w_attn, hid, dh, vec):
    _, rows, width = hid.shape
    tn = w_attn.shape[0]
    nt = dqr.shape[0]
    row = pl.BlockSpec((1, RB, width), lambda m, i, o: (m, i, 0))
    vecs = pl.BlockSpec((1, 8, width), lambda m, i, o: (m, 0, 0))
    q_spec = lambda n: pl.BlockSpec((n, 1, RB, PAD), lambda m, i, o: (0, m, i, 0))
    kv_spec = lambda n: pl.BlockSpec((n, 2, 1, RB, PAD), lambda m, i, o: (0, 0, m, i, 0))
    return pl.pallas_call(
        last_kernel,
        grid_spec=pltpu.PrefetchScalarGridSpec(
            num_scalar_prefetch=1,
            grid=(2, rows // RB),
            in_specs=[
                q_spec(1),
                kv_spec(1),
                kv_spec(1),
                q_spec(nt),
                kv_spec(nt),
                kv_spec(nt),
                whole((tn, width, 3 * PAD)),
                row,
                row,
                vecs,
            ],
            out_specs=[row, vecs],
        ),
        out_shape=[
            jax.ShapeDtypeStruct((2, rows, width), f32),
            jax.ShapeDtypeStruct((2, 8, width), f32),
        ],
        compiler_params=params(48, 2),
        cost_estimate=cost(2 * 2 * rows * width * tn * 3 * PAD, 24 * MIB),
        name="first_norm_bwd",
    )(own, dqo, kvo, rvo, dqr, kvr, rvr, w_attn, hid, dh, vec)


def spread(x, axes):
    count = lax.axis_size(axes)
    many = jnp.broadcast_to(x[None], (count,) + x.shape)
    return lax.all_to_all(many, axes, split_axis=0, concat_axis=0, tiled=True)


def join_cores(part, rank):
    other = lax.ppermute(part, "ctx", SWAP)
    fs, tn, rows, width = part.shape
    both = jnp.stack([jnp.where(rank == 0, part, other), jnp.where(rank == 0, other, part)], axis=1)
    return both.transpose(2, 0, 1, 3, 4).reshape(tn, fs * 2 * rows, width)


def gather_weight(shard, rank):
    along = lax.all_gather(shard, "tp", axis=0, tiled=False)
    return join_cores(spread(along, "fsdp"), rank)


def reduce_to_shard(grad, rank):
    fs = lax.axis_size("fsdp")
    rows = grad.shape[0] // (2 * fs)
    parts = grad.reshape(fs, 2, rows, grad.shape[1])
    mine = lax.dynamic_index_in_dim(parts, rank, 1, keepdims=False)
    theirs = lax.dynamic_index_in_dim(parts, 1 - rank, 1, keepdims=False)
    got = lax.ppermute(theirs.astype(bf16), "ctx", SWAP)
    half = (mine + got.astype(f32)).astype(bf16)
    got = lax.all_to_all(half, "fsdp", split_axis=0, concat_axis=0, tiled=True)
    return jnp.sum(got.astype(f32), axis=0)


def rotary_tables(positions):
    steps = jnp.arange(HEAD_DIM // 2, dtype=f32)
    freq = jnp.exp(steps * (-2.0 * math.log(10000.0) / HEAD_DIM))
    angles = positions.astype(f32)[:, None] * freq[None, :]
    cos = jnp.cos(angles)
    sin = jnp.sin(angles)
    return jnp.concatenate([cos] * 4, axis=1), jnp.concatenate([-sin, sin] * 2, axis=1)


def on_device(
    hidden_in,
    cond_vec,
    segment_ids,
    pad_mask,
    out_cot,
    qkv_weight,
    attn_weight,
    up_weight,
    up_bias,
    down_weight,
    down_bias,
    ada_weight,
    ada_bias,
    attn_norm,
    mlp_norm,
):
    rank = lax.axis_index("ctx")
    own = lax.axis_index("tp")
    fs = lax.axis_size("fsdp")
    tn = lax.axis_size("tp")
    hid = hidden_in[:, 0]
    _, rows, width = hid.shape
    shard = qkv_weight.shape[1]
    heads_w = qkv_weight.shape[2]
    cond_w = cond_vec.shape[2]
    highest = lax.Precision.HIGHEST

    attn_t = attn_weight.T
    pieces = []
    for j in range(3):
        pieces += [qkv_weight[j], attn_t[:, j * HEAD_DIM : (j + 1) * HEAD_DIM]]
    w_attn = gather_weight(jnp.concatenate(pieces, axis=1), rank)

    ada_cols = ada_bias.shape[0]
    small = jnp.concatenate(
        [
            cond_vec.reshape(-1).astype(f32),
            up_bias.astype(f32),
            down_bias.astype(f32),
            attn_norm.astype(f32),
            mlp_norm.astype(f32),
            ada_bias.astype(f32),
        ]
    )
    used = small.shape[0]
    small = jnp.pad(small, (0, -used % 1024)).reshape(-1, 128)
    small = spread(small, ("tp", "fsdp", "ctx")).reshape(tn, fs, 2, -1)
    cuts = [2 * cond_w]
    for size in (shard, shard, shard, shard, ada_cols):
        cuts.append(cuts[-1] + size)
    cond_all = small[0, :, 0, : cuts[0]].reshape(fs, 2, cond_w)
    upb_full = small[:, :, :, cuts[0] : cuts[1]].reshape(tn, 1, -1)
    dnb_full = small[0, :, :, cuts[1] : cuts[2]].reshape(-1)
    norm_one = small[0, :, :, cuts[2] : cuts[3]].reshape(-1)
    norm_two = small[0, :, :, cuts[3] : cuts[4]].reshape(-1)
    adab_full = small[0, :, :, cuts[4] : cuts[5]].reshape(-1)
    ada_full = spread(ada_weight, FC)

    cond_own = cond_vec[:, 0].astype(f32)
    modulation = (
        jnp.einsum("mk,fkc->mfc", cond_own, ada_full.astype(f32), precision=highest).reshape(2, -1)
        + adab_full
    )
    shift_one, scale_one, gate_one, shift_two, scale_two, gate_two = jnp.split(modulation, 6, axis=1)
    gain_one = norm_one * (1.0 + scale_one)
    gain_two = norm_two * (1.0 + scale_two)
    zero = jnp.zeros_like(gain_one)
    vec = jnp.stack(
        [
            gate_one,
            gain_two,
            shift_two,
            gate_two,
            jnp.broadcast_to(dnb_full, gain_one.shape),
            gain_one,
            zero,
            zero,
        ],
        axis=1,
    )

    hid_other = lax.ppermute(hid, "ctx", SWAP)
    hid_all = jnp.stack([hid, hid_other]).astype(f32)
    unit, _ = normalise(hid_all)
    normed_all = (unit * gain_one[None, :, None, :] + shift_one[None, :, None, :]).astype(bf16)
    normed_own = normed_all[0].reshape(2 * rows, width)
    starts = jnp.stack([rank * rows, (1 - rank) * rows])
    cos, sin = rotary_tables((starts[:, None] + jnp.arange(rows)).reshape(-1))
    cos = cos.reshape(2, rows, 128)
    sin = sin.reshape(2, rows, 128)
    seg = segment_ids[:, 0]
    seg_own = lax.dynamic_slice_in_dim(seg, rank * rows, rows, axis=1)
    seg_oth = lax.dynamic_slice_in_dim(seg, (1 - rank) * rows, rows, axis=1)
    seg_keys = jnp.concatenate([seg_own, seg_oth], axis=1)
    mask = lax.dynamic_slice_in_dim(pad_mask[:, 0], rank * rows, rows, axis=1).astype(f32)
    cot = out_cot[:, 0]
    down_low = (cot.astype(f32) * mask[:, :, None] * gate_two[:, None, :]).astype(bf16)

    q, k, v = qkv_call(normed_all.reshape(4, rows, width), w_attn, cos, sin)
    mixed, lse = attn_fwd_call(q, k, v, seg_own[:, :, None], seg_keys[:, None, :])

    w_up = gather_weight(up_weight, rank)
    w_down = gather_weight(down_weight.T, rank)
    w_out = jnp.concatenate(
        [w_attn[:, :, j * PAD + heads_w : (j + 1) * PAD] for j in range(3)]
        + [jnp.zeros(w_attn.shape[:2] + (PAD - heads_w,), bf16)],
        axis=2,
    )
    branch, hidden_one, normed_two = outproj_call(mixed, w_out, hid, vec)
    own_index = own.reshape(1).astype(jnp.int32)
    down, ngrad_two, active, upper_low = mlp_call(
        own_index,
        normed_two.reshape(2 * rows, width),
        down_low.reshape(2 * rows, width),
        w_up,
        w_down,
        upb_full,
    )
    down = down.reshape(2, rows, width)
    ngrad_two = ngrad_two.reshape(2, rows, width)

    grad_up = lax.dot_general(
        normed_two.reshape(2 * rows, width),
        upper_low,
        (((0,), (0,)), ((), ())),
        preferred_element_type=f32,
    )
    grad_down_t = lax.dot_general(
        down_low.reshape(2 * rows, width),
        active,
        (((0,), (0,)), ((), ())),
        preferred_element_type=f32,
    )
    up_shard = reduce_to_shard(grad_up, rank)
    down_shard = reduce_to_shard(grad_down_t, rank)
    upbias_sum = jnp.sum(upper_low.astype(f32), axis=0)

    block_out, dh_one, branch_low, mixed_grad, sums_two = middle_call(
        down, ngrad_two, hidden_one, branch, cot, mask[:, :, None], w_out, vec
    )

    bwd = functools.partial(
        attn_bwd_call,
        q=q,
        k=k,
        v=v,
        g=mixed_grad,
        lse=lse,
        seg_row_q=seg_own[:, None, :],
        seg_col_k=seg_keys[:, :, None],
        cos=cos,
        sin=sin,
    )
    rest = lax.rem(own + 1 + jnp.arange(tn - 1, dtype=jnp.int32), tn).astype(jnp.int32)
    dq_own, kv_own, send_own = bwd(own_index)
    got_own = lax.ppermute(send_own, "ctx", SWAP)
    dq_rest, kv_rest, send_rest = bwd(rest)
    got_rest = lax.ppermute(send_rest, "ctx", SWAP)

    kv_low = (kv_own[0] + got_own[0].astype(f32)).astype(bf16)
    proj_low = jnp.concatenate([dq_own[0], kv_low[0], kv_low[1]], axis=2).reshape(2 * rows, 3 * PAD)
    grad_proj = lax.dot_general(
        normed_own, proj_low, (((0,), (0,)), ((), ())), preferred_element_type=f32
    )
    mixed_own = lax.dynamic_slice_in_dim(mixed, own * PAD, PAD, axis=2).reshape(2 * rows, PAD)
    grad_attn_t = lax.dot_general(
        branch_low.reshape(2 * rows, width),
        mixed_own,
        (((0,), (0,)), ((), ())),
        preferred_element_type=f32,
    )
    pieces = []
    for j in range(3):
        pieces += [
            grad_proj[:, j * PAD : j * PAD + heads_w],
            grad_attn_t[:, j * HEAD_DIM : (j + 1) * HEAD_DIM],
        ]
    attn_shard = reduce_to_shard(jnp.concatenate(pieces, axis=1), rank)

    hidden_grad, sums_one = last_call(
        own_index, dq_own, kv_own, got_own, dq_rest, kv_rest, got_rest, w_attn, hid, dh_one, vec
    )

    gate2_grad = sums_two[:, 0]
    downbias = jnp.sum(sums_two[:, 1] * gate_two, axis=0)
    shift2_grad = sums_two[:, 2]
    scale2_grad = sums_two[:, 3] * norm_two
    mlpnorm = jnp.sum(sums_two[:, 3] * (1.0 + scale_two), axis=0)
    gate1_grad = sums_two[:, 4]
    shift1_grad = sums_one[:, 0]
    scale1_grad = sums_one[:, 1] * norm_one
    attnnorm = jnp.sum(sums_one[:, 1] * (1.0 + scale_one), axis=0)
    mod_grad = jnp.concatenate(
        [shift1_grad, scale1_grad, gate1_grad, shift2_grad, scale2_grad, gate2_grad], axis=1
    )
    group = 2 * fs
    packed = jnp.concatenate(
        [
            mod_grad[0].reshape(group, -1),
            mod_grad[1].reshape(group, -1),
            attnnorm.reshape(group, -1),
            mlpnorm.reshape(group, -1),
            downbias.reshape(group, -1),
            upbias_sum.reshape(group, -1),
        ],
        axis=1,
    )
    used = packed.shape[1]
    packed = jnp.pad(packed, ((0, 0), (0, -used % 1024))).reshape(group, -1, 128)
    packed = lax.all_to_all(packed, FC, split_axis=0, concat_axis=0, tiled=True)
    packed = packed.reshape(fs, 2, -1)
    packed = packed[:, 0] + packed[:, 1]
    mod_parts = packed[:, : 2 * ada_cols].reshape(fs * 2, ada_cols)
    grad_ada = lax.dot_general(
        cond_all.reshape(fs * 2, cond_w),
        mod_parts,
        (((0,), (0,)), ((), ())),
        precision=highest,
        preferred_element_type=f32,
    )
    grad_adabias = jnp.sum(mod_parts, axis=0)
    tail = jnp.sum(packed[:, 2 * ada_cols : used], axis=0).reshape(4, shard)
    cond_part = jnp.einsum(
        "mfc,fkc->mk",
        mod_grad.reshape(2, group, ada_cols),
        ada_full.astype(f32),
        precision=highest,
    )
    cond_grad = cond_part + lax.ppermute(cond_part, "ctx", SWAP)

    grad_qkv = jnp.stack([attn_shard[:, j * PAD : j * PAD + heads_w] for j in range(3)])
    grad_attn = jnp.concatenate(
        [attn_shard[:, j * PAD + heads_w : (j + 1) * PAD] for j in range(3)], axis=1
    ).T
    return (
        block_out[:, None],
        hidden_grad[:, None],
        cond_grad[:, None],
        grad_qkv,
        grad_attn,
        up_shard,
        tail[3],
        down_shard.T,
        tail[2],
        grad_ada,
        grad_adabias,
        tail[0],
        tail[1],
    )


def solution(mesh):
    tokens = P(None, "fsdp", "ctx", None)
    per_seq = P(None, "fsdp", None)
    weights = (
        P(None, FC, "tp"),
        P("tp", FC),
        P(FC, "tp"),
        P(("tp",) + FC),
        P("tp", FC),
        P(FC),
        P(None, FC),
        P(FC),
        P(FC),
        P(FC),
    )
    return jax.shard_map(
        on_device,
        mesh=mesh,
        in_specs=(tokens, per_seq, per_seq, per_seq, tokens) + weights,
        out_specs=(tokens, tokens, per_seq) + weights,
        check_vma=False,
    )
```

```python
import functools
import math

import jax
import jax.numpy as jnp
from jax import lax
from jax.experimental import pallas as pl
from jax.experimental.pallas import tpu as pltpu
from jax.sharding import PartitionSpec as P

HEAD_DIM = 64
HEADS_PER_BLOCK = 3
PAD = 256
NORM_EPS = 1e-05
GELU_C = math.sqrt(2.0 / math.pi)
bf16 = jnp.bfloat16
f32 = jnp.float32
FC = ("fsdp", "ctx")
SWAP = [(0, 1), (1, 0)]
MIB = 1 << 20
LIMIT = 60


def dot_nn(a, b):
    return lax.dot_general(a, b, (((1,), (0,)), ((), ())), preferred_element_type=f32)


def dot_nt(a, b):
    return lax.dot_general(a, b, (((1,), (1,)), ((), ())), preferred_element_type=f32)


def params(limit, axes=1):
    return pltpu.CompilerParams(
        dimension_semantics=("arbitrary",) * axes, vmem_limit_bytes=limit * MIB
    )


def cost(flops, nbytes, trans=0):
    return pl.CostEstimate(flops=flops, bytes_accessed=nbytes, transcendentals=trans)


def whole(shape, **kw):
    return pl.BlockSpec(shape, lambda *_: (0,) * len(shape), **kw)


def turn(x, first):
    return jnp.where(first, pltpu.roll(x, 96, 1), pltpu.roll(x, 32, 1))


def interleave(rank, own_ref, oth_ref, out_ref, col):
    count, shard = own_ref.shape[0], own_ref.shape[2]
    cols = slice(col, col + out_ref.shape[1])
    for c in range(2):

        @pl.when(rank == c)
        def _():
            for f in range(count):
                at = 2 * f * shard
                mine, theirs = at + c * shard, at + (1 - c) * shard
                out_ref[mine : mine + shard, :] = own_ref[f, 0, :, cols]
                out_ref[theirs : theirs + shard, :] = oth_ref[f, 0, :, cols]


def qkv_kernel(rank_ref, x_ref, own_ref, oth_ref, cos_ref, sin_ref, q_ref, k_ref, v_ref, w_ref, wo_ref):
    b = pl.program_id(1)
    x = x_ref[0]
    rows, width = x.shape
    lane = lax.broadcasted_iota(jnp.int32, (rows, 128), 1)
    first = (lane % HEAD_DIM) < HEAD_DIM // 2
    low = lane < HEAD_DIM
    cos = cos_ref[0]
    sin = sin_ref[0]

    @pl.when(b == 0)
    def _():
        interleave(rank_ref[0], own_ref, oth_ref, w_ref.at[0], 0)
        for j in range(3):
            hole = (j + 1) * PAD - HEAD_DIM
            wo_ref[0, :, j * HEAD_DIM : (j + 1) * HEAD_DIM] = w_ref[0, :, hole : hole + HEAD_DIM]
        wo_ref[0, :, PAD - HEAD_DIM :] = jnp.zeros((width, HEAD_DIM), bf16)

    def rotated(y, ch):
        z = y[:, 128 * ch : 128 * ch + 128]
        return z * cos + turn(z, first) * sin

    @pl.when(b < 2)
    def _():
        y = dot_nn(x, w_ref[0, :, 0:PAD])
        scale = HEAD_DIM ** (-0.5)
        q_ref[0, :, 0:128] = rotated(y, 0).astype(bf16) * scale
        q_ref[0, :, 128:PAD] = jnp.where(low, rotated(y, 1), 0.0).astype(bf16) * scale

    y = dot_nn(x, w_ref[0, :, PAD : 2 * PAD])
    k_ref[0, :, 0:128] = rotated(y, 0).astype(bf16)
    k_ref[0, :, 128:PAD] = rotated(y, 1).astype(bf16)
    v_ref[0] = dot_nn(x, w_ref[0, :, 2 * PAD : 3 * PAD]).astype(bf16)


def qkv_call(rank, x_all, w_own, w_oth, cos, sin):
    blocks, rows, width = x_all.shape
    fs, tn, shard, _ = w_own.shape
    w_spec = pl.BlockSpec((fs, 1, shard, 3 * PAD), lambda t, b, r: (0, t, 0, 0))
    return pl.pallas_call(
        qkv_kernel,
        grid_spec=pltpu.PrefetchScalarGridSpec(
            num_scalar_prefetch=1,
            grid=(tn, blocks),
            in_specs=[
                pl.BlockSpec((1, rows, width), lambda t, b, r: (b, 0, 0)),
                w_spec,
                w_spec,
                pl.BlockSpec((1, rows, 128), lambda t, b, r: (b // 2, 0, 0)),
                pl.BlockSpec((1, rows, 128), lambda t, b, r: (b // 2, 0, 0)),
            ],
            out_specs=[
                pl.BlockSpec((1, rows, PAD), lambda t, b, r: (jnp.minimum(b, 1), 0, t)),
                pl.BlockSpec((1, rows, PAD), lambda t, b, r: (b, 0, t)),
                pl.BlockSpec((1, rows, PAD), lambda t, b, r: (b, 0, t)),
                pl.BlockSpec((1, width, 3 * PAD), lambda t, b, r: (t, 0, 0)),
                pl.BlockSpec((1, width, PAD), lambda t, b, r: (t, 0, 0)),
            ],
        ),
        out_shape=[
            jax.ShapeDtypeStruct((2, rows, tn * PAD), bf16),
            jax.ShapeDtypeStruct((blocks, rows, tn * PAD), bf16),
            jax.ShapeDtypeStruct((blocks, rows, tn * PAD), bf16),
            jax.ShapeDtypeStruct((tn, width, 3 * PAD), bf16),
            jax.ShapeDtypeStruct((tn, width, PAD), bf16),
        ],
        compiler_params=params(LIMIT, 2),
        cost_estimate=cost(2 * blocks * rows * width * 640 * tn, 16 * MIB),
        name="qkv_rope",
    )(rank, x_all, w_own, w_oth, cos, sin)


def pack_kernel(qkv_ref, attn_ref, up_ref, down_ref, a_ref, bc_ref):
    ff = up_ref.shape[1]
    heads_w = qkv_ref.shape[2]
    for j in range(3):
        a_ref[:, j * PAD : j * PAD + heads_w] = qkv_ref[j]
        a_ref[:, j * PAD + heads_w : (j + 1) * PAD] = attn_ref[:, j * HEAD_DIM : (j + 1) * HEAD_DIM]
    bc_ref[:, :ff] = up_ref[...]
    bc_ref[:, ff:] = down_ref[...]


def pack_weights(qkv_weight, attn_weight, up_weight, down_weight):
    shard, ff = up_weight.shape
    heads_w = qkv_weight.shape[2]
    if shard % 16:
        attn_t = attn_weight.T
        pieces = []
        for j in range(3):
            pieces += [qkv_weight[j], attn_t[:, j * HEAD_DIM : (j + 1) * HEAD_DIM]]
        return (
            jnp.concatenate(pieces, axis=1),
            jnp.concatenate([up_weight, down_weight.T], axis=1),
        )
    return pl.pallas_call(
        pack_kernel,
        out_shape=[
            jax.ShapeDtypeStruct((shard, 3 * PAD), bf16),
            jax.ShapeDtypeStruct((shard, 2 * ff), bf16),
        ],
        name="pack_weights",
    )(qkv_weight, attn_weight.T, up_weight, down_weight.T)


QB = 256


def head_lanes(x, h):
    if h == 2:
        return x
    lane = lax.broadcasted_iota(jnp.int32, x.shape, 1)
    keep = (lane < HEAD_DIM) if h == 0 else (lane >= HEAD_DIM)
    return jnp.where(keep, x, jnp.zeros_like(x))


def attn_fwd_kernel(q_ref, k_ref, v_ref, sq_ref, sk_ref, o_ref, lse_ref):
    rows = q_ref.shape[1]
    keys = 2 * rows
    k = k_ref[...].reshape(keys, PAD)
    v = v_ref[...].reshape(keys, PAD)
    sk = sk_ref[0]
    lse_ref[...] = jnp.zeros_like(lse_ref)
    low = lax.broadcasted_iota(jnp.int32, (QB, 128), 1) < HEAD_DIM
    for qb in range(rows // QB):
        span = pl.ds(qb * QB, QB)
        same = sq_ref[0, span, :] == sk
        outs = []
        for h in range(HEADS_PER_BLOCK):
            ch = slice(128 * (h // 2), 128 * (h // 2) + 128)
            qh = head_lanes(q_ref[0, span, ch], h)
            s = jnp.where(same, dot_nt(qh, k[:, ch]), -1e30)
            top = jnp.max(s, axis=1, keepdims=True)
            p = jnp.exp(s - top)
            total = jnp.sum(p, axis=1, keepdims=True)
            o = dot_nn(p.astype(bf16), v[:, ch]) / total
            outs.append(o)
            lse = jnp.broadcast_to(top + jnp.log(total), (QB, 128))
            lse_ref[0, 0, h : h + 1, span] = lse.T[0:1, :]
        pair = jnp.where(low, outs[0], outs[1]).astype(bf16)
        o_ref[0, span, :] = jnp.concatenate([pair, outs[2].astype(bf16)], axis=1)


def attn_fwd_call(q, k, v, seg_col, seg_row):
    _, rows, wide = q.shape
    tn = wide // PAD
    k4 = k.reshape(2, 2, rows, wide)
    v4 = v.reshape(2, 2, rows, wide)
    return pl.pallas_call(
        attn_fwd_kernel,
        grid=(2, tn),
        in_specs=[
            pl.BlockSpec((1, rows, PAD), lambda m, t: (m, 0, t)),
            pl.BlockSpec((2, 1, rows, PAD), lambda m, t: (0, m, 0, t)),
            pl.BlockSpec((2, 1, rows, PAD), lambda m, t: (0, m, 0, t)),
            pl.BlockSpec((1, rows, 1), lambda m, t: (m, 0, 0)),
            pl.BlockSpec((1, 1, 2 * rows), lambda m, t: (m, 0, 0)),
        ],
        out_specs=[
            pl.BlockSpec((1, rows, PAD), lambda m, t: (m, 0, t)),
            pl.BlockSpec((1, 1, 8, rows), lambda m, t: (m, t, 0, 0)),
        ],
        out_shape=[
            jax.ShapeDtypeStruct((2, rows, wide), bf16),
            jax.ShapeDtypeStruct((2, tn, 8, rows), f32),
        ],
        compiler_params=params(LIMIT, 2),
        cost_estimate=cost(
            2 * tn * 3 * 2 * 2 * rows * 2 * rows * 128 * 2, 12 * MIB, 2 * tn * 3 * rows * 2 * rows
        ),
        name="attn_fwd",
    )(q, k4, v4, seg_col, seg_row)


def attn_bwd_kernel(
    tl_ref,
    q_ref,
    k_ref,
    v_ref,
    g_ref,
    lse_ref,
    sq_ref,
    sk_ref,
    cq_ref,
    sinq_ref,
    ck_ref,
    sink_ref,
    dq_ref,
    own_ref,
    oth_ref,
):
    rows = q_ref.shape[1]
    keys = 2 * rows
    k = k_ref[...].reshape(keys, PAD)
    v = v_ref[...].reshape(keys, PAD)
    sk = sk_ref[0]
    low = lax.broadcasted_iota(jnp.int32, (QB, 128), 1) < HEAD_DIM

    def first_lanes(n):
        return (lax.broadcasted_iota(jnp.int32, (n, 128), 1) % HEAD_DIM) < HEAD_DIM // 2

    for chunk in range(2):
        ch = slice(128 * chunk, 128 * chunk + 128)
        kc = k[:, ch]
        vc = v[:, ch]
        kt = kc.T
        dk = jnp.zeros((keys, 128), f32)
        dv = jnp.zeros((keys, 128), f32)
        for qb in range(rows // QB):
            span = pl.ds(qb * QB, QB)
            same = sk == sq_ref[0, :, span]
            qc = q_ref[0, span, ch]
            gc = g_ref[0, span, ch]
            dqs = []
            for h in (0, 1) if chunk == 0 else (2,):
                qh = head_lanes(qc, h)
                gh = head_lanes(gc, h)
                s = dot_nt(kc, qh)
                p = jnp.exp(jnp.where(same, s - lse_ref[0, 0, h : h + 1, span], -1e30))
                dp = dot_nt(vc, gh)
                t = p * dp
                inner = jnp.sum(t, axis=0, keepdims=True)
                ds = (t - p * inner).astype(bf16)
                dv += dot_nn(p.astype(bf16), gh)
                dk += dot_nn(ds, qh)
                dqs.append(dot_nn(kt, ds).T * HEAD_DIM ** (-0.5))
            dq = jnp.where(low, dqs[0], dqs[1]) if chunk == 0 else jnp.where(low, dqs[0], 0.0)
            dq = dq * cq_ref[span, :] - turn(dq, first_lanes(QB)) * sinq_ref[span, :]
            dq_ref[0, 0, span, ch] = dq.astype(bf16)
        dk = dk * ck_ref[...] - turn(dk, first_lanes(keys)) * sink_ref[...]
        own_ref[0, 0, 0, :, ch] = dk[:rows]
        own_ref[0, 1, 0, :, ch] = dv[:rows]
        oth_ref[0, 0, 0, :, ch] = dk[rows:].astype(bf16)
        oth_ref[0, 1, 0, :, ch] = dv[rows:].astype(bf16)


def attn_bwd_call(tlist, g, q, k, v, lse, seg_row_q, seg_col_k, cos, sin):
    _, rows, wide = q.shape
    nt = tlist.shape[0]
    k4 = k.reshape(2, 2, rows, wide)
    v4 = v.reshape(2, 2, rows, wide)
    cos_all = cos.reshape(2 * rows, 128)
    sin_all = sin.reshape(2 * rows, 128)
    return pl.pallas_call(
        attn_bwd_kernel,
        grid_spec=pltpu.PrefetchScalarGridSpec(
            num_scalar_prefetch=1,
            grid=(nt, 2),
            in_specs=[
                pl.BlockSpec((1, rows, PAD), lambda i, m, tl: (m, 0, tl[i])),
                pl.BlockSpec((2, 1, rows, PAD), lambda i, m, tl: (0, m, 0, tl[i])),
                pl.BlockSpec((2, 1, rows, PAD), lambda i, m, tl: (0, m, 0, tl[i])),
                pl.BlockSpec((1, rows, PAD), lambda i, m, tl: (m, 0, tl[i])),
                pl.BlockSpec((1, 1, 8, rows), lambda i, m, tl: (m, tl[i], 0, 0)),
                pl.BlockSpec((1, 1, rows), lambda i, m, tl: (m, 0, 0)),
                pl.BlockSpec((1, 2 * rows, 1), lambda i, m, tl: (m, 0, 0)),
                whole((rows, 128)),
                whole((rows, 128)),
                whole((2 * rows, 128)),
                whole((2 * rows, 128)),
            ],
            out_specs=[
                pl.BlockSpec((1, 1, rows, PAD), lambda i, m, tl: (i, m, 0, 0)),
                pl.BlockSpec((1, 2, 1, rows, PAD), lambda i, m, tl: (i, 0, m, 0, 0)),
                pl.BlockSpec((1, 2, 1, rows, PAD), lambda i, m, tl: (i, 0, m, 0, 0)),
            ],
        ),
        out_shape=[
            jax.ShapeDtypeStruct((nt, 2, rows, PAD), bf16),
            jax.ShapeDtypeStruct((nt, 2, 2, rows, PAD), f32),
            jax.ShapeDtypeStruct((nt, 2, 2, rows, PAD), bf16),
        ],
        compiler_params=params(LIMIT, 2),
        cost_estimate=cost(
            2 * nt * 3 * 5 * 2 * rows * 2 * rows * 128, 5 * nt * MIB, 2 * nt * 3 * rows * 2 * rows
        ),
        name="attn_bwd",
    )(tlist, q, k4, v4, g, lse, seg_row_q, seg_col_k, cos_all[:rows], sin_all[:rows], cos_all, sin_all)


RB = 256


def dot_tn(a, b):
    return lax.dot_general(a, b, (((0,), (0,)), ((), ())), preferred_element_type=f32)


def normalise(h):
    mean = jnp.mean(h, axis=-1, keepdims=True)
    cent = h - mean
    var = jnp.mean(cent * cent, axis=-1, keepdims=True)
    rstd = lax.rsqrt(var + NORM_EPS)
    return cent * rstd, rstd


def block_kernel(
    flag_ref,
    mix_ref,
    wout_ref,
    hid_ref,
    vec_ref,
    cot_ref,
    mask_ref,
    wo_ref,
    wt_ref,
    ub_ref,
    out_ref,
    dh_ref,
    mg_ref,
    sum_ref,
    wff_ref,
    wat_ref,
    h1_ref,
    br_ref,
    x_ref,
    g_ref,
    down_ref,
    ng_ref,
    up_ref,
    dn_ref,
    act_ref,
    ul_ref,
):
    j = pl.program_id(0)
    tn = pl.num_programs(0)
    own = flag_ref[0]
    rows = x_ref.shape[0]
    ff = up_ref.shape[1]
    steps = rows // RB
    half = steps // 2
    interleave(flag_ref[1], wo_ref, wt_ref, up_ref, 0)
    interleave(flag_ref[1], wo_ref, wt_ref, dn_ref, ff)

    def vec(m, i):
        return vec_ref[m, i : i + 1, :]

    @pl.when(j == 0)
    def _():
        for m in range(2):

            def before(i, carry):
                span = pl.ds((m * half + i) * RB, RB)
                acc = dot_nt(mix_ref[span, 0:PAD], wout_ref[0])
                for t in range(1, wout_ref.shape[0]):
                    acc += dot_nt(mix_ref[span, t * PAD : (t + 1) * PAD], wout_ref[t])
                br_ref[span, :] = acc
                h1 = hid_ref[span, :].astype(f32) + vec(m, 0) * acc
                h1_ref[span, :] = h1
                n, _ = normalise(h1)
                x_ref[span, :] = (n * vec(m, 1) + vec(m, 2)).astype(bf16)
                cot = cot_ref[span, :].astype(f32) * mask_ref[span, :]
                g_ref[span, :] = (cot * vec(m, 3)).astype(bf16)
                return carry

            lax.fori_loop(0, half, before, 0)

    bias = ub_ref[0]

    def step(i, carry):
        span = pl.ds(i * RB, RB)
        u = dot_nn(x_ref[span, :], up_ref[...]) + bias
        da = dot_nn(g_ref[span, :], dn_ref[...])
        u2 = u * u
        th = jnp.tanh(GELU_C * u * (1.0 + 0.044715 * u2))
        half_up = 0.5 * (1.0 + th)
        act = (u * half_up).astype(bf16)
        slope = half_up + (0.5 * GELU_C) * u * (1.0 - th * th) * (1.0 + (3 * 0.044715) * u2)
        ul = (da * slope).astype(bf16)
        d = dot_nt(act, dn_ref[...])
        n = dot_nt(ul, up_ref[...])

        @pl.when(j == 0)
        def _():
            down_ref[span, :] = d
            ng_ref[span, :] = n

        @pl.when(j > 0)
        def _():
            down_ref[span, :] += d
            ng_ref[span, :] += n

        @pl.when(j == own)
        def _():
            act_ref[span, :] = act
            ul_ref[span, :] = ul

        return carry

    lax.fori_loop(0, steps, step, 0)

    @pl.when(j == tn - 1)
    def _():
        sum_ref[...] = jnp.zeros_like(sum_ref)
        for m in range(2):

            def after(i, carry):
                span = pl.ds((m * half + i) * RB, RB)
                cot = cot_ref[span, :].astype(f32) * mask_ref[span, :]
                down = down_ref[span, :] + vec(m, 4)
                h1 = h1_ref[span, :]
                out_ref[span, :] = (h1 + vec(m, 3) * down).astype(bf16)
                n, rstd = normalise(h1)
                g = ng_ref[span, :]
                gn = g * n
                e = g * vec(m, 1)
                en = gn * vec(m, 1)
                dh = cot + rstd * (
                    e - jnp.mean(e, axis=-1, keepdims=True) - n * jnp.mean(en, axis=-1, keepdims=True)
                )
                dh_ref[span, :] = dh
                bl = (dh * vec(m, 0)).astype(bf16)
                x_low = bl
                for t in range(wout_ref.shape[0]):
                    mg_ref[span, t * PAD : (t + 1) * PAD] = dot_nn(bl, wout_ref[t]).astype(bf16)
                parts = (cot * down, cot, g, gn, dh * br_ref[span, :])
                for r, part in enumerate(parts):
                    sum_ref[m, r : r + 1, :] += jnp.sum(part, axis=0, keepdims=True)
                sum_ref[m, 5:6, :] += jnp.sum(ul_ref[span, :].astype(f32), axis=0, keepdims=True)
                br_ref[span, :] = x_low.astype(f32)
                return carry

            lax.fori_loop(0, half, after, 0)

        for col in range(0, ff, PAD):
            cols = slice(col, col + PAD)
            wff_ref[:, cols] = dot_tn(x_ref[...], ul_ref[:, cols]).astype(bf16)
            wff_ref[:, ff + col : ff + col + PAD] = dot_tn(g_ref[...], act_ref[:, cols]).astype(bf16)
        mine = mix_ref[:, pl.ds(pl.multiple_of(own * PAD, PAD), PAD)]
        wat_ref[...] = dot_tn(br_ref[...].astype(bf16), mine).astype(bf16)


def block_call(flags, mixed, w_out, hid, vec, cot, mask_col, f_own, f_oth, up_bias):
    rows, wide = mixed.shape
    width = hid.shape[1]
    fs, tn, shard, ff = f_own.shape
    ff = ff // 2
    w_spec = pl.BlockSpec((fs, 1, shard, 2 * ff), lambda j, o: (0, j, 0, 0))
    one = pl.Buffered(1)
    const = lambda *shape: whole(shape, pipeline_mode=one)
    tokens = lambda dtype, w: pltpu.VMEM((rows, w), dtype)
    return pl.pallas_call(
        block_kernel,
        grid_spec=pltpu.PrefetchScalarGridSpec(
            num_scalar_prefetch=1,
            grid=(tn,),
            in_specs=[
                const(rows, wide),
                const(tn, width, PAD),
                const(rows, width),
                const(2, 8, width),
                const(rows, width),
                const(rows, 1),
                w_spec,
                w_spec,
                pl.BlockSpec((1, 1, ff), lambda j, o: (j, 0, 0)),
            ],
            out_specs=[
                const(rows, width),
                const(rows, width),
                const(rows, wide),
                const(2, 8, width),
                const(width, 2 * ff),
                const(width, PAD),
            ],
            scratch_shapes=[
                tokens(f32, width),
                tokens(f32, width),
                tokens(bf16, width),
                tokens(bf16, width),
                tokens(f32, width),
                tokens(f32, width),
                pltpu.VMEM((width, ff), bf16),
                pltpu.VMEM((width, ff), bf16),
                tokens(bf16, ff),
                tokens(bf16, ff),
            ],
        ),
        out_shape=[
            jax.ShapeDtypeStruct((rows, width), bf16),
            jax.ShapeDtypeStruct((rows, width), f32),
            jax.ShapeDtypeStruct((rows, wide), bf16),
            jax.ShapeDtypeStruct((2, 8, width), f32),
            jax.ShapeDtypeStruct((width, 2 * ff), bf16),
            jax.ShapeDtypeStruct((width, PAD), bf16),
        ],
        compiler_params=params(LIMIT),
        cost_estimate=cost(
            4 * 2 * rows * width * ff * tn + 8 * rows * width * width, 32 * MIB, rows * ff * tn
        ),
        name="block_both",
    )(flags, mixed, w_out, hid, vec, cot, mask_col, f_own, f_oth, up_bias)


def proj_grad_kernel(n_ref, dq_ref, own_ref, oth_ref, wat_ref, out_ref):
    heads_w = PAD - HEAD_DIM
    rows = dq_ref.shape[0]
    for j in range(3):
        if j == 0:
            part = dot_tn(n_ref[0], dq_ref[...])
        else:
            part = dot_tn(n_ref[0], own_ref[j - 1].astype(bf16)) + dot_tn(n_ref[1], oth_ref[j - 1])
        out_ref[:, j * PAD : j * PAD + heads_w] = part[:, :heads_w].astype(bf16)
        out_ref[:, j * PAD + heads_w : (j + 1) * PAD] = wat_ref[
            :, j * HEAD_DIM : (j + 1) * HEAD_DIM
        ]


def proj_grad_call(normed, dq, kv_own, kv_oth, wat):
    _, rows, width = normed.shape
    return pl.pallas_call(
        proj_grad_kernel,
        out_shape=jax.ShapeDtypeStruct((width, 3 * PAD), bf16),
        compiler_params=pltpu.CompilerParams(vmem_limit_bytes=LIMIT * MIB),
        cost_estimate=cost(2 * 5 * rows * width * PAD, 10 * MIB),
        name="proj_grad",
    )(normed, dq, kv_own, kv_oth, wat)


def last_kernel(
    own_ref, dqo_ref, kvo_ref, rvo_ref, dqr_ref, kvr_ref, rvr_ref, w_ref, hid_ref, dh_ref, vec_ref, out_ref, sum_ref
):
    first = pl.program_id(1) == 0
    own = own_ref[0]
    tn = w_ref.shape[0]
    acc = jnp.zeros(dh_ref.shape[1:], f32)
    for t in range(tn):
        mine = own == t
        slot = jnp.minimum(lax.rem(t - own - 1 + 2 * tn, tn), tn - 2)
        dq = jnp.where(mine, dqo_ref[0, 0], dqr_ref[slot, 0])
        acc += dot_nt(dq, w_ref[t, :, 0:PAD])
        for j in range(2):
            d = jnp.where(
                mine,
                kvo_ref[0, j, 0] + rvo_ref[0, j, 0].astype(f32),
                kvr_ref[slot, j, 0] + rvr_ref[slot, j, 0].astype(f32),
            )
            acc += dot_nt(d.astype(bf16), w_ref[t, :, (j + 1) * PAD : (j + 2) * PAD])
    gain1 = vec_ref[0, 5:6, :]
    n, rstd = normalise(hid_ref[0].astype(f32))
    gn = acc * n
    e = acc * gain1
    en = gn * gain1
    out_ref[0] = dh_ref[0] + rstd * (
        e - jnp.mean(e, axis=-1, keepdims=True) - n * jnp.mean(en, axis=-1, keepdims=True)
    )

    @pl.when(first)
    def _():
        sum_ref[...] = jnp.zeros_like(sum_ref)

    sum_ref[0, 0:1, :] += jnp.sum(acc, axis=0, keepdims=True)
    sum_ref[0, 1:2, :] += jnp.sum(gn, axis=0, keepdims=True)


def last_call(own, dqo, kvo, rvo, dqr, kvr, rvr, w_attn, hid, dh, vec):
    _, rows, width = hid.shape
    tn = w_attn.shape[0]
    nt = dqr.shape[0]
    row = pl.BlockSpec((1, RB, width), lambda m, i, o: (m, i, 0))
    vecs = pl.BlockSpec((1, 8, width), lambda m, i, o: (m, 0, 0))
    q_spec = lambda n: pl.BlockSpec((n, 1, RB, PAD), lambda m, i, o: (0, m, i, 0))
    kv_spec = lambda n: pl.BlockSpec((n, 2, 1, RB, PAD), lambda m, i, o: (0, 0, m, i, 0))
    return pl.pallas_call(
        last_kernel,
        grid_spec=pltpu.PrefetchScalarGridSpec(
            num_scalar_prefetch=1,
            grid=(2, rows // RB),
            in_specs=[
                q_spec(1),
                kv_spec(1),
                kv_spec(1),
                q_spec(nt),
                kv_spec(nt),
                kv_spec(nt),
                whole((tn, width, 3 * PAD)),
                row,
                row,
                vecs,
            ],
            out_specs=[row, vecs],
        ),
        out_shape=[
            jax.ShapeDtypeStruct((2, rows, width), f32),
            jax.ShapeDtypeStruct((2, 8, width), f32),
        ],
        compiler_params=params(LIMIT, 2),
        cost_estimate=cost(2 * 2 * rows * width * tn * 3 * PAD, 24 * MIB),
        name="first_norm_bwd",
    )(own, dqo, kvo, rvo, dqr, kvr, rvr, w_attn, hid, dh, vec)


def spread(x, axes):
    count = lax.axis_size(axes)
    many = jnp.broadcast_to(x[None], (count,) + x.shape)
    return lax.all_to_all(many, axes, split_axis=0, concat_axis=0, tiled=True)


def join_cores(part, other, rank):
    fs, tn, rows, width = part.shape
    both = jnp.stack([jnp.where(rank == 0, part, other), jnp.where(rank == 0, other, part)], axis=1)
    return both.transpose(2, 0, 1, 3, 4).reshape(1, tn, fs * 2 * rows, width)


def exchange_to_shard(grad):
    group = lax.axis_size(FC)
    parts = grad.reshape(group, -1, grad.shape[1])
    return lax.all_to_all(parts, FC, split_axis=0, concat_axis=0, tiled=True)


def rotary_tables(positions):
    steps = jnp.arange(HEAD_DIM // 2, dtype=f32)
    freq = jnp.exp(steps * (-2.0 * math.log(10000.0) / HEAD_DIM))
    angles = positions.astype(f32)[:, None] * freq[None, :]
    cos = jnp.cos(angles)
    sin = jnp.sin(angles)
    return jnp.concatenate([cos] * 4, axis=1), jnp.concatenate([-sin, sin] * 2, axis=1)


def on_device(
    hidden_in,
    cond_vec,
    segment_ids,
    pad_mask,
    out_cot,
    qkv_weight,
    attn_weight,
    up_weight,
    up_bias,
    down_weight,
    down_bias,
    ada_weight,
    ada_bias,
    attn_norm,
    mlp_norm,
):
    rank = lax.axis_index("ctx")
    own = lax.axis_index("tp")
    fs = lax.axis_size("fsdp")
    tn = lax.axis_size("tp")
    hid = hidden_in[:, 0]
    _, rows, width = hid.shape
    shard = qkv_weight.shape[1]
    heads_w = qkv_weight.shape[2]
    cond_w = cond_vec.shape[2]
    highest = lax.Precision.HIGHEST

    w_attn_shard, w_ff_shard = pack_weights(qkv_weight, attn_weight, up_weight, down_weight)
    ada_cols = ada_bias.shape[0]
    extra = [cond_vec[:, 0]]
    for x in (down_bias, attn_norm, mlp_norm, up_bias, ada_bias):
        extra.append(jnp.pad(x, (0, -x.shape[0] % cond_w)).reshape(-1, cond_w))
    extra = jnp.concatenate(extra, axis=0)
    ada_rows = jnp.concatenate([ada_weight.T, extra], axis=0)
    ada_rows = jnp.pad(ada_rows, ((0, -ada_rows.shape[0] % 16), (0, 0)))
    ada_rows = lax.all_gather(ada_rows, FC, axis=0, tiled=False)
    along = lax.all_gather(w_attn_shard, "tp", axis=0, tiled=False)
    w_own = spread(along, "fsdp")
    w_ff_along, w_ff_shard = lax.optimization_barrier((along, w_ff_shard))
    w_ff_along = lax.all_gather(w_ff_shard, "tp", axis=0, tiled=False)

    ada_full = ada_rows[:, :ada_cols].astype(f32)
    small = ada_rows[:, ada_cols:].astype(f32)
    cond_all = small[:, :2].reshape(fs, 2, 2, cond_w)[:, 0]
    dnb_full = small[:, 2, :shard].reshape(-1)
    norm_one = small[:, 3, :shard].reshape(-1)
    norm_two = small[:, 4, :shard].reshape(-1)
    upb_own = small[:, 5, :shard].reshape(1, -1)
    adab_full = small[:, 6:].reshape(2 * fs, -1)[:, :ada_cols].reshape(-1)
    upb_full = lax.all_gather(upb_own, "tp", axis=0, tiled=False)

    modulation_all = (
        jnp.einsum("smk,fck->smfc", cond_all, ada_full, precision=highest).reshape(fs, 2, -1)
        + adab_full
    )
    modulation = lax.dynamic_index_in_dim(modulation_all, lax.axis_index("fsdp"), 0, keepdims=False)
    shift_one, scale_one, gate_one, shift_two, scale_two, gate_two = jnp.split(modulation, 6, axis=1)
    gain_one = norm_one * (1.0 + scale_one)
    gain_two = norm_two * (1.0 + scale_two)
    zero = jnp.zeros_like(gain_one)
    vec = jnp.stack(
        [
            gate_one,
            gain_two,
            shift_two,
            gate_two,
            jnp.broadcast_to(dnb_full, gain_one.shape),
            gain_one,
            zero,
            zero,
        ],
        axis=1,
    )

    hid_other = lax.ppermute(hid, "ctx", SWAP)
    hid_all = jnp.stack([hid, hid_other]).astype(f32)
    unit, _ = normalise(hid_all)
    normed_all = (unit * gain_one[None, :, None, :] + shift_one[None, :, None, :]).astype(bf16)
    starts = jnp.stack([rank * rows, (1 - rank) * rows])
    cos, sin = rotary_tables((starts[:, None] + jnp.arange(rows)).reshape(-1))
    cos = cos.reshape(2, rows, 128)
    sin = sin.reshape(2, rows, 128)
    seg = segment_ids[:, 0]
    seg_own = lax.dynamic_slice_in_dim(seg, rank * rows, rows, axis=1)
    seg_oth = lax.dynamic_slice_in_dim(seg, (1 - rank) * rows, rows, axis=1)
    seg_keys = jnp.concatenate([seg_own, seg_oth], axis=1)
    mask = lax.dynamic_slice_in_dim(pad_mask[:, 0], rank * rows, rows, axis=1).astype(f32)
    cot = out_cot[:, 0]

    rank_index = rank.reshape(1).astype(jnp.int32)
    w_own, normed_all, cos, sin, upb_full, vec = lax.optimization_barrier(
        (w_own, normed_all, cos, sin, upb_full, vec)
    )
    normed_own = normed_all[0].reshape(2 * rows, width)
    w_oth = lax.ppermute(w_own, "ctx", SWAP)
    f_own = spread(w_ff_along, "fsdp")
    f_rank = rank_index
    if shard % 16:
        halves = lambda w: (w[:, :, : width // 2], w[:, :, width // 2 :])
        w_own, w_oth = halves(join_cores(w_own, w_oth, rank))
        rank_index = rank_index * 0
    q, k, v, w_attn, w_out = qkv_call(
        rank_index, normed_all.reshape(4, rows, width), w_own, w_oth, cos, sin
    )
    mixed, lse = attn_fwd_call(q, k, v, seg_own[:, :, None], seg_keys[:, None, :])

    f_own, mixed = lax.optimization_barrier((f_own, mixed))
    f_oth = lax.ppermute(f_own, "ctx", SWAP)
    if shard % 16:
        f_own, f_oth = halves(join_cores(f_own, f_oth, rank))
    own_index = own.reshape(1).astype(jnp.int32)
    flat = lambda x: x.reshape(2 * rows, -1)
    block_out, dh_one, mixed_grad, sums_two, ff_low, attn_low = block_call(
        jnp.concatenate([own_index, rank_index]),
        flat(mixed),
        w_out,
        flat(hid),
        vec,
        flat(cot),
        mask.reshape(-1, 1),
        f_own,
        f_oth,
        upb_full,
    )
    mixed_grad = mixed_grad.reshape(2, rows, -1)
    ff_low, mixed_grad = lax.optimization_barrier((ff_low, mixed_grad))
    ff_got = exchange_to_shard(ff_low)

    bwd = functools.partial(
        attn_bwd_call,
        q=q,
        k=k,
        v=v,
        lse=lse,
        seg_row_q=seg_own[:, None, :],
        seg_col_k=seg_keys[:, :, None],
        cos=cos,
        sin=sin,
    )
    rest = lax.rem(own + 1 + jnp.arange(tn - 1, dtype=jnp.int32), tn).astype(jnp.int32)
    dq_own, kv_own, send_own = bwd(own_index, g=mixed_grad)
    got_own = lax.ppermute(send_own, "ctx", SWAP)
    proj_low = proj_grad_call(
        normed_all.reshape(2, 2 * rows, width),
        flat(dq_own),
        kv_own.reshape(2, 2 * rows, PAD),
        send_own.reshape(2, 2 * rows, PAD),
        attn_low,
    )

    gate2_grad = sums_two[:, 0]
    downbias = jnp.sum(sums_two[:, 1] * gate_two, axis=0)
    shift2_grad = sums_two[:, 2]
    scale2_grad = sums_two[:, 3] * norm_two
    mlpnorm = jnp.sum(sums_two[:, 3] * (1.0 + scale_two), axis=0)
    gate1_grad = sums_two[:, 4]
    mod_late = jnp.zeros_like(gate1_grad)
    mod_early = jnp.concatenate(
        [mod_late, mod_late, gate1_grad, shift2_grad, scale2_grad, gate2_grad], axis=1
    )
    group = 2 * fs
    early = jnp.concatenate(
        [
            mod_early[0].reshape(group, -1),
            mod_early[1].reshape(group, -1),
            mlpnorm.reshape(group, -1),
            downbias.reshape(group, -1),
            (sums_two[0, 5] + sums_two[1, 5]).reshape(group, -1),
        ],
        axis=1,
    )
    used = early.shape[1]
    early = jnp.pad(early, ((0, 0), (0, -used % 1024))).reshape(group, -1, 128)

    mixed_grad, proj_low, early, ff_got = lax.optimization_barrier(
        (mixed_grad, proj_low, early, ff_got)
    )
    proj_got = exchange_to_shard(proj_low)
    dq_rest, kv_rest, send_rest = bwd(rest, g=mixed_grad)
    got_rest = lax.ppermute(send_rest, "ctx", SWAP)
    got_rest, proj_got = lax.optimization_barrier((got_rest, proj_got))

    hidden_grad, sums_one = last_call(
        own_index, dq_own, kv_own, got_own, dq_rest, kv_rest, got_rest, w_attn, hid, dh_one.reshape(hid.shape), vec
    )
    ff_shard = jnp.sum(ff_got.astype(f32), axis=0)
    attn_shard = jnp.sum(proj_got.astype(f32), axis=0)

    late = sums_one[:, 0:2].reshape(1, -1, 128)
    both = jnp.concatenate([early, jnp.broadcast_to(late, (group,) + late.shape[1:])], axis=1)
    both = lax.all_to_all(both, FC, split_axis=0, concat_axis=0, tiled=True)
    early = both[:, : early.shape[1]]
    late_all = both[:, early.shape[1] :].reshape(fs, 2, 2, 2, width)
    late_all = late_all[:, 0] + late_all[:, 1]
    late_mod = late_all * jnp.stack([jnp.ones_like(norm_one), norm_one])
    late_mod = jnp.pad(late_mod.reshape(fs * 2, 2 * width), ((0, 0), (0, 4 * width)))
    place = lax.axis_index(FC)
    early = early.reshape(fs, 2, -1)
    early = early[:, 0] + early[:, 1]
    mod_parts = early[:, : 2 * ada_cols].reshape(fs * 2, ada_cols) + lax.dynamic_slice_in_dim(
        late_mod, place * ada_cols, ada_cols, axis=1
    )
    grad_ada = lax.dot_general(
        cond_all.reshape(fs * 2, cond_w),
        mod_parts,
        (((0,), (0,)), ((), ())),
        precision=highest,
        preferred_element_type=f32,
    )
    grad_adabias = jnp.sum(mod_parts, axis=0)
    tail = jnp.sum(early[:, 2 * ada_cols : used], axis=0).reshape(3, shard)
    scale_all = modulation_all[:, :, width : 2 * width]
    attnnorm = jnp.sum(late_all[:, :, 1] * (1.0 + scale_all), axis=(0, 1))
    attnnorm = lax.dynamic_slice_in_dim(attnnorm, place * shard, shard, axis=0)
    mod_grad = mod_early + jnp.pad(
        jnp.concatenate([sums_one[:, 0], sums_one[:, 1] * norm_one], axis=1), ((0, 0), (0, 4 * width))
    )
    cond_part = jnp.einsum(
        "mfc,fck->mk",
        mod_grad.reshape(2, group, ada_cols),
        ada_full,
        precision=highest,
    )
    cond_grad = cond_part + lax.ppermute(cond_part, "ctx", SWAP)

    grad_qkv = jnp.stack([attn_shard[:, j * PAD : j * PAD + heads_w] for j in range(3)])
    grad_attn = jnp.concatenate(
        [attn_shard[:, j * PAD + heads_w : (j + 1) * PAD] for j in range(3)], axis=1
    ).T
    return (
        block_out.reshape(hidden_in.shape),
        hidden_grad[:, None],
        cond_grad[:, None],
        grad_qkv,
        grad_attn,
        ff_shard[:, : ff_shard.shape[1] // 2],
        tail[2],
        ff_shard[:, ff_shard.shape[1] // 2 :].T,
        tail[1],
        grad_ada,
        grad_adabias,
        attnnorm,
        tail[0],
    )


def solution(mesh):
    tokens = P(None, "fsdp", "ctx", None)
    per_seq = P(None, "fsdp", None)
    weights = (
        P(None, FC, "tp"),
        P("tp", FC),
        P(FC, "tp"),
        P(("tp",) + FC),
        P("tp", FC),
        P(FC),
        P(None, FC),
        P(FC),
        P(FC),
        P(FC),
    )
    return jax.shard_map(
        on_device,
        mesh=mesh,
        in_specs=(tokens, per_seq, per_seq, per_seq, tokens) + weights,
        out_specs=(tokens, tokens, per_seq) + weights,
        check_vma=False,
    )
```

```python
import functools
import math

import jax
import jax.numpy as jnp
from jax import lax
from jax.experimental import pallas as pl
from jax.experimental.pallas import tpu as pltpu
from jax.sharding import PartitionSpec as P

HEAD_DIM = 64
HEADS_PER_BLOCK = 3
PAD = 256
NORM_EPS = 1e-05
GELU_C = math.sqrt(2.0 / math.pi)
bf16 = jnp.bfloat16
f32 = jnp.float32
FC = ("fsdp", "ctx")
SWAP = [(0, 1), (1, 0)]
ALONG_X = [(0, 1), (1, 0), (2, 3), (3, 2)]
ALONG_Y = [(0, 2), (2, 0), (1, 3), (3, 1)]
MIB = 1 << 20
LIMIT = 60


def dot_nn(a, b):
    return lax.dot_general(a, b, (((1,), (0,)), ((), ())), preferred_element_type=f32)


def dot_nt(a, b):
    return lax.dot_general(a, b, (((1,), (1,)), ((), ())), preferred_element_type=f32)


def params(limit, axes=1):
    return pltpu.CompilerParams(
        dimension_semantics=("arbitrary",) * axes, vmem_limit_bytes=limit * MIB
    )


def cost(flops, nbytes, trans=0):
    return pl.CostEstimate(flops=flops, bytes_accessed=nbytes, transcendentals=trans)


def whole(shape, **kw):
    return pl.BlockSpec(shape, lambda *_: (0,) * len(shape), **kw)


def turn(x, first):
    return jnp.where(first, pltpu.roll(x, 96, 1), pltpu.roll(x, 32, 1))


def interleave(rank, own_ref, oth_ref, out_ref, col):
    count, shard = own_ref.shape[0], own_ref.shape[2]
    cols = slice(col, col + out_ref.shape[1])
    for c in range(2):

        @pl.when(rank == c)
        def _():
            for f in range(count):
                at = 2 * f * shard
                mine, theirs = at + c * shard, at + (1 - c) * shard
                out_ref[mine : mine + shard, :] = own_ref[f, 0, :, cols]
                out_ref[theirs : theirs + shard, :] = oth_ref[f, 0, :, cols]


def lay_weight(flag_ref, t, tn, refs, out_ref, held):
    half = tn // 2
    if len(refs) == 2:
        own_ref, oth_ref = refs if held else [ref.at[:, t : t + 1] for ref in refs]
        interleave(flag_ref[1], own_ref, oth_ref, out_ref, 0)
        return
    shard = refs[0].shape[1]

    def copy(src, row):
        out_ref[pl.ds(pl.multiple_of(row * shard, shard), shard), :] = src

    for core in range(2):
        parts = refs[7 * core : 7 * core + 7]
        for k in range(4):
            row = flag_ref[2 + 4 * core + k]
            if k == 0:
                copy(parts[0][0 if held else t], row)
            elif held:
                pl.when(t < half)(lambda: copy(parts[2 * k - 1][0], row))
                pl.when(t >= half)(lambda: copy(parts[2 * k][0], row))
            else:
                copy(parts[2 * k - 1 if t < half else 2 * k][t % half], row)


def weight_specs(weights, tn):
    width = weights[0].shape[-1]
    shard = weights[0].shape[-2]
    if len(weights) == 2:
        fs = weights[0].shape[0]
        return [pl.BlockSpec((fs, 1, shard, width), lambda t, r: (0, t, 0, 0))] * 2
    half = tn // 2
    at = [lambda t, r: (t, 0, 0)]
    at += [lambda t, r: (jnp.minimum(t, half - 1), 0, 0), lambda t, r: (jnp.maximum(t - half, 0), 0, 0)] * 3
    return [pl.BlockSpec((1, shard, width), index) for index in at * 2]


def qkv_kernel(flag_ref, x_ref, cos_ref, sin_ref, *refs):
    q_ref, k_ref, v_ref, wo_ref, w_ref = refs[-5:]
    rows, width = x_ref.shape[1:]
    lane = lax.broadcasted_iota(jnp.int32, (rows, 128), 1)
    first = (lane & (HEAD_DIM - 1)) < HEAD_DIM // 2
    low = lane < HEAD_DIM
    lay_weight(flag_ref, pl.program_id(0), pl.num_programs(0), refs[:-5], w_ref, True)
    for j in range(3):
        hole = (j + 1) * PAD - HEAD_DIM
        wo_ref[0, :, j * HEAD_DIM : (j + 1) * HEAD_DIM] = w_ref[:, hole : hole + HEAD_DIM]
    wo_ref[0, :, PAD - HEAD_DIM :] = jnp.zeros((width, HEAD_DIM), bf16)

    def rotated(y, half, ch):
        z = y[:, 128 * ch : 128 * ch + 128]
        return z * cos_ref[half] + turn(z, first) * sin_ref[half]

    for b in range(4):
        x = x_ref[b]
        y = dot_nn(x, w_ref[:, PAD : 2 * PAD])
        k_ref[b, :, 0:128] = rotated(y, b // 2, 0).astype(bf16)
        k_ref[b, :, 128:PAD] = rotated(y, b // 2, 1).astype(bf16)
        v_ref[b] = dot_nn(x, w_ref[:, 2 * PAD : 3 * PAD]).astype(bf16)
        if b < 2:
            y = dot_nn(x, w_ref[:, 0:PAD])
            scale = HEAD_DIM ** (-0.5)
            q_ref[b, :, 0:128] = rotated(y, 0, 0).astype(bf16) * scale
            q_ref[b, :, 128:PAD] = jnp.where(low, rotated(y, 0, 1), 0.0).astype(bf16) * scale


def qkv_call(flags, tn, x_all, weights, cos, sin):
    blocks, rows, width = x_all.shape
    out = lambda n: pl.BlockSpec((n, rows, PAD), lambda t, r: (0, 0, t))
    one = pl.Buffered(1)
    return pl.pallas_call(
        qkv_kernel,
        grid_spec=pltpu.PrefetchScalarGridSpec(
            num_scalar_prefetch=1,
            grid=(tn,),
            in_specs=[
                whole((blocks, rows, width), pipeline_mode=one),
                whole((2, rows, 128), pipeline_mode=one),
                whole((2, rows, 128), pipeline_mode=one),
                *weight_specs(weights, tn),
            ],
            out_specs=[
                out(2),
                out(blocks),
                out(blocks),
                pl.BlockSpec((1, width, PAD), lambda t, r: (t, 0, 0)),
            ],
            scratch_shapes=[pltpu.VMEM((width, 3 * PAD), bf16)],
        ),
        out_shape=[
            jax.ShapeDtypeStruct((2, rows, tn * PAD), bf16),
            jax.ShapeDtypeStruct((blocks, rows, tn * PAD), bf16),
            jax.ShapeDtypeStruct((blocks, rows, tn * PAD), bf16),
            jax.ShapeDtypeStruct((tn, width, PAD), bf16),
        ],
        compiler_params=params(LIMIT),
        cost_estimate=cost(2 * blocks * rows * width * 640 * tn, 16 * MIB),
        name="qkv_rope",
    )(flags, x_all, cos, sin, *weights)


def pack_kernel(qkv_ref, attn_ref, a_ref):
    heads_w = qkv_ref.shape[2]
    for j in range(3):
        a_ref[:, j * PAD : j * PAD + heads_w] = qkv_ref[j]
        a_ref[:, j * PAD + heads_w : (j + 1) * PAD] = attn_ref[:, j * HEAD_DIM : (j + 1) * HEAD_DIM]


def pack_weights(qkv_weight, attn_weight):
    shard = qkv_weight.shape[1]
    attn_t = attn_weight.T
    if shard % 16:
        pieces = []
        for j in range(3):
            pieces += [qkv_weight[j], attn_t[:, j * HEAD_DIM : (j + 1) * HEAD_DIM]]
        return jnp.concatenate(pieces, axis=1)
    return pl.pallas_call(
        pack_kernel,
        out_shape=jax.ShapeDtypeStruct((shard, 3 * PAD), bf16),
        name="pack_weights",
    )(qkv_weight, attn_t)


QB = 256
NEG = -1e30


def head_lanes(x, h):
    if h == 2:
        return x
    lane = lax.broadcasted_iota(jnp.int32, x.shape, 1)
    keep = (lane < HEAD_DIM) if h == 0 else (lane >= HEAD_DIM)
    return jnp.where(keep, x, jnp.zeros_like(x))


def in_terms(base, lane, at, x):
    hi = x.astype(bf16).astype(f32)
    rest = x - hi
    mid = rest.astype(bf16).astype(f32)
    out = jnp.where(lane == at + 1, mid, jnp.where(lane == at + 2, rest - mid, base))
    return jnp.where(lane == at, hi, out).astype(bf16)


def attn_fwd_kernel(q_ref, k_ref, v_ref, sq_ref, sk_ref, o_ref, lo_ref, x_ref):
    rows = q_ref.shape[1]
    keys = 2 * rows
    cols_k = sk_ref[0]
    ones = jnp.ones((keys, 128), bf16)
    part = lambda ref, c: ref[..., 128 * c : 128 * c + 128].reshape(keys, 128)
    kx = [jnp.concatenate([part(k_ref, c), cols_k], axis=1) for c in range(2)]
    vx = [jnp.concatenate([part(v_ref, c), ones], axis=1) for c in range(2)]
    lane = lax.broadcasted_iota(jnp.int32, (QB, 128), 1)
    low = lane < HEAD_DIM
    for qb in range(rows // QB):
        span = pl.ds(qb * QB, QB)
        cols_q = sq_ref[0, span, :]
        outs = []
        for h in range(HEADS_PER_BLOCK):
            c = h // 2
            qh = head_lanes(q_ref[0, span, 128 * c : 128 * c + 128], h)
            s = dot_nt(jnp.concatenate([qh, cols_q], axis=1), kx[c])
            top = jnp.max(s, axis=1, keepdims=True)
            o = dot_nn(jnp.exp(s - top).astype(bf16), vx[c])
            total = o[:, 128:]
            outs.append(o[:, :128] / total)
            lse = top + jnp.log(total[:, 0:1])
            x_ref[0, 0, h, span, :] = in_terms(cols_q.astype(f32), lane, 128 - 3, -lse)
        for c, o in enumerate((jnp.where(low, outs[0], outs[1]), outs[2])):
            hi = o.astype(bf16)
            o_ref[0, span, 128 * c : 128 * c + 128] = hi
            lo_ref[0, span, 128 * c : 128 * c + 128] = (o - hi.astype(f32)).astype(bf16)


def attn_fwd_call(q, k, v, cols_q, cols_k):
    _, rows, wide = q.shape
    tn = wide // PAD
    k4 = k.reshape(2, 2, rows, wide)
    v4 = v.reshape(2, 2, rows, wide)
    mine = pl.BlockSpec((1, rows, PAD), lambda m, t: (m, 0, t))
    all_keys = pl.BlockSpec((2, 1, rows, PAD), lambda m, t: (0, m, 0, t))
    return pl.pallas_call(
        attn_fwd_kernel,
        grid=(2, tn),
        in_specs=[
            mine,
            all_keys,
            all_keys,
            pl.BlockSpec((1, rows, 128), lambda m, t: (m, 0, 0)),
            pl.BlockSpec((1, 2 * rows, 128), lambda m, t: (m, 0, 0)),
        ],
        out_specs=[
            mine,
            mine,
            pl.BlockSpec((1, 1, HEADS_PER_BLOCK, rows, 128), lambda m, t: (m, t, 0, 0, 0)),
        ],
        out_shape=[
            jax.ShapeDtypeStruct((2, rows, wide), bf16),
            jax.ShapeDtypeStruct((2, rows, wide), bf16),
            jax.ShapeDtypeStruct((2, tn, HEADS_PER_BLOCK, rows, 128), bf16),
        ],
        compiler_params=params(LIMIT, 2),
        cost_estimate=cost(
            2 * tn * 3 * 2 * 2 * rows * 2 * rows * 256, 18 * MIB, 2 * tn * 3 * rows * 2 * rows
        ),
        name="attn_fwd",
    )(q, k4, v4, cols_q, cols_k)


def attn_bwd_kernel(
    tl_ref, q_ref, k_ref, v_ref, g_ref, o_ref, lo_ref, x_ref, sk_ref, cos_ref, sin_ref, dq_ref, own_ref, oth_ref
):
    rows = q_ref.shape[1]
    keys = 2 * rows
    cols_k = sk_ref[0]
    lane = lax.broadcasted_iota(jnp.int32, (QB, 128), 1)
    low = lane < HEAD_DIM
    key_lane = lax.broadcasted_iota(jnp.int32, (keys, 128), 1)
    terms = jnp.where(key_lane < 3, 1.0, 0.0).astype(bf16)

    def unrotated(y, lanes, cos, sin):
        return y * cos - turn(y, (lanes & (HEAD_DIM - 1)) < HEAD_DIM // 2) * sin

    for c in range(2):
        ch = slice(128 * c, 128 * c + 128)
        kc = k_ref[..., ch].reshape(keys, 128)
        kt = kc.T
        kx = jnp.concatenate([kc, cols_k], axis=1)
        vx = jnp.concatenate([v_ref[..., ch].reshape(keys, 128), terms], axis=1)
        dk = jnp.zeros((keys, 128), f32)
        dv = jnp.zeros((keys, 128), f32)
        for qb in range(rows // QB):
            span = pl.ds(qb * QB, QB)
            qc = q_ref[0, span, ch]
            gc = g_ref[0, span, ch]
            prod = gc.astype(f32) * (o_ref[0, span, ch].astype(f32) + lo_ref[0, span, ch].astype(f32))
            dqs = []
            for h in (0, 1) if c == 0 else (2,):
                qh = head_lanes(qc, h)
                gh = head_lanes(gc, h)
                inner = jnp.sum(head_lanes(prod, h), axis=1, keepdims=True)
                gx = in_terms(jnp.zeros((QB, 128), f32), lane, 0, -inner)
                p = jnp.exp(dot_nt(kx, jnp.concatenate([qh, x_ref[0, 0, h, span, :]], axis=1)))
                ds = (p * dot_nt(vx, jnp.concatenate([gh, gx], axis=1))).astype(bf16)
                dv += dot_nn(p.astype(bf16), gh)
                dk += dot_nn(ds, qh)
                dqs.append(dot_nn(kt, ds).T * HEAD_DIM ** (-0.5))
            dq = jnp.where(low, dqs[0], dqs[1] if c == 0 else 0.0)
            dq_ref[0, 0, span, ch] = unrotated(dq, lane, cos_ref[span, :], sin_ref[span, :]).astype(bf16)
        dk = unrotated(dk, key_lane, cos_ref[...], sin_ref[...])
        for half, ref in enumerate((own_ref, oth_ref)):
            some = slice(half * rows, (half + 1) * rows)
            ref[0, 0, 0, :, ch] = dk[some].astype(bf16)
            ref[0, 1, 0, :, ch] = dv[some].astype(bf16)


def attn_bwd_call(tlist, g, q, k, v, o, lo, x, cols_k, cos, sin):
    _, rows, wide = q.shape
    nt = tlist.shape[0]
    k4 = k.reshape(2, 2, rows, wide)
    v4 = v.reshape(2, 2, rows, wide)
    mine = pl.BlockSpec((1, rows, PAD), lambda i, m, tl: (m, 0, tl[i]))
    all_keys = pl.BlockSpec((2, 1, rows, PAD), lambda i, m, tl: (0, m, 0, tl[i]))
    kv_out = pl.BlockSpec((1, 2, 1, rows, PAD), lambda i, m, tl: (i, 0, m, 0, 0))
    return pl.pallas_call(
        attn_bwd_kernel,
        grid_spec=pltpu.PrefetchScalarGridSpec(
            num_scalar_prefetch=1,
            grid=(nt, 2),
            in_specs=[
                mine,
                all_keys,
                all_keys,
                mine,
                mine,
                mine,
                pl.BlockSpec(
                    (1, 1, HEADS_PER_BLOCK, rows, 128), lambda i, m, tl: (m, tl[i], 0, 0, 0)
                ),
                pl.BlockSpec((1, 2 * rows, 128), lambda i, m, tl: (m, 0, 0)),
                whole((2 * rows, 128)),
                whole((2 * rows, 128)),
            ],
            out_specs=[
                pl.BlockSpec((1, 1, rows, PAD), lambda i, m, tl: (i, m, 0, 0)),
                kv_out,
                kv_out,
            ],
        ),
        out_shape=[
            jax.ShapeDtypeStruct((nt, 2, rows, PAD), bf16),
            jax.ShapeDtypeStruct((nt, 2, 2, rows, PAD), bf16),
            jax.ShapeDtypeStruct((nt, 2, 2, rows, PAD), bf16),
        ],
        compiler_params=params(LIMIT, 2),
        cost_estimate=cost(
            2 * nt * 3 * 5 * 2 * rows * 2 * rows * 256, 5 * nt * MIB, 2 * nt * 3 * rows * 2 * rows
        ),
        name="attn_bwd",
    )(tlist, q, k4, v4, g, o, lo, x, cols_k, cos.reshape(2 * rows, 128), sin.reshape(2 * rows, 128))


RB = 512
UNROLL = 1


def dot_tn(a, b):
    return lax.dot_general(a, b, (((0,), (0,)), ((), ())), preferred_element_type=f32)


def normalise(h):
    mean = jnp.mean(h, axis=-1, keepdims=True)
    cent = h - mean
    var = jnp.mean(cent * cent, axis=-1, keepdims=True)
    rstd = lax.rsqrt(var + NORM_EPS)
    return cent * rstd, rstd


def block_kernel(
    flag_ref,
    mix_ref,
    wout_ref,
    hid_ref,
    vec_ref,
    cot_ref,
    mask_ref,
    up_ref,
    dn_ref,
    ub_ref,
    out_ref,
    dh_ref,
    mg_ref,
    sum_ref,
    wff_ref,
    wat_ref,
    h1_ref,
    br_ref,
    x_ref,
    g_ref,
    down_ref,
    ng_ref,
    act_ref,
    ul_ref,
):
    j = pl.program_id(0)
    tn = pl.num_programs(0)
    own = flag_ref[0]
    rows = x_ref.shape[0]
    width = x_ref.shape[1]
    ff = act_ref.shape[1]
    steps = rows // RB
    half = steps // 2
    up = up_ref[0]
    dn = dn_ref[0]

    def vec(m, i):
        return vec_ref[m, i : i + 1, :]

    @pl.when(j == 0)
    def _():
        for m in range(2):

            def before(i, carry):
                span = pl.ds((m * half + i) * RB, RB)
                acc = dot_nt(mix_ref[span, 0:PAD], wout_ref[0])
                for t in range(1, wout_ref.shape[0]):
                    acc += dot_nt(mix_ref[span, t * PAD : (t + 1) * PAD], wout_ref[t])
                br_ref[span, :] = acc
                h1 = hid_ref[span, :].astype(f32) + vec(m, 0) * acc
                h1_ref[span, :] = h1
                n, _ = normalise(h1)
                x_ref[span, :] = (n * vec(m, 1) + vec(m, 2)).astype(bf16)
                cot = cot_ref[span, :].astype(f32) * mask_ref[span, :]
                g_ref[span, :] = (cot * vec(m, 3)).astype(bf16)
                return carry

            lax.fori_loop(0, half, before, 0)

    bias = ub_ref[0]

    def step(i, carry):
        span = pl.ds(i * RB, RB)
        u = dot_nn(x_ref[span, :], up) + bias
        da = dot_nn(g_ref[span, :], dn)
        u2 = u * u
        th = jnp.tanh(GELU_C * u * (1.0 + 0.044715 * u2))
        half_up = 0.5 * (1.0 + th)
        act = (u * half_up).astype(bf16)
        slope = half_up + (0.5 * GELU_C) * u * (1.0 - th * th) * (1.0 + (3 * 0.044715) * u2)
        ul = (da * slope).astype(bf16)
        d = dot_nt(act, dn)
        n = dot_nt(ul, up)

        @pl.when(j == 0)
        def _():
            down_ref[span, :] = d
            ng_ref[span, :] = n

        @pl.when(j > 0)
        def _():
            down_ref[span, :] += d
            ng_ref[span, :] += n

        @pl.when(j == own)
        def _():
            act_ref[span, :] = act
            ul_ref[span, :] = ul

        return carry

    lax.fori_loop(0, steps, step, 0, unroll=UNROLL)

    @pl.when(j == tn - 1)
    def _():
        sum_ref[...] = jnp.zeros_like(sum_ref)
        for m in range(2):

            def after(i, carry):
                span = pl.ds((m * half + i) * RB, RB)
                cot = cot_ref[span, :].astype(f32) * mask_ref[span, :]
                down = down_ref[span, :] + vec(m, 4)
                h1 = h1_ref[span, :]
                out_ref[span, :] = (h1 + vec(m, 3) * down).astype(bf16)
                n, rstd = normalise(h1)
                g = ng_ref[span, :]
                gn = g * n
                e = g * vec(m, 1)
                en = gn * vec(m, 1)
                dh = cot + rstd * (
                    e - jnp.mean(e, axis=-1, keepdims=True) - n * jnp.mean(en, axis=-1, keepdims=True)
                )
                dh_ref[span, :] = dh
                bl = (dh * vec(m, 0)).astype(bf16)
                x_low = bl
                for t in range(wout_ref.shape[0]):
                    mg_ref[span, t * PAD : (t + 1) * PAD] = dot_nn(bl, wout_ref[t]).astype(bf16)
                parts = (cot * down, cot, g, gn, dh * br_ref[span, :])
                for r, part in enumerate(parts):
                    sum_ref[m, r : r + 1, :] += jnp.sum(part, axis=0, keepdims=True)
                sum_ref[m, 5:6, :] += jnp.sum(ul_ref[span, :].astype(f32), axis=0, keepdims=True)
                br_ref[span, :] = x_low.astype(f32)
                return carry

            lax.fori_loop(0, half, after, 0)

        for col in range(0, ff, PAD):
            cols = slice(col, col + PAD)
            wff_ref[:, cols] = dot_tn(x_ref[...], ul_ref[:, cols]).astype(bf16)
            wff_ref[:, ff + col : ff + col + PAD] = dot_tn(g_ref[...], act_ref[:, cols]).astype(bf16)
        mine = mix_ref[:, pl.ds(pl.multiple_of(own * PAD, PAD), PAD)]
        wat_ref[...] = dot_tn(br_ref[...].astype(bf16), mine).astype(bf16)


def block_call(flags, mixed, w_out, hid, vec, cot, mask_col, w_ff, up_bias):
    rows, wide = mixed.shape
    width = hid.shape[1]
    tn, _, ff = w_ff.shape
    ff = ff // 2
    one = pl.Buffered(1)
    const = lambda *shape: whole(shape, pipeline_mode=one)
    tokens = lambda dtype, w: pltpu.VMEM((rows, w), dtype)
    return pl.pallas_call(
        block_kernel,
        grid_spec=pltpu.PrefetchScalarGridSpec(
            num_scalar_prefetch=1,
            grid=(tn,),
            in_specs=[
                const(rows, wide),
                const(tn, width, PAD),
                const(rows, width),
                const(2, 8, width),
                const(rows, width),
                const(rows, 1),
                pl.BlockSpec((1, width, ff), lambda j, o: (j, 0, 0)),
                pl.BlockSpec((1, width, ff), lambda j, o: (j, 0, 1)),
                pl.BlockSpec((1, 1, ff), lambda j, o: (lax.rem(o[0] - j + tn, tn), 0, 0)),
            ],
            out_specs=[
                const(rows, width),
                const(rows, width),
                const(rows, wide),
                const(2, 8, width),
                const(width, 2 * ff),
                const(width, PAD),
            ],
            scratch_shapes=[
                tokens(f32, width),
                tokens(f32, width),
                tokens(bf16, width),
                tokens(bf16, width),
                tokens(f32, width),
                tokens(f32, width),
                tokens(bf16, ff),
                tokens(bf16, ff),
            ],
        ),
        out_shape=[
            jax.ShapeDtypeStruct((rows, width), bf16),
            jax.ShapeDtypeStruct((rows, width), f32),
            jax.ShapeDtypeStruct((rows, wide), bf16),
            jax.ShapeDtypeStruct((2, 8, width), f32),
            jax.ShapeDtypeStruct((width, 2 * ff), bf16),
            jax.ShapeDtypeStruct((width, PAD), bf16),
        ],
        compiler_params=params(LIMIT),
        cost_estimate=cost(
            4 * 2 * rows * width * ff * tn + 8 * rows * width * width, 32 * MIB, rows * ff * tn
        ),
        name="block_both",
    )(flags, mixed, w_out, hid, vec, cot, mask_col, w_ff, w_ff, up_bias)


def norm_kernel(hid_ref, oth_ref, vec_ref, out_ref):
    gain, shift = vec_ref[0, 5:6, :], vec_ref[0, 6:7, :]
    for half, ref in enumerate((hid_ref, oth_ref)):
        n, _ = normalise(ref[0].astype(f32))
        out_ref[half, 0] = (n * gain + shift).astype(bf16)


def norm_call(hid, other, vec):
    _, rows, width = hid.shape
    row = pl.BlockSpec((1, RB // 2, width), lambda m, i: (m, i, 0))
    out = pl.pallas_call(
        norm_kernel,
        grid=(2, 2 * rows // RB),
        in_specs=[row, row, pl.BlockSpec((1, 8, width), lambda m, i: (m, 0, 0))],
        out_specs=pl.BlockSpec((2, 1, RB // 2, width), lambda m, i: (0, m, i, 0)),
        out_shape=jax.ShapeDtypeStruct((2, 2, rows, width), bf16),
        compiler_params=params(LIMIT, 2),
        cost_estimate=cost(20 * rows * width, 7 * MIB),
        name="first_norm",
    )(hid, other, vec)
    return out.reshape(4, rows, width)


def table_kernel(flag_ref, seg_ref, cos_ref, sin_ref, sq_ref, sk_ref):
    rows = seg_ref.shape[3]
    lane = lax.broadcasted_iota(jnp.int32, (rows, 128), 1)
    fixed = lane >= 128 - 3
    pair = (lane & (HEAD_DIM // 2 - 1)).astype(f32)
    freq = jnp.exp(pair * (-2.0 * math.log(10000.0) / HEAD_DIM))
    sign = jnp.where((lane & (HEAD_DIM - 1)) < HEAD_DIM // 2, -1.0, 1.0)
    row = lax.broadcasted_iota(jnp.int32, (rows, 128), 0)
    for half in range(2):
        angle = (row + flag_ref[half]).astype(f32) * freq
        cos_ref[half] = jnp.cos(angle)
        sin_ref[half] = jnp.sin(angle) * sign
        for m in range(2):
            ids = jnp.broadcast_to(seg_ref[m, half].astype(f32), (128, rows)).T
            same = (ids == lane.astype(f32)) | fixed
            sk_ref[m, half] = jnp.where(same, 1.0, 0.0).astype(bf16)
            if half == 0:
                sq_ref[m] = jnp.where(same, 0.0, NEG).astype(bf16)


def table_call(starts, segments):
    _, _, _, rows = segments.shape
    cos, sin, cols_q, cols_k = pl.pallas_call(
        table_kernel,
        grid_spec=pltpu.PrefetchScalarGridSpec(
            num_scalar_prefetch=1,
            grid=(1,),
            in_specs=[whole(segments.shape)],
            out_specs=[
                whole((2, rows, 128)),
                whole((2, rows, 128)),
                whole((2, rows, 128)),
                whole((2, 2, rows, 128)),
            ],
        ),
        out_shape=[
            jax.ShapeDtypeStruct((2, rows, 128), f32),
            jax.ShapeDtypeStruct((2, rows, 128), f32),
            jax.ShapeDtypeStruct((2, rows, 128), bf16),
            jax.ShapeDtypeStruct((2, 2, rows, 128), bf16),
        ],
        compiler_params=params(LIMIT),
        cost_estimate=cost(100 * 2 * rows * 128, 3 * MIB),
        name="tables",
    )(starts, segments)
    return cos, sin, cols_q, cols_k.reshape(2, 2 * rows, 128)


def proj_grad_kernel(n_ref, dq_ref, own_ref, oth_ref, wat_ref, out_ref):
    heads_w = PAD - HEAD_DIM
    rows = dq_ref.shape[0]
    for j in range(3):
        if j == 0:
            part = dot_tn(n_ref[0], dq_ref[...])
        else:
            part = dot_tn(n_ref[0], own_ref[j - 1]) + dot_tn(n_ref[1], oth_ref[j - 1])
        out_ref[:, j * PAD : j * PAD + heads_w] = part[:, :heads_w].astype(bf16)
        out_ref[:, j * PAD + heads_w : (j + 1) * PAD] = wat_ref[
            :, j * HEAD_DIM : (j + 1) * HEAD_DIM
        ]


def proj_grad_call(normed, dq, kv_own, kv_oth, wat):
    _, rows, width = normed.shape
    return pl.pallas_call(
        proj_grad_kernel,
        out_shape=jax.ShapeDtypeStruct((width, 3 * PAD), bf16),
        compiler_params=pltpu.CompilerParams(vmem_limit_bytes=LIMIT * MIB),
        cost_estimate=cost(2 * 5 * rows * width * PAD, 10 * MIB),
        name="proj_grad",
    )(normed, dq, kv_own, kv_oth, wat)


def last_kernel(
    flag_ref,
    dqo_ref,
    kvo_ref,
    rvo_ref,
    dqr_ref,
    kvr_ref,
    rvr_ref,
    hid_ref,
    dh_ref,
    vec_ref,
    *refs,
):
    out_ref, sum_ref, w_ref = refs[-3:]
    first = pl.program_id(1) == 0
    own = flag_ref[0]
    tn = w_ref.shape[0]

    @pl.when(first & (pl.program_id(0) == 0))
    def _():
        for t in range(tn):
            lay_weight(flag_ref, t, tn, refs[:-3], w_ref.at[t], False)

    acc = jnp.zeros(dh_ref.shape[1:], f32)
    for t in range(tn):
        mine = own == t
        slot = jnp.minimum(lax.rem(t - own - 1 + 2 * tn, tn), tn - 2)
        dq = jnp.where(mine, dqo_ref[0, 0], dqr_ref[slot, 0])
        acc += dot_nt(dq, w_ref[t, :, 0:PAD])
        for j in range(2):
            d = jnp.where(mine, kvo_ref[0, j, 0], kvr_ref[slot, j, 0]).astype(f32) + jnp.where(
                mine, rvo_ref[0, j, 0], rvr_ref[slot, j, 0]
            ).astype(f32)
            acc += dot_nt(d.astype(bf16), w_ref[t, :, (j + 1) * PAD : (j + 2) * PAD])
    gain1 = vec_ref[0, 5:6, :]
    n, rstd = normalise(hid_ref[0].astype(f32))
    gn = acc * n
    e = acc * gain1
    en = gn * gain1
    out_ref[0] = dh_ref[0] + rstd * (
        e - jnp.mean(e, axis=-1, keepdims=True) - n * jnp.mean(en, axis=-1, keepdims=True)
    )

    @pl.when(first)
    def _():
        sum_ref[...] = jnp.zeros_like(sum_ref)

    sum_ref[0, 0:1, :] += jnp.sum(acc, axis=0, keepdims=True)
    sum_ref[0, 1:2, :] += jnp.sum(gn, axis=0, keepdims=True)


def last_call(flags, dqo, kvo, rvo, dqr, kvr, rvr, weights, hid, dh, vec):
    _, rows, width = hid.shape
    nt = dqr.shape[0]
    tn = nt + 1
    row = pl.BlockSpec((1, RB, width), lambda m, i, o: (m, i, 0))
    vecs = pl.BlockSpec((1, 8, width), lambda m, i, o: (m, 0, 0))
    q_spec = lambda n: pl.BlockSpec((n, 1, RB, PAD), lambda m, i, o: (0, m, i, 0))
    kv_spec = lambda n: pl.BlockSpec((n, 2, 1, RB, PAD), lambda m, i, o: (0, 0, m, i, 0))
    return pl.pallas_call(
        last_kernel,
        grid_spec=pltpu.PrefetchScalarGridSpec(
            num_scalar_prefetch=1,
            grid=(2, rows // RB),
            in_specs=[
                q_spec(1),
                kv_spec(1),
                kv_spec(1),
                q_spec(nt),
                kv_spec(nt),
                kv_spec(nt),
                row,
                row,
                vecs,
                *[whole(w.shape, pipeline_mode=pl.Buffered(1)) for w in weights],
            ],
            out_specs=[row, vecs],
            scratch_shapes=[pltpu.VMEM((tn, width, 3 * PAD), bf16)],
        ),
        out_shape=[
            jax.ShapeDtypeStruct((2, rows, width), f32),
            jax.ShapeDtypeStruct((2, 8, width), f32),
        ],
        compiler_params=params(LIMIT, 2),
        cost_estimate=cost(2 * 2 * rows * width * tn * 3 * PAD, 24 * MIB),
        name="first_norm_bwd",
    )(flags, dqo, kvo, rvo, dqr, kvr, rvr, hid, dh, vec, *weights)


def spread(x, axes):
    count = lax.axis_size(axes)
    many = jnp.broadcast_to(x[None], (count,) + x.shape)
    return lax.all_to_all(many, axes, split_axis=0, concat_axis=0, tiled=True)


def join_cores(part, other, rank):
    fs, tn, rows, width = part.shape
    both = jnp.stack([jnp.where(rank == 0, part, other), jnp.where(rank == 0, other, part)], axis=1)
    return both.transpose(2, 0, 1, 3, 4).reshape(1, tn, fs * 2 * rows, width)


def bf16_terms(x):
    hi = lax.reduce_precision(x, 8, 7)
    mid = lax.reduce_precision(x - hi, 8, 7)
    return jnp.stack([hi, mid, x - hi - mid]).astype(bf16)


def gather_rows(row):
    tn = lax.axis_size("tp")
    got = [row]
    for step in range(1, tn):
        got.append(lax.ppermute(row, "tp", [(i, (i + step) % tn) for i in range(tn)]))
    return jnp.stack(got).astype(f32)


def exchange_to_shard(grad):
    group = lax.axis_size(FC)
    parts = grad.reshape(group, -1, grad.shape[1])
    return lax.all_to_all(parts, FC, split_axis=0, concat_axis=0, tiled=True)


def on_device(
    hidden_in,
    cond_vec,
    segment_ids,
    pad_mask,
    out_cot,
    qkv_weight,
    attn_weight,
    up_weight,
    up_bias,
    down_weight,
    down_bias,
    ada_weight,
    ada_bias,
    attn_norm,
    mlp_norm,
):
    rank = lax.axis_index("ctx")
    own = lax.axis_index("tp")
    fs = lax.axis_size("fsdp")
    tn = lax.axis_size("tp")
    hid = hidden_in[:, 0]
    _, rows, width = hid.shape
    shard = qkv_weight.shape[1]
    heads_w = qkv_weight.shape[2]
    cond_w = cond_vec.shape[2]
    highest = lax.Precision.HIGHEST

    w_attn_shard = pack_weights(qkv_weight, attn_weight)
    ada_cols = ada_bias.shape[0]
    extra = [cond_vec[:, 0]]
    for x in (down_bias, attn_norm, mlp_norm, up_bias, ada_bias):
        extra.append(jnp.pad(x, (0, -x.shape[0] % cond_w)).reshape(-1, cond_w))
    extra = jnp.concatenate(extra, axis=0)
    ada_rows = jnp.concatenate([ada_weight.T, extra], axis=0)
    ada_rows = jnp.pad(ada_rows, ((0, -ada_rows.shape[0] % 16), (0, 0)))
    w_ff = jnp.concatenate([up_weight, down_weight.T], axis=1)
    w_ff = lax.all_gather(w_ff, ("tp",) + FC, axis=0, tiled=True).reshape(tn, width, -1)
    ada_rows = spread(ada_rows, FC)
    along = lax.all_gather(w_attn_shard, "tp", axis=0, tiled=False)
    in_parts = fs == 4 and tn % 2 == 0 and shard % 16 == 0
    if in_parts:
        lower, upper = along[: tn // 2], along[tn // 2 :]
        x_lower = lax.ppermute(lower, "fsdp", ALONG_X)
        y_upper = lax.ppermute(upper, "fsdp", ALONG_Y)
        x_upper = lax.ppermute(upper, "fsdp", ALONG_X)
        y_lower = lax.ppermute(lower, "fsdp", ALONG_Y)

    ada_full = ada_rows[:, :ada_cols]
    small = ada_rows[:, ada_cols:]
    cond_all = small[:, :2].reshape(fs, 2, 2, cond_w)[:, 0]
    modulation_all = jnp.einsum(
        "smk,fck->smfc", cond_all, ada_full, preferred_element_type=f32
    ).reshape(fs, 2, -1)
    small = small.astype(f32)
    dnb_full = small[:, 2, :shard].reshape(-1)
    norm_one = small[:, 3, :shard].reshape(-1)
    norm_two = small[:, 4, :shard].reshape(-1)
    upb_own = ada_rows[:, ada_cols + 5, :shard].reshape(1, -1)
    upb_full = gather_rows(upb_own)
    adab_full = small[:, 6:].reshape(2 * fs, -1)[:, :ada_cols].reshape(-1)
    modulation_all = modulation_all + adab_full
    modulation = lax.dynamic_index_in_dim(modulation_all, lax.axis_index("fsdp"), 0, keepdims=False)
    shift_one, scale_one, gate_one, shift_two, scale_two, gate_two = jnp.split(modulation, 6, axis=1)
    gain_one = norm_one * (1.0 + scale_one)
    gain_two = norm_two * (1.0 + scale_two)
    zero = jnp.zeros_like(gain_one)
    vec = jnp.stack(
        [
            gate_one,
            gain_two,
            shift_two,
            gate_two,
            jnp.broadcast_to(dnb_full, gain_one.shape),
            gain_one,
            shift_one,
            zero,
        ],
        axis=1,
    )

    hid_other = lax.ppermute(hid, "ctx", SWAP)
    seg = segment_ids[:, 0]
    halves = jnp.where(rank == 0, seg.reshape(2, 2, 1, rows), seg.reshape(2, 2, 1, rows)[:, ::-1])
    starts = jnp.stack([rank * rows, (1 - rank) * rows]).astype(jnp.int32)
    cos, sin, cols_q, cols_k = table_call(starts, halves)
    normed_all = norm_call(hid, hid_other, vec)
    mask = lax.dynamic_slice_in_dim(pad_mask[:, 0], rank * rows, rows, axis=1).astype(f32)
    cot = out_cot[:, 0]

    if in_parts:
        x_lower, y_upper, normed_all, upb_full = lax.optimization_barrier(
            (x_lower, y_upper, normed_all, upb_full)
        )
        d_lower = lax.ppermute(x_lower, "fsdp", ALONG_Y)
        d_upper = lax.ppermute(y_upper, "fsdp", ALONG_X)
        w_attn = [along, x_lower, x_upper, y_lower, y_upper, d_lower, d_upper]
        w_attn = w_attn + [lax.ppermute(part, "ctx", SWAP) for part in w_attn]
    else:
        w_own = spread(along, "fsdp")
        w_own = join_cores(w_own, lax.ppermute(w_own, "ctx", SWAP), rank)
        w_attn = [w_own[:, :, : width // 2], w_own[:, :, width // 2 :]]
    sources = lax.axis_index("fsdp") ^ jnp.arange(4, dtype=jnp.int32)
    flags = jnp.concatenate(
        [own.reshape(1), jnp.zeros((1,), jnp.int32), 2 * sources + rank, 2 * sources + 1 - rank]
    ).astype(jnp.int32)
    q, k, v, w_out = qkv_call(flags, tn, normed_all, w_attn, cos, sin)
    mixed, mixed_lo, score_cols = attn_fwd_call(q, k, v, cols_q, cols_k)

    own_index = own.reshape(1).astype(jnp.int32)
    flat = lambda x: x.reshape(2 * rows, -1)
    block_out, dh_one, mixed_grad, sums_two, ff_low, attn_low = block_call(
        flags,
        flat(mixed),
        w_out,
        flat(hid),
        vec,
        flat(cot),
        mask.reshape(-1, 1),
        w_ff,
        upb_full,
    )
    mixed_grad = mixed_grad.reshape(2, rows, -1)
    ff_low, mixed_grad = lax.optimization_barrier((ff_low, mixed_grad))
    ff_got = exchange_to_shard(ff_low)

    bwd = functools.partial(
        attn_bwd_call,
        q=q,
        k=k,
        v=v,
        o=mixed,
        lo=mixed_lo,
        x=score_cols,
        cols_k=cols_k,
        cos=cos,
        sin=sin,
    )
    rest = lax.rem(own + 1 + jnp.arange(tn - 1, dtype=jnp.int32), tn).astype(jnp.int32)
    dq_own, kv_own, send_own = bwd(own_index, g=mixed_grad)
    got_own = lax.ppermute(send_own, "ctx", SWAP)
    proj_low = proj_grad_call(
        normed_all.reshape(2, 2 * rows, width),
        flat(dq_own),
        kv_own.reshape(2, 2 * rows, PAD),
        send_own.reshape(2, 2 * rows, PAD),
        attn_low,
    )

    gate2_grad = sums_two[:, 0]
    downbias = jnp.sum(sums_two[:, 1] * gate_two, axis=0)
    shift2_grad = sums_two[:, 2]
    scale2_grad = sums_two[:, 3] * norm_two
    mlpnorm = jnp.sum(sums_two[:, 3] * (1.0 + scale_two), axis=0)
    gate1_grad = sums_two[:, 4]
    mod_late = jnp.zeros_like(gate1_grad)
    mod_early = jnp.concatenate(
        [mod_late, mod_late, gate1_grad, shift2_grad, scale2_grad, gate2_grad], axis=1
    )
    group = 2 * fs
    early = jnp.concatenate(
        [
            mod_early[0].reshape(group, -1),
            mod_early[1].reshape(group, -1),
            mlpnorm.reshape(group, -1),
            downbias.reshape(group, -1),
            (sums_two[0, 5] + sums_two[1, 5]).reshape(group, -1),
        ],
        axis=1,
    )
    used = early.shape[1]
    early = jnp.pad(early, ((0, 0), (0, -used % 1024))).reshape(group, -1, 128)

    mixed_grad, proj_low, early, ff_got = lax.optimization_barrier(
        (mixed_grad, proj_low, early, ff_got)
    )
    proj_got = exchange_to_shard(proj_low)
    dq_rest, kv_rest, send_rest = bwd(rest, g=mixed_grad)
    send_rest, proj_got = lax.optimization_barrier((send_rest, proj_got))
    got_rest = lax.ppermute(send_rest, "ctx", SWAP)

    hidden_grad, sums_one = last_call(
        flags,
        dq_own,
        kv_own,
        got_own,
        dq_rest,
        kv_rest,
        got_rest,
        w_attn,
        hid,
        dh_one.reshape(hid.shape),
        vec,
    )
    ff_shard = jnp.sum(ff_got.astype(f32), axis=0)
    attn_shard = jnp.sum(proj_got.astype(f32), axis=0)

    late = sums_one[:, 0:2].reshape(1, -1, 128)
    both = jnp.concatenate([early, jnp.broadcast_to(late, (group,) + late.shape[1:])], axis=1)
    both = lax.all_to_all(both, FC, split_axis=0, concat_axis=0, tiled=True)
    early = both[:, : early.shape[1]]
    late_all = both[:, early.shape[1] :].reshape(fs, 2, 2, 2, width)
    late_all = late_all[:, 0] + late_all[:, 1]
    late_mod = late_all * jnp.stack([jnp.ones_like(norm_one), norm_one])
    late_mod = jnp.pad(late_mod.reshape(fs * 2, 2 * width), ((0, 0), (0, 4 * width)))
    place = lax.axis_index(FC)
    early = early.reshape(fs, 2, -1)
    early = early[:, 0] + early[:, 1]
    mod_parts = early[:, : 2 * ada_cols].reshape(fs * 2, ada_cols) + lax.dynamic_slice_in_dim(
        late_mod, place * ada_cols, ada_cols, axis=1
    )
    grad_ada = lax.dot_general(
        cond_all.reshape(fs * 2, cond_w).astype(f32),
        mod_parts,
        (((0,), (0,)), ((), ())),
        precision=highest,
        preferred_element_type=f32,
    )
    grad_adabias = jnp.sum(mod_parts, axis=0)
    tail = jnp.sum(early[:, 2 * ada_cols : used], axis=0).reshape(3, shard)
    scale_all = modulation_all[:, :, width : 2 * width]
    attnnorm = jnp.sum(late_all[:, :, 1] * (1.0 + scale_all), axis=(0, 1))
    attnnorm = lax.dynamic_slice_in_dim(attnnorm, place * shard, shard, axis=0)
    mod_grad = mod_early + jnp.pad(
        jnp.concatenate([sums_one[:, 0], sums_one[:, 1] * norm_one], axis=1), ((0, 0), (0, 4 * width))
    )
    terms = bf16_terms(mod_grad.reshape(2, group, ada_cols))
    cond_part = jnp.sum(
        jnp.einsum("xmfc,fck->xmk", terms, ada_full, preferred_element_type=f32), axis=0
    )
    cond_grad = cond_part + lax.ppermute(cond_part, "ctx", SWAP)

    grad_qkv = jnp.stack([attn_shard[:, j * PAD : j * PAD + heads_w] for j in range(3)])
    grad_attn = jnp.concatenate(
        [attn_shard[:, j * PAD + heads_w : (j + 1) * PAD] for j in range(3)], axis=1
    ).T
    return (
        block_out.reshape(hidden_in.shape),
        hidden_grad[:, None],
        cond_grad[:, None],
        grad_qkv,
        grad_attn,
        ff_shard[:, : ff_shard.shape[1] // 2],
        tail[2],
        ff_shard[:, ff_shard.shape[1] // 2 :].T,
        tail[1],
        grad_ada,
        grad_adabias,
        attnnorm,
        tail[0],
    )


def solution(mesh):
    tokens = P(None, "fsdp", "ctx", None)
    per_seq = P(None, "fsdp", None)
    weights = (
        P(None, FC, "tp"),
        P("tp", FC),
        P(FC, "tp"),
        P(("tp",) + FC),
        P("tp", FC),
        P(FC),
        P(None, FC),
        P(FC),
        P(FC),
        P(FC),
    )
    return jax.shard_map(
        on_device,
        mesh=mesh,
        in_specs=(tokens, per_seq, per_seq, per_seq, tokens) + weights,
        out_specs=(tokens, tokens, per_seq) + weights,
        check_vma=False,
    )
```

```python
import functools
import math

import jax
import jax.numpy as jnp
from jax import lax
from jax.experimental import pallas as pl
from jax.experimental.pallas import tpu as pltpu
from jax.sharding import PartitionSpec as P

HEAD_DIM = 64
HEADS_PER_BLOCK = 3
PAD = 256
NORM_EPS = 1e-05
GELU_C = math.sqrt(2.0 / math.pi)
bf16 = jnp.bfloat16
f32 = jnp.float32
FC = ("fsdp", "ctx")
SWAP = [(0, 1), (1, 0)]
ALONG_X = [(0, 1), (1, 0), (2, 3), (3, 2)]
ALONG_Y = [(0, 2), (2, 0), (1, 3), (3, 1)]
MIB = 1 << 20
LIMIT = 60


def dot_nn(a, b):
    return lax.dot_general(a, b, (((1,), (0,)), ((), ())), preferred_element_type=f32)


def dot_nt(a, b):
    return lax.dot_general(a, b, (((1,), (1,)), ((), ())), preferred_element_type=f32)


def params(limit, axes=1):
    return pltpu.CompilerParams(
        dimension_semantics=("arbitrary",) * axes, vmem_limit_bytes=limit * MIB
    )


def cost(flops, nbytes, trans=0):
    return pl.CostEstimate(flops=flops, bytes_accessed=nbytes, transcendentals=trans)


def whole(shape, **kw):
    return pl.BlockSpec(shape, lambda *_: (0,) * len(shape), **kw)


def turn(x, first):
    return jnp.where(first, pltpu.roll(x, 96, 1), pltpu.roll(x, 32, 1))


def interleave(rank, own_ref, oth_ref, out_ref, col):
    count, shard = own_ref.shape[0], own_ref.shape[2]
    cols = slice(col, col + out_ref.shape[1])
    for c in range(2):

        @pl.when(rank == c)
        def _():
            for f in range(count):
                at = 2 * f * shard
                mine, theirs = at + c * shard, at + (1 - c) * shard
                out_ref[mine : mine + shard, :] = own_ref[f, 0, :, cols]
                out_ref[theirs : theirs + shard, :] = oth_ref[f, 0, :, cols]


def lay_weight(flag_ref, t, tn, refs, out_ref, held):
    half = tn // 2
    if len(refs) == 2:
        own_ref, oth_ref = refs if held else [ref.at[:, t : t + 1] for ref in refs]
        interleave(flag_ref[1], own_ref, oth_ref, out_ref, 0)
        return
    shard = refs[0].shape[1]

    def copy(src, row):
        out_ref[pl.ds(pl.multiple_of(row * shard, shard), shard), :] = src

    for core in range(2):
        parts = refs[7 * core : 7 * core + 7]
        for k in range(4):
            row = flag_ref[2 + 4 * core + k]
            if k == 0:
                copy(parts[0][0 if held else t], row)
            elif held:
                pl.when(t < half)(lambda: copy(parts[2 * k - 1][0], row))
                pl.when(t >= half)(lambda: copy(parts[2 * k][0], row))
            else:
                copy(parts[2 * k - 1 if t < half else 2 * k][t % half], row)


def weight_specs(weights, tn):
    width = weights[0].shape[-1]
    shard = weights[0].shape[-2]
    if len(weights) == 2:
        fs = weights[0].shape[0]
        return [pl.BlockSpec((fs, 1, shard, width), lambda t, r: (0, t, 0, 0))] * 2
    half = tn // 2
    at = [lambda t, r: (t, 0, 0)]
    at += [lambda t, r: (jnp.minimum(t, half - 1), 0, 0), lambda t, r: (jnp.maximum(t - half, 0), 0, 0)] * 3
    return [pl.BlockSpec((1, shard, width), index) for index in at * 2]


def qkv_kernel(flag_ref, x_ref, cos_ref, sin_ref, *refs):
    q_ref, k_ref, v_ref, wo_ref, w_ref = refs[-5:]
    rows, width = x_ref.shape[1:]
    lane = lax.broadcasted_iota(jnp.int32, (rows, 128), 1)
    first = (lane & (HEAD_DIM - 1)) < HEAD_DIM // 2
    low = lane < HEAD_DIM
    lay_weight(flag_ref, pl.program_id(0), pl.num_programs(0), refs[:-5], w_ref, True)
    for j in range(3):
        hole = (j + 1) * PAD - HEAD_DIM
        wo_ref[0, :, j * HEAD_DIM : (j + 1) * HEAD_DIM] = w_ref[:, hole : hole + HEAD_DIM]
    wo_ref[0, :, PAD - HEAD_DIM :] = jnp.zeros((width, HEAD_DIM), bf16)

    def rotated(y, half, ch):
        z = y[:, 128 * ch : 128 * ch + 128]
        return z * cos_ref[half] + turn(z, first) * sin_ref[half]

    for b in range(4):
        x = x_ref[b]
        y = dot_nn(x, w_ref[:, PAD : 2 * PAD])
        k_ref[b, :, 0:128] = rotated(y, b // 2, 0).astype(bf16)
        k_ref[b, :, 128:PAD] = rotated(y, b // 2, 1).astype(bf16)
        v_ref[b] = dot_nn(x, w_ref[:, 2 * PAD : 3 * PAD]).astype(bf16)
        if b < 2:
            y = dot_nn(x, w_ref[:, 0:PAD])
            scale = HEAD_DIM ** (-0.5)
            q_ref[b, :, 0:128] = rotated(y, 0, 0).astype(bf16) * scale
            q_ref[b, :, 128:PAD] = jnp.where(low, rotated(y, 0, 1), 0.0).astype(bf16) * scale


def qkv_call(flags, tn, x_all, weights, cos, sin):
    blocks, rows, width = x_all.shape
    out = lambda n: pl.BlockSpec((n, rows, PAD), lambda t, r: (0, 0, t))
    one = pl.Buffered(1)
    return pl.pallas_call(
        qkv_kernel,
        grid_spec=pltpu.PrefetchScalarGridSpec(
            num_scalar_prefetch=1,
            grid=(tn,),
            in_specs=[
                whole((blocks, rows, width), pipeline_mode=one),
                whole((2, rows, 128), pipeline_mode=one),
                whole((2, rows, 128), pipeline_mode=one),
                *weight_specs(weights, tn),
            ],
            out_specs=[
                out(2),
                out(blocks),
                out(blocks),
                pl.BlockSpec((1, width, PAD), lambda t, r: (t, 0, 0)),
            ],
            scratch_shapes=[pltpu.VMEM((width, 3 * PAD), bf16)],
        ),
        out_shape=[
            jax.ShapeDtypeStruct((2, rows, tn * PAD), bf16),
            jax.ShapeDtypeStruct((blocks, rows, tn * PAD), bf16),
            jax.ShapeDtypeStruct((blocks, rows, tn * PAD), bf16),
            jax.ShapeDtypeStruct((tn, width, PAD), bf16),
        ],
        compiler_params=params(LIMIT),
        cost_estimate=cost(2 * blocks * rows * width * 640 * tn, 16 * MIB),
        name="qkv_rope",
    )(flags, x_all, cos, sin, *weights)


def pack_kernel(qkv_ref, attn_ref, a_ref):
    heads_w = qkv_ref.shape[2]
    for j in range(3):
        a_ref[:, j * PAD : j * PAD + heads_w] = qkv_ref[j]
        a_ref[:, j * PAD + heads_w : (j + 1) * PAD] = attn_ref[:, j * HEAD_DIM : (j + 1) * HEAD_DIM]


def pack_weights(qkv_weight, attn_weight):
    shard = qkv_weight.shape[1]
    attn_t = attn_weight.T
    if shard % 16:
        pieces = []
        for j in range(3):
            pieces += [qkv_weight[j], attn_t[:, j * HEAD_DIM : (j + 1) * HEAD_DIM]]
        return jnp.concatenate(pieces, axis=1)
    return pl.pallas_call(
        pack_kernel,
        out_shape=jax.ShapeDtypeStruct((shard, 3 * PAD), bf16),
        name="pack_weights",
    )(qkv_weight, attn_t)


QB = 256
NEG = -1e30


def head_lanes(x, h):
    if h == 2:
        return x
    lane = lax.broadcasted_iota(jnp.int32, x.shape, 1)
    keep = (lane < HEAD_DIM) if h == 0 else (lane >= HEAD_DIM)
    return jnp.where(keep, x, jnp.zeros_like(x))


def in_terms(base, lane, at, x):
    hi = x.astype(bf16).astype(f32)
    rest = x - hi
    mid = rest.astype(bf16).astype(f32)
    out = jnp.where(lane == at + 1, mid, jnp.where(lane == at + 2, rest - mid, base))
    return jnp.where(lane == at, hi, out).astype(bf16)


def attn_fwd_kernel(q_ref, k_ref, v_ref, sq_ref, sk_ref, o_ref, lo_ref, x_ref):
    rows = q_ref.shape[1]
    keys = 2 * rows
    cols_k = sk_ref[0]
    ones = jnp.ones((keys, 128), bf16)
    part = lambda ref, c: ref[..., 128 * c : 128 * c + 128].reshape(keys, 128)
    kx = [jnp.concatenate([part(k_ref, c), cols_k], axis=1) for c in range(2)]
    vx = [jnp.concatenate([part(v_ref, c), ones], axis=1) for c in range(2)]
    lane = lax.broadcasted_iota(jnp.int32, (QB, 128), 1)
    low = lane < HEAD_DIM
    for qb in range(rows // QB):
        span = pl.ds(qb * QB, QB)
        cols_q = sq_ref[0, span, :]
        outs = []
        for h in range(HEADS_PER_BLOCK):
            c = h // 2
            qh = head_lanes(q_ref[0, span, 128 * c : 128 * c + 128], h)
            s = dot_nt(jnp.concatenate([qh, cols_q], axis=1), kx[c])
            top = jnp.max(s, axis=1, keepdims=True)
            o = dot_nn(jnp.exp(s - top).astype(bf16), vx[c])
            total = o[:, 128:]
            outs.append(o[:, :128] / total)
            lse = top + jnp.log(total[:, 0:1])
            x_ref[0, 0, h, span, :] = in_terms(cols_q.astype(f32), lane, 128 - 3, -lse)
        for c, o in enumerate((jnp.where(low, outs[0], outs[1]), outs[2])):
            hi = o.astype(bf16)
            o_ref[0, span, 128 * c : 128 * c + 128] = hi
            lo_ref[0, span, 128 * c : 128 * c + 128] = (o - hi.astype(f32)).astype(bf16)


def attn_fwd_call(q, k, v, cols_q, cols_k):
    _, rows, wide = q.shape
    tn = wide // PAD
    k4 = k.reshape(2, 2, rows, wide)
    v4 = v.reshape(2, 2, rows, wide)
    mine = pl.BlockSpec((1, rows, PAD), lambda m, t: (m, 0, t))
    all_keys = pl.BlockSpec((2, 1, rows, PAD), lambda m, t: (0, m, 0, t))
    return pl.pallas_call(
        attn_fwd_kernel,
        grid=(2, tn),
        in_specs=[
            mine,
            all_keys,
            all_keys,
            pl.BlockSpec((1, rows, 128), lambda m, t: (m, 0, 0)),
            pl.BlockSpec((1, 2 * rows, 128), lambda m, t: (m, 0, 0)),
        ],
        out_specs=[
            mine,
            mine,
            pl.BlockSpec((1, 1, HEADS_PER_BLOCK, rows, 128), lambda m, t: (m, t, 0, 0, 0)),
        ],
        out_shape=[
            jax.ShapeDtypeStruct((2, rows, wide), bf16),
            jax.ShapeDtypeStruct((2, rows, wide), bf16),
            jax.ShapeDtypeStruct((2, tn, HEADS_PER_BLOCK, rows, 128), bf16),
        ],
        compiler_params=params(LIMIT, 2),
        cost_estimate=cost(
            2 * tn * 3 * 2 * 2 * rows * 2 * rows * 256, 18 * MIB, 2 * tn * 3 * rows * 2 * rows
        ),
        name="attn_fwd",
    )(q, k4, v4, cols_q, cols_k)


def attn_bwd_kernel(
    tl_ref,
    q_ref,
    k_ref,
    v_ref,
    g_ref,
    o_ref,
    lo_ref,
    x_ref,
    sk_ref,
    cos_ref,
    sin_ref,
    norm_ref,
    wat_ref,
    dq_ref,
    own_ref,
    oth_ref,
    proj_ref,
    acc_ref,
):
    rows = q_ref.shape[1]
    keys = 2 * rows
    cols_k = sk_ref[0]
    lane = lax.broadcasted_iota(jnp.int32, (QB, 128), 1)
    low = lane < HEAD_DIM
    key_lane = lax.broadcasted_iota(jnp.int32, (keys, 128), 1)
    terms = jnp.where(key_lane < 3, 1.0, 0.0).astype(bf16)

    def unrotated(y, lanes, cos, sin):
        return y * cos - turn(y, (lanes & (HEAD_DIM - 1)) < HEAD_DIM // 2) * sin

    for c in range(2):
        ch = slice(128 * c, 128 * c + 128)
        kc = k_ref[..., ch].reshape(keys, 128)
        kt = kc.T
        kx = jnp.concatenate([kc, cols_k], axis=1)
        vx = jnp.concatenate([v_ref[..., ch].reshape(keys, 128), terms], axis=1)
        dk = jnp.zeros((keys, 128), f32)
        dv = jnp.zeros((keys, 128), f32)
        for qb in range(rows // QB):
            span = pl.ds(qb * QB, QB)
            qc = q_ref[0, span, ch]
            gc = g_ref[0, span, ch]
            prod = gc.astype(f32) * (o_ref[0, span, ch].astype(f32) + lo_ref[0, span, ch].astype(f32))
            dqs = []
            for h in (0, 1) if c == 0 else (2,):
                qh = head_lanes(qc, h)
                gh = head_lanes(gc, h)
                inner = jnp.sum(head_lanes(prod, h), axis=1, keepdims=True)
                gx = in_terms(jnp.zeros((QB, 128), f32), lane, 0, -inner)
                p = jnp.exp(dot_nt(kx, jnp.concatenate([qh, x_ref[0, 0, h, span, :]], axis=1)))
                ds = (p * dot_nt(vx, jnp.concatenate([gh, gx], axis=1))).astype(bf16)
                dv += dot_nn(p.astype(bf16), gh)
                dk += dot_nn(ds, qh)
                dqs.append(dot_nn(kt, ds).T * HEAD_DIM ** (-0.5))
            dq = jnp.where(low, dqs[0], dqs[1] if c == 0 else 0.0)
            dq_ref[0, 0, span, ch] = unrotated(dq, lane, cos_ref[span, :], sin_ref[span, :]).astype(bf16)
        dk = unrotated(dk, key_lane, cos_ref[...], sin_ref[...])
        for half, ref in enumerate((own_ref, oth_ref)):
            some = slice(half * rows, (half + 1) * rows)
            ref[0, 0, 0, :, ch] = dk[some].astype(bf16)
            ref[0, 1, 0, :, ch] = dv[some].astype(bf16)

    slot, m = pl.program_id(0), pl.program_id(1)
    for j in range(3):

        @pl.when(slot == 0)
        def _():
            cols = slice(j * PAD, (j + 1) * PAD)
            if j == 0:
                part = dot_tn(norm_ref[0, 0], dq_ref[0, 0])
            else:
                part = dot_tn(norm_ref[0, 0], own_ref[0, j - 1, 0])
                part += dot_tn(norm_ref[1, 0], oth_ref[0, j - 1, 0])

            @pl.when(m == 0)
            def _():
                acc_ref[:, cols] = part

            @pl.when(m == 1)
            def _():
                edge = (j + 1) * PAD - HEAD_DIM
                total = acc_ref[:, cols] + part
                proj_ref[:, j * PAD : edge] = total[:, : PAD - HEAD_DIM].astype(bf16)
                proj_ref[:, edge : edge + HEAD_DIM] = wat_ref[:, j * HEAD_DIM : (j + 1) * HEAD_DIM]


def attn_bwd_call(tlist, g, q, k, v, o, lo, x, cols_k, cos, sin, normed, wat):
    _, rows, wide = q.shape
    width = normed.shape[-1]
    one = pl.Buffered(1)
    nt = tlist.shape[0]
    k4 = k.reshape(2, 2, rows, wide)
    v4 = v.reshape(2, 2, rows, wide)
    mine = pl.BlockSpec((1, rows, PAD), lambda i, m, tl: (m, 0, tl[i]))
    all_keys = pl.BlockSpec((2, 1, rows, PAD), lambda i, m, tl: (0, m, 0, tl[i]))
    kv_out = pl.BlockSpec((1, 2, 1, rows, PAD), lambda i, m, tl: (i, 0, m, 0, 0))
    return pl.pallas_call(
        attn_bwd_kernel,
        grid_spec=pltpu.PrefetchScalarGridSpec(
            num_scalar_prefetch=1,
            grid=(nt, 2),
            in_specs=[
                mine,
                all_keys,
                all_keys,
                mine,
                mine,
                mine,
                pl.BlockSpec(
                    (1, 1, HEADS_PER_BLOCK, rows, 128), lambda i, m, tl: (m, tl[i], 0, 0, 0)
                ),
                pl.BlockSpec((1, 2 * rows, 128), lambda i, m, tl: (m, 0, 0)),
                whole((2 * rows, 128), pipeline_mode=one),
                whole((2 * rows, 128), pipeline_mode=one),
                pl.BlockSpec(
                    (2, 1, rows, width), lambda i, m, tl: (0, jnp.where(i == 0, m, 1), 0, 0)
                ),
                whole((width, PAD), pipeline_mode=one),
            ],
            out_specs=[
                pl.BlockSpec((1, 1, rows, PAD), lambda i, m, tl: (i, m, 0, 0)),
                kv_out,
                kv_out,
                whole((width, 3 * PAD), pipeline_mode=one),
            ],
            scratch_shapes=[pltpu.VMEM((width, 3 * PAD), f32)],
        ),
        out_shape=[
            jax.ShapeDtypeStruct((nt, 2, rows, PAD), bf16),
            jax.ShapeDtypeStruct((nt, 2, 2, rows, PAD), bf16),
            jax.ShapeDtypeStruct((nt, 2, 2, rows, PAD), bf16),
            jax.ShapeDtypeStruct((width, 3 * PAD), bf16),
        ],
        compiler_params=params(LIMIT, 2),
        cost_estimate=cost(
            2 * nt * 3 * 5 * 2 * rows * 2 * rows * 256, 5 * nt * MIB, 2 * nt * 3 * rows * 2 * rows
        ),
        name="attn_bwd",
    )(
        tlist,
        q,
        k4,
        v4,
        g,
        o,
        lo,
        x,
        cols_k,
        cos.reshape(2 * rows, 128),
        sin.reshape(2 * rows, 128),
        normed.reshape(2, 2, rows, width),
        wat,
    )


RB = 512
UNROLL = 1


def dot_tn(a, b):
    return lax.dot_general(a, b, (((0,), (0,)), ((), ())), preferred_element_type=f32)


def normalise(h):
    mean = jnp.mean(h, axis=-1, keepdims=True)
    cent = h - mean
    var = jnp.mean(cent * cent, axis=-1, keepdims=True)
    rstd = lax.rsqrt(var + NORM_EPS)
    return cent * rstd, rstd


def block_kernel(
    flag_ref,
    mix_ref,
    wout_ref,
    hid_ref,
    vec_ref,
    cot_ref,
    mask_ref,
    ub_ref,
    ff_ref,
    out_ref,
    dh_ref,
    mg_ref,
    sum_ref,
    wff_ref,
    wat_ref,
    up_ref,
    dn_ref,
    x_ref,
    g_ref,
    bl_ref,
    mine_ref,
    act_ref,
    ul_ref,
    acts_ref,
    uls_ref,
    h1_ref,
    br_ref,
    d_ref,
    n_ref,
    sem,
):
    step = pl.program_id(0)
    steps = pl.num_programs(0)
    own = flag_ref[0]
    width = hid_ref.shape[1]
    tn = ff_ref.shape[0]
    ff = ub_ref.shape[2]
    here = pl.ds(pl.multiple_of(step * RB, RB), RB)

    def fetch(j):
        cols = pl.ds(pl.multiple_of(j * ff, ff), ff)
        return (
            pltpu.make_async_copy(ff_ref.at[j, :, 0:ff], up_ref.at[:, cols], sem.at[2 * j]),
            pltpu.make_async_copy(ff_ref.at[j, :, ff : 2 * ff], dn_ref.at[:, cols], sem.at[2 * j + 1]),
        )

    @pl.when(step == 0)
    def _():
        for j in range(tn):
            for copy in fetch(j):
                copy.start()

    gate1, gain2, shift2 = vec_ref[0, 0:1, :], vec_ref[0, 1:2, :], vec_ref[0, 2:3, :]
    gate2, dbias = vec_ref[0, 3:4, :], vec_ref[0, 4:5, :]
    acc = dot_nt(mix_ref[:, 0:PAD], wout_ref[0])
    for t in range(1, tn):
        acc += dot_nt(mix_ref[:, t * PAD : (t + 1) * PAD], wout_ref[t])
    br_ref[...] = acc
    h1 = hid_ref[...].astype(f32) + gate1 * acc
    h1_ref[...] = h1
    n, _ = normalise(h1)
    x = (n * gain2 + shift2).astype(bf16)
    x_ref[here, :] = x
    cot = cot_ref[...].astype(f32) * mask_ref[...]
    g = (cot * gate2).astype(bf16)
    g_ref[here, :] = g
    mine_ref[here, :] = mix_ref[:, pl.ds(pl.multiple_of(own * PAD, PAD), PAD)]

    def units(j, carry):
        @pl.when(step == 0)
        def _():
            for copy in fetch(j):
                copy.wait()

        cols = pl.ds(pl.multiple_of(j * ff, ff), ff)
        u = dot_nn(x_ref[here, :], up_ref[:, cols]) + ub_ref[lax.rem(own - j + tn, tn)]
        da = dot_nn(g_ref[here, :], dn_ref[:, cols])
        u2 = u * u
        th = jnp.tanh(GELU_C * u * (1.0 + 0.044715 * u2))
        half_up = 0.5 * (1.0 + th)
        slope = half_up + (0.5 * GELU_C) * u * (1.0 - th * th) * (1.0 + (3 * 0.044715) * u2)
        acts_ref[:, cols] = (u * half_up).astype(bf16)
        uls_ref[:, cols] = (da * slope).astype(bf16)
        return carry

    lax.fori_loop(0, tn, units, 0)
    mine = pl.ds(pl.multiple_of(own * ff, ff), ff)
    act_ref[here, :] = acts_ref[:, mine]
    ul_ref[here, :] = uls_ref[:, mine]
    for c in range(0, width, PAD):
        cols = slice(c, c + PAD)
        d_ref[:, cols] = dot_nt(acts_ref[...], dn_ref[cols, :])
        n_ref[:, cols] = dot_nt(uls_ref[...], up_ref[cols, :])

    down = d_ref[...] + dbias
    h1 = h1_ref[...]
    out_ref[...] = (h1 + gate2 * down).astype(bf16)
    n, rstd = normalise(h1)
    grad = n_ref[...]
    gn = grad * n
    e = grad * gain2
    en = gn * gain2
    dh = cot + rstd * (
        e - jnp.mean(e, axis=-1, keepdims=True) - n * jnp.mean(en, axis=-1, keepdims=True)
    )
    dh_ref[...] = dh
    bl = (dh * gate1).astype(bf16)
    bl_ref[here, :] = bl
    for t in range(tn):
        mg_ref[:, t * PAD : (t + 1) * PAD] = dot_nn(bl, wout_ref[t]).astype(bf16)

    @pl.when(lax.rem(step, steps // 2) == 0)
    def _():
        sum_ref[...] = jnp.zeros_like(sum_ref)

    parts = (cot * down, cot, grad, gn, dh * br_ref[...], uls_ref[:, mine].astype(f32))
    for r, part in enumerate(parts):
        sum_ref[0, r : r + 1, :] += jnp.sum(part, axis=0, keepdims=True)

    @pl.when(step == steps - 1)
    def _():
        def column(c, carry):
            cols = pl.ds(pl.multiple_of(c * PAD, PAD), PAD)
            wff_ref[:, cols] = dot_tn(x_ref[...], ul_ref[:, cols]).astype(bf16)
            far = pl.ds(pl.multiple_of(ff + c * PAD, PAD), PAD)
            wff_ref[:, far] = dot_tn(g_ref[...], act_ref[:, cols]).astype(bf16)
            return carry

        lax.fori_loop(0, ff // PAD, column, 0)
        wat_ref[...] = dot_tn(bl_ref[...], mine_ref[...]).astype(bf16)


def block_call(flags, mixed, w_out, hid, vec, cot, mask_col, w_ff, up_bias):
    rows, wide = mixed.shape
    width = hid.shape[1]
    tn, _, ff = w_ff.shape
    ff = ff // 2
    one = pl.Buffered(1)
    steps = rows // RB
    row = lambda w: pl.BlockSpec((RB, w), lambda i, o: (i, 0))
    vecs = pl.BlockSpec((1, 8, width), lambda i, o: (i // (steps // 2), 0, 0))
    tokens = lambda dtype, w, n=rows: pltpu.VMEM((n, w), dtype)
    return pl.pallas_call(
        block_kernel,
        grid_spec=pltpu.PrefetchScalarGridSpec(
            num_scalar_prefetch=1,
            grid=(steps,),
            in_specs=[
                row(wide),
                whole((tn, width, PAD), pipeline_mode=one),
                row(width),
                vecs,
                row(width),
                row(1),
                whole((tn, 1, ff), pipeline_mode=one),
                pl.BlockSpec(memory_space=pl.ANY),
            ],
            out_specs=[
                row(width),
                row(width),
                row(wide),
                vecs,
                whole((width, 2 * ff), pipeline_mode=one),
                whole((width, PAD), pipeline_mode=one),
            ],
            scratch_shapes=[
                tokens(bf16, tn * ff, width),
                tokens(bf16, tn * ff, width),
                tokens(bf16, width),
                tokens(bf16, width),
                tokens(bf16, width),
                tokens(bf16, PAD),
                tokens(bf16, ff),
                tokens(bf16, ff),
                tokens(bf16, tn * ff, RB),
                tokens(bf16, tn * ff, RB),
                tokens(f32, width, RB),
                tokens(f32, width, RB),
                tokens(f32, width, RB),
                tokens(f32, width, RB),
                pltpu.SemaphoreType.DMA((2 * tn,)),
            ],
        ),
        out_shape=[
            jax.ShapeDtypeStruct((rows, width), bf16),
            jax.ShapeDtypeStruct((rows, width), f32),
            jax.ShapeDtypeStruct((rows, wide), bf16),
            jax.ShapeDtypeStruct((2, 8, width), f32),
            jax.ShapeDtypeStruct((width, 2 * ff), bf16),
            jax.ShapeDtypeStruct((width, PAD), bf16),
        ],
        compiler_params=params(LIMIT),
        cost_estimate=cost(
            4 * 2 * rows * width * ff * tn + 8 * rows * width * width, 32 * MIB, rows * ff * tn
        ),
        name="block_both",
    )(flags, mixed, w_out, hid, vec, cot, mask_col, up_bias, w_ff)


def norm_kernel(hid_ref, oth_ref, vec_ref, out_ref):
    gain, shift = vec_ref[0, 5:6, :], vec_ref[0, 6:7, :]
    for half, ref in enumerate((hid_ref, oth_ref)):
        n, _ = normalise(ref[0].astype(f32))
        out_ref[half, 0] = (n * gain + shift).astype(bf16)


def norm_call(hid, other, vec):
    _, rows, width = hid.shape
    row = pl.BlockSpec((1, RB // 2, width), lambda m, i: (m, i, 0))
    out = pl.pallas_call(
        norm_kernel,
        grid=(2, 2 * rows // RB),
        in_specs=[row, row, pl.BlockSpec((1, 8, width), lambda m, i: (m, 0, 0))],
        out_specs=pl.BlockSpec((2, 1, RB // 2, width), lambda m, i: (0, m, i, 0)),
        out_shape=jax.ShapeDtypeStruct((2, 2, rows, width), bf16),
        compiler_params=params(LIMIT, 2),
        cost_estimate=cost(20 * rows * width, 7 * MIB),
        name="first_norm",
    )(hid, other, vec)
    return out.reshape(4, rows, width)


def table_kernel(flag_ref, seg_ref, cos_ref, sin_ref, sq_ref, sk_ref):
    rows = seg_ref.shape[3]
    lane = lax.broadcasted_iota(jnp.int32, (rows, 128), 1)
    fixed = lane >= 128 - 3
    pair = (lane & (HEAD_DIM // 2 - 1)).astype(f32)
    freq = jnp.exp(pair * (-2.0 * math.log(10000.0) / HEAD_DIM))
    sign = jnp.where((lane & (HEAD_DIM - 1)) < HEAD_DIM // 2, -1.0, 1.0)
    row = lax.broadcasted_iota(jnp.int32, (rows, 128), 0)
    for half in range(2):
        angle = (row + flag_ref[half]).astype(f32) * freq
        cos_ref[half] = jnp.cos(angle)
        sin_ref[half] = jnp.sin(angle) * sign
        for m in range(2):
            ids = jnp.broadcast_to(seg_ref[m, half].astype(f32), (128, rows)).T
            same = (ids == lane.astype(f32)) | fixed
            sk_ref[m, half] = jnp.where(same, 1.0, 0.0).astype(bf16)
            if half == 0:
                sq_ref[m] = jnp.where(same, 0.0, NEG).astype(bf16)


def table_call(starts, segments):
    _, _, _, rows = segments.shape
    cos, sin, cols_q, cols_k = pl.pallas_call(
        table_kernel,
        grid_spec=pltpu.PrefetchScalarGridSpec(
            num_scalar_prefetch=1,
            grid=(1,),
            in_specs=[whole(segments.shape)],
            out_specs=[
                whole((2, rows, 128)),
                whole((2, rows, 128)),
                whole((2, rows, 128)),
                whole((2, 2, rows, 128)),
            ],
        ),
        out_shape=[
            jax.ShapeDtypeStruct((2, rows, 128), f32),
            jax.ShapeDtypeStruct((2, rows, 128), f32),
            jax.ShapeDtypeStruct((2, rows, 128), bf16),
            jax.ShapeDtypeStruct((2, 2, rows, 128), bf16),
        ],
        compiler_params=params(LIMIT),
        cost_estimate=cost(100 * 2 * rows * 128, 3 * MIB),
        name="tables",
    )(starts, segments)
    return cos, sin, cols_q, cols_k.reshape(2, 2 * rows, 128)


def last_kernel(
    flag_ref,
    dq_ref,
    kv_ref,
    rv_ref,
    hid_ref,
    dh_ref,
    vec_ref,
    early_ref,
    *refs,
):
    out_ref, sum_ref, w_ref = refs[-3:]
    first = pl.program_id(1) == 0
    own = flag_ref[0]
    tn = w_ref.shape[0]

    @pl.when(first & (pl.program_id(0) == 0))
    def _():
        for t in range(tn):
            lay_weight(flag_ref, t, tn, refs[:-3], w_ref.at[t], False)

    acc = jnp.zeros(dh_ref.shape[1:], f32)
    for t in range(tn):
        slot = lax.rem(t - own + tn, tn)
        acc += dot_nt(dq_ref[slot, 0], w_ref[t, :, 0:PAD])
        for j in range(2):
            d = kv_ref[slot, j, 0].astype(f32) + rv_ref[slot, j, 0].astype(f32)
            acc += dot_nt(d.astype(bf16), w_ref[t, :, (j + 1) * PAD : (j + 2) * PAD])
    gain1 = vec_ref[0, 5:6, :]
    n, rstd = normalise(hid_ref[0].astype(f32))
    gn = acc * n
    e = acc * gain1
    en = gn * gain1
    out_ref[0] = dh_ref[0] + rstd * (
        e - jnp.mean(e, axis=-1, keepdims=True) - n * jnp.mean(en, axis=-1, keepdims=True)
    )

    @pl.when(first)
    def _():
        sum_ref[0, 0:2, :] = jnp.zeros((2, sum_ref.shape[2]), f32)
        sum_ref[0, 2:8, :] = early_ref[0, 0:6, :]

    sum_ref[0, 0:1, :] += jnp.sum(acc, axis=0, keepdims=True)
    sum_ref[0, 1:2, :] += jnp.sum(gn, axis=0, keepdims=True)


def last_call(flags, dq, kv, rv, weights, hid, dh, vec, early):
    _, rows, width = hid.shape
    tn = dq.shape[0]
    row = pl.BlockSpec((1, RB, width), lambda m, i, o: (m, i, 0))
    vecs = pl.BlockSpec((1, 8, width), lambda m, i, o: (m, 0, 0))
    q_spec = lambda n: pl.BlockSpec((n, 1, RB, PAD), lambda m, i, o: (0, m, i, 0))
    kv_spec = lambda n: pl.BlockSpec((n, 2, 1, RB, PAD), lambda m, i, o: (0, 0, m, i, 0))
    return pl.pallas_call(
        last_kernel,
        grid_spec=pltpu.PrefetchScalarGridSpec(
            num_scalar_prefetch=1,
            grid=(2, rows // RB),
            in_specs=[
                q_spec(tn),
                kv_spec(tn),
                kv_spec(tn),
                row,
                row,
                vecs,
                vecs,
                *[whole(w.shape, pipeline_mode=pl.Buffered(1)) for w in weights],
            ],
            out_specs=[row, vecs],
            scratch_shapes=[pltpu.VMEM((tn, width, 3 * PAD), bf16)],
        ),
        out_shape=[
            jax.ShapeDtypeStruct((2, rows, width), f32),
            jax.ShapeDtypeStruct((2, 8, width), f32),
        ],
        compiler_params=params(LIMIT, 2),
        cost_estimate=cost(2 * 2 * rows * width * tn * 3 * PAD, 24 * MIB),
        name="first_norm_bwd",
    )(flags, dq, kv, rv, hid, dh, vec, early, *weights)


def split_terms(x):
    hi = x.astype(bf16)
    rest = x - hi.astype(f32)
    mid = rest.astype(bf16)
    return [hi, mid, (rest - mid.astype(f32)).astype(bf16)]


def finish_kernel(flag_ref, sums_ref, mod_ref, norm_ref, cond_ref, ada_ref, *refs):
    gada_ref, gadab_ref, gcond_ref, gn1_ref, gn2_ref, gdb_ref, gub_ref, all_ref = refs
    group, ada_cols, _ = ada_ref.shape
    width = sums_ref.shape[3]
    place = flag_ref[0]
    norm_one, norm_two = norm_ref[0:1, :], norm_ref[1:2, :]
    one = jnp.zeros((1, width), f32)
    small = [one, one, one, one]
    for f in range(group // 2):
        for m in range(2):
            s = 2 * f + m
            r = sums_ref[2 * f, m] + sums_ref[2 * f + 1, m]
            r = [r[i : i + 1, :] for i in range(8)]
            parts = (r[0], r[1] * norm_one, r[6], r[4], r[5] * norm_two, r[2])
            for i, part in enumerate(parts):
                all_ref[s : s + 1, i * width : (i + 1) * width] = part
            scale_one, scale_two, gate_two = (
                mod_ref[s : s + 1, i * width : (i + 1) * width] for i in (1, 4, 5)
            )
            terms = (r[1] * (1.0 + scale_one), r[5] * (1.0 + scale_two), r[3] * gate_two, r[7])
            small = [total + term for total, term in zip(small, terms)]

    def own_columns(x, count):
        total = x.shape[1]
        return pltpu.roll(x, lax.rem(total - place * count, total), 1)[:, :count]

    for ref, total in zip((gn1_ref, gn2_ref, gdb_ref, gub_ref), small):
        shard = ref.shape[1]
        ref[...] = own_columns(jnp.broadcast_to(total, (8, width)), shard)[0:1, :]
    mine = own_columns(all_ref[...], ada_cols)
    gadab_ref[...] = jnp.sum(mine, axis=0, keepdims=True)
    cond = cond_ref[...]
    terms = split_terms(mine)
    gada_ref[...] = dot_tn(terms[0], cond) + dot_tn(terms[1], cond) + dot_tn(terms[2], cond)
    total = jnp.zeros((8, cond.shape[1]), f32)
    seqs = all_ref[pl.ds(pl.multiple_of(flag_ref[1] * 8, 8), 8), :]
    for term in split_terms(seqs):
        for c in range(group):
            total += dot_nn(term[:, c * ada_cols : (c + 1) * ada_cols], ada_ref[c])
    gcond_ref[...] = total


def finish_call(flags, sums, mod_all, norms, cond, ada):
    group, ada_cols, cond_w = ada.shape
    shard = sums.shape[3] // group
    out = [(ada_cols, cond_w), (1, ada_cols), (8, cond_w)] + [(1, shard)] * 4
    return pl.pallas_call(
        finish_kernel,
        grid_spec=pltpu.PrefetchScalarGridSpec(
            num_scalar_prefetch=1,
            grid=(1,),
            in_specs=[whole(x.shape) for x in (sums, mod_all, norms, cond, ada)],
            out_specs=[whole(x) for x in out],
            scratch_shapes=[pltpu.VMEM(mod_all.shape, f32)],
        ),
        out_shape=[jax.ShapeDtypeStruct(x, f32) for x in out],
        compiler_params=params(LIMIT),
        cost_estimate=cost(1 << 20, 3 * MIB),
        name="finish",
    )(flags, sums, mod_all, norms, cond, ada)


def spread(x, axes):
    count = lax.axis_size(axes)
    many = jnp.broadcast_to(x[None], (count,) + x.shape)
    return lax.all_to_all(many, axes, split_axis=0, concat_axis=0, tiled=True)


def join_cores(part, other, rank):
    fs, tn, rows, width = part.shape
    both = jnp.stack([jnp.where(rank == 0, part, other), jnp.where(rank == 0, other, part)], axis=1)
    return both.transpose(2, 0, 1, 3, 4).reshape(1, tn, fs * 2 * rows, width)


def gather_rows(row):
    tn = lax.axis_size("tp")
    got = [row]
    for step in range(1, tn):
        got.append(lax.ppermute(row, "tp", [(i, (i + step) % tn) for i in range(tn)]))
    return jnp.stack(got).astype(f32)


def exchange_to_shard(grad):
    group = lax.axis_size(FC)
    parts = grad.reshape(group, -1, grad.shape[1])
    return lax.all_to_all(parts, FC, split_axis=0, concat_axis=0, tiled=True)


def on_device(
    hidden_in,
    cond_vec,
    segment_ids,
    pad_mask,
    out_cot,
    qkv_weight,
    attn_weight,
    up_weight,
    up_bias,
    down_weight,
    down_bias,
    ada_weight,
    ada_bias,
    attn_norm,
    mlp_norm,
):
    rank = lax.axis_index("ctx")
    own = lax.axis_index("tp")
    fs = lax.axis_size("fsdp")
    tn = lax.axis_size("tp")
    hid = hidden_in[:, 0]
    _, rows, width = hid.shape
    shard = qkv_weight.shape[1]
    heads_w = qkv_weight.shape[2]
    cond_w = cond_vec.shape[2]
    highest = lax.Precision.HIGHEST

    w_attn_shard = pack_weights(qkv_weight, attn_weight)
    ada_cols = ada_bias.shape[0]
    extra = [cond_vec[:, 0]]
    for x in (down_bias, attn_norm, mlp_norm, up_bias, ada_bias):
        extra.append(jnp.pad(x, (0, -x.shape[0] % cond_w)).reshape(-1, cond_w))
    extra = jnp.concatenate(extra, axis=0)
    ada_rows = jnp.concatenate([ada_weight.T, extra], axis=0)
    ada_rows = jnp.pad(ada_rows, ((0, -ada_rows.shape[0] % 16), (0, 0)))
    w_ff = jnp.concatenate([up_weight, down_weight.T], axis=1)
    w_ff = lax.all_gather(w_ff, ("tp",) + FC, axis=0, tiled=True).reshape(tn, width, -1)
    ada_rows = spread(ada_rows, FC)
    along = lax.all_gather(w_attn_shard, "tp", axis=0, tiled=False)
    in_parts = fs == 4 and tn % 2 == 0 and shard % 16 == 0
    if in_parts:
        lower, upper = along[: tn // 2], along[tn // 2 :]
        x_lower = lax.ppermute(lower, "fsdp", ALONG_X)
        y_upper = lax.ppermute(upper, "fsdp", ALONG_Y)
        x_upper = lax.ppermute(upper, "fsdp", ALONG_X)
        y_lower = lax.ppermute(lower, "fsdp", ALONG_Y)

    ada_full = ada_rows[:, :ada_cols]
    small = ada_rows[:, ada_cols:]
    cond_all = small[:, :2].reshape(fs, 2, 2, cond_w)[:, 0]
    modulation_all = jnp.einsum(
        "smk,fck->smfc", cond_all, ada_full, preferred_element_type=f32
    ).reshape(fs, 2, -1)
    small = small.astype(f32)
    dnb_full = small[:, 2, :shard].reshape(-1)
    norm_one = small[:, 3, :shard].reshape(-1)
    norm_two = small[:, 4, :shard].reshape(-1)
    upb_own = ada_rows[:, ada_cols + 5, :shard].reshape(1, -1)
    upb_full = gather_rows(upb_own)
    adab_full = small[:, 6:].reshape(2 * fs, -1)[:, :ada_cols].reshape(-1)
    modulation_all = modulation_all + adab_full
    modulation = lax.dynamic_index_in_dim(modulation_all, lax.axis_index("fsdp"), 0, keepdims=False)
    shift_one, scale_one, gate_one, shift_two, scale_two, gate_two = jnp.split(modulation, 6, axis=1)
    gain_one = norm_one * (1.0 + scale_one)
    gain_two = norm_two * (1.0 + scale_two)
    zero = jnp.zeros_like(gain_one)
    vec = jnp.stack(
        [
            gate_one,
            gain_two,
            shift_two,
            gate_two,
            jnp.broadcast_to(dnb_full, gain_one.shape),
            gain_one,
            shift_one,
            zero,
        ],
        axis=1,
    )

    hid_other = lax.ppermute(hid, "ctx", SWAP)
    seg = segment_ids[:, 0]
    halves = jnp.where(rank == 0, seg.reshape(2, 2, 1, rows), seg.reshape(2, 2, 1, rows)[:, ::-1])
    starts = jnp.stack([rank * rows, (1 - rank) * rows]).astype(jnp.int32)
    cos, sin, cols_q, cols_k = table_call(starts, halves)
    normed_all = norm_call(hid, hid_other, vec)
    mask = lax.dynamic_slice_in_dim(pad_mask[:, 0], rank * rows, rows, axis=1).astype(f32)
    cot = out_cot[:, 0]

    if in_parts:
        x_lower, y_upper, normed_all, upb_full = lax.optimization_barrier(
            (x_lower, y_upper, normed_all, upb_full)
        )
        d_lower = lax.ppermute(x_lower, "fsdp", ALONG_Y)
        d_upper = lax.ppermute(y_upper, "fsdp", ALONG_X)
        w_attn = [along, x_lower, x_upper, y_lower, y_upper, d_lower, d_upper]
        w_attn = w_attn + [lax.ppermute(part, "ctx", SWAP) for part in w_attn]
    else:
        w_own = spread(along, "fsdp")
        w_own = join_cores(w_own, lax.ppermute(w_own, "ctx", SWAP), rank)
        w_attn = [w_own[:, :, : width // 2], w_own[:, :, width // 2 :]]
    sources = lax.axis_index("fsdp") ^ jnp.arange(4, dtype=jnp.int32)
    flags = jnp.concatenate(
        [own.reshape(1), jnp.zeros((1,), jnp.int32), 2 * sources + rank, 2 * sources + 1 - rank]
    ).astype(jnp.int32)
    q, k, v, w_out = qkv_call(flags, tn, normed_all, w_attn, cos, sin)
    mixed, mixed_lo, score_cols = attn_fwd_call(q, k, v, cols_q, cols_k)

    own_index = own.reshape(1).astype(jnp.int32)
    flat = lambda x: x.reshape(2 * rows, -1)
    block_out, dh_one, mixed_grad, sums_two, ff_low, attn_low = block_call(
        flags,
        flat(mixed),
        w_out,
        flat(hid),
        vec,
        flat(cot),
        mask.reshape(-1, 1),
        w_ff,
        upb_full,
    )
    mixed_grad = mixed_grad.reshape(2, rows, -1)
    ff_low, mixed_grad = lax.optimization_barrier((ff_low, mixed_grad))
    ff_got = exchange_to_shard(ff_low)

    order = lax.rem(own + jnp.arange(tn, dtype=jnp.int32), tn).astype(jnp.int32)
    dq, kv_own, kv_send, proj_low = attn_bwd_call(
        order, mixed_grad, q, k, v, mixed, mixed_lo, score_cols, cols_k, cos, sin, normed_all, attn_low
    )

    kv_send, proj_low, ff_got = lax.optimization_barrier((kv_send, proj_low, ff_got))
    kv_got = lax.ppermute(kv_send, "ctx", SWAP)
    proj_got = exchange_to_shard(proj_low)

    hidden_grad, sums_one = last_call(
        flags, dq, kv_own, kv_got, w_attn, hid, dh_one.reshape(hid.shape), vec, sums_two
    )

    all_sums = lax.all_gather(sums_one, FC, axis=0, tiled=False)
    all_sums, proj_got, ff_got = lax.optimization_barrier((all_sums, proj_got, ff_got))
    seq = lax.axis_index("fsdp")
    finish_flags = jnp.stack([lax.axis_index(FC), seq // 4]).astype(jnp.int32)
    grads = finish_call(
        finish_flags,
        all_sums,
        modulation_all.reshape(2 * fs, -1),
        jnp.stack([norm_one, norm_two]),
        cond_all.reshape(2 * fs, cond_w),
        ada_full,
    )
    grad_ada, grad_adabias, cond_grad, attnnorm, mlpnorm, downbias, upbias = grads
    cond_grad = lax.dynamic_slice_in_dim(cond_grad, 2 * (seq % 4), 2, axis=0)
    ff_shard = jnp.sum(ff_got.astype(f32), axis=0)
    attn_shard = jnp.sum(proj_got.astype(f32), axis=0)

    grad_qkv = jnp.stack([attn_shard[:, j * PAD : j * PAD + heads_w] for j in range(3)])
    grad_attn = jnp.concatenate(
        [attn_shard[:, j * PAD + heads_w : (j + 1) * PAD] for j in range(3)], axis=1
    ).T
    return (
        block_out.reshape(hidden_in.shape),
        hidden_grad[:, None],
        cond_grad[:, None],
        grad_qkv,
        grad_attn,
        ff_shard[:, : ff_shard.shape[1] // 2],
        upbias.reshape(-1),
        ff_shard[:, ff_shard.shape[1] // 2 :].T,
        downbias.reshape(-1),
        grad_ada.T,
        grad_adabias.reshape(-1),
        attnnorm.reshape(-1),
        mlpnorm.reshape(-1),
    )


def solution(mesh):
    tokens = P(None, "fsdp", "ctx", None)
    per_seq = P(None, "fsdp", None)
    weights = (
        P(None, FC, "tp"),
        P("tp", FC),
        P(FC, "tp"),
        P(("tp",) + FC),
        P("tp", FC),
        P(FC),
        P(None, FC),
        P(FC),
        P(FC),
        P(FC),
    )
    return jax.shard_map(
        on_device,
        mesh=mesh,
        in_specs=(tokens, per_seq, per_seq, per_seq, tokens) + weights,
        out_specs=(tokens, tokens, per_seq) + weights,
        check_vma=False,
    )
```

```python
import functools
import math

import jax
import jax.numpy as jnp
from jax import lax
from jax.experimental import pallas as pl
from jax.experimental.pallas import tpu as pltpu
from jax.sharding import PartitionSpec as P

HEAD_DIM = 64
HEADS_PER_BLOCK = 3
PAD = 256
NORM_EPS = 1e-05
GELU_C = math.sqrt(2.0 / math.pi)
bf16 = jnp.bfloat16
f32 = jnp.float32
FC = ("fsdp", "ctx")
SWAP = [(0, 1), (1, 0)]
ALONG_X = [(0, 1), (1, 0), (2, 3), (3, 2)]
ALONG_Y = [(0, 2), (2, 0), (1, 3), (3, 1)]
MIB = 1 << 20
LIMIT = 60


def dot_nn(a, b):
    return lax.dot_general(a, b, (((1,), (0,)), ((), ())), preferred_element_type=f32)


def dot_nt(a, b):
    return lax.dot_general(a, b, (((1,), (1,)), ((), ())), preferred_element_type=f32)


def params(limit, axes=1):
    return pltpu.CompilerParams(
        dimension_semantics=("arbitrary",) * axes, vmem_limit_bytes=limit * MIB
    )


def cost(flops, nbytes, trans=0):
    return pl.CostEstimate(flops=flops, bytes_accessed=nbytes, transcendentals=trans)


def whole(shape, **kw):
    return pl.BlockSpec(shape, lambda *_: (0,) * len(shape), **kw)


def turn(x, first):
    return jnp.where(first, pltpu.roll(x, 96, 1), pltpu.roll(x, 32, 1))


def interleave(rank, own_ref, oth_ref, out_ref, col):
    count, shard = own_ref.shape[0], own_ref.shape[2]
    cols = slice(col, col + out_ref.shape[1])
    for c in range(2):

        @pl.when(rank == c)
        def _():
            for f in range(count):
                at = 2 * f * shard
                mine, theirs = at + c * shard, at + (1 - c) * shard
                out_ref[mine : mine + shard, :] = own_ref[f, 0, :, cols]
                out_ref[theirs : theirs + shard, :] = oth_ref[f, 0, :, cols]


def lay_weight(flag_ref, t, tn, refs, out_ref, held):
    half = tn // 2
    if len(refs) == 2:
        own_ref, oth_ref = refs if held else [ref.at[:, t : t + 1] for ref in refs]
        interleave(flag_ref[1], own_ref, oth_ref, out_ref, 0)
        return
    shard = refs[0].shape[1]

    def copy(src, row):
        out_ref[pl.ds(pl.multiple_of(row * shard, shard), shard), :] = src

    for core in range(2):
        parts = refs[7 * core : 7 * core + 7]
        for k in range(4):
            row = flag_ref[2 + 4 * core + k]
            if k == 0:
                copy(parts[0][0 if held else t], row)
            elif held:
                pl.when(t < half)(lambda: copy(parts[2 * k - 1][0], row))
                pl.when(t >= half)(lambda: copy(parts[2 * k][0], row))
            else:
                copy(parts[2 * k - 1 if t < half else 2 * k][t % half], row)


def weight_specs(weights, tn):
    width = weights[0].shape[-1]
    shard = weights[0].shape[-2]
    if len(weights) == 2:
        fs = weights[0].shape[0]
        return [pl.BlockSpec((fs, 1, shard, width), lambda t, r: (0, t, 0, 0))] * 2
    half = tn // 2
    at = [lambda t, r: (t, 0, 0)]
    at += [lambda t, r: (jnp.minimum(t, half - 1), 0, 0), lambda t, r: (jnp.maximum(t - half, 0), 0, 0)] * 3
    return [pl.BlockSpec((1, shard, width), index) for index in at * 2]


def qkv_kernel(flag_ref, hid_ref, other_ref, vec_ref, cos_ref, sin_ref, *refs):
    q_ref, k_ref, v_ref, wo_ref, x_ref, w_ref = refs[-6:]
    rows, width = x_ref.shape[1:]

    @pl.when(pl.program_id(0) == 0)
    def _():
        for half, ref in enumerate((hid_ref, other_ref)):
            for m in range(2):
                n, _ = normalise(ref[m].astype(f32))
                x_ref[2 * half + m] = (n * vec_ref[m, 5:6, :] + vec_ref[m, 6:7, :]).astype(bf16)

    lane = lax.broadcasted_iota(jnp.int32, (rows, 128), 1)
    first = (lane & (HEAD_DIM - 1)) < HEAD_DIM // 2
    low = lane < HEAD_DIM
    lay_weight(flag_ref, pl.program_id(0), pl.num_programs(0), refs[:-6], w_ref, True)
    for j in range(3):
        hole = (j + 1) * PAD - HEAD_DIM
        wo_ref[0, :, j * HEAD_DIM : (j + 1) * HEAD_DIM] = w_ref[:, hole : hole + HEAD_DIM]
    wo_ref[0, :, PAD - HEAD_DIM :] = jnp.zeros((width, HEAD_DIM), bf16)

    def rotated(y, half, ch):
        z = y[:, 128 * ch : 128 * ch + 128]
        return z * cos_ref[half] + turn(z, first) * sin_ref[half]

    for b in range(4):
        x = x_ref[b]
        y = dot_nn(x, w_ref[:, PAD : 2 * PAD])
        k_ref[b, :, 0:128] = rotated(y, b // 2, 0).astype(bf16)
        k_ref[b, :, 128:PAD] = rotated(y, b // 2, 1).astype(bf16)
        v_ref[b] = dot_nn(x, w_ref[:, 2 * PAD : 3 * PAD]).astype(bf16)
        if b < 2:
            y = dot_nn(x, w_ref[:, 0:PAD])
            scale = HEAD_DIM ** (-0.5)
            q_ref[b, :, 0:128] = rotated(y, 0, 0).astype(bf16) * scale
            q_ref[b, :, 128:PAD] = jnp.where(low, rotated(y, 0, 1), 0.0).astype(bf16) * scale


def qkv_call(flags, tn, hid, other, vec, weights, cos, sin):
    _, rows, width = hid.shape
    blocks = 4
    out = lambda n: pl.BlockSpec((n, rows, PAD), lambda t, r: (0, 0, t))
    one = pl.Buffered(1)
    return pl.pallas_call(
        qkv_kernel,
        grid_spec=pltpu.PrefetchScalarGridSpec(
            num_scalar_prefetch=1,
            grid=(tn,),
            in_specs=[
                whole((2, rows, width), pipeline_mode=one),
                whole((2, rows, width), pipeline_mode=one),
                whole((2, 8, width), pipeline_mode=one),
                whole((2, rows, 128), pipeline_mode=one),
                whole((2, rows, 128), pipeline_mode=one),
                *weight_specs(weights, tn),
            ],
            out_specs=[
                out(2),
                out(blocks),
                out(blocks),
                pl.BlockSpec((1, width, PAD), lambda t, r: (t, 0, 0)),
                whole((blocks, rows, width), pipeline_mode=one),
            ],
            scratch_shapes=[pltpu.VMEM((width, 3 * PAD), bf16)],
        ),
        out_shape=[
            jax.ShapeDtypeStruct((2, rows, tn * PAD), bf16),
            jax.ShapeDtypeStruct((blocks, rows, tn * PAD), bf16),
            jax.ShapeDtypeStruct((blocks, rows, tn * PAD), bf16),
            jax.ShapeDtypeStruct((tn, width, PAD), bf16),
            jax.ShapeDtypeStruct((blocks, rows, width), bf16),
        ],
        compiler_params=params(LIMIT),
        cost_estimate=cost(2 * blocks * rows * width * 640 * tn, 16 * MIB),
        name="qkv_rope",
    )(flags, hid, other, vec, cos, sin, *weights)


def pack_kernel(qkv_ref, attn_ref, a_ref):
    heads_w = qkv_ref.shape[2]
    for j in range(3):
        a_ref[:, j * PAD : j * PAD + heads_w] = qkv_ref[j]
        a_ref[:, j * PAD + heads_w : (j + 1) * PAD] = attn_ref[:, j * HEAD_DIM : (j + 1) * HEAD_DIM]


def pack_weights(qkv_weight, attn_weight):
    shard = qkv_weight.shape[1]
    attn_t = attn_weight.T
    if shard % 16:
        pieces = []
        for j in range(3):
            pieces += [qkv_weight[j], attn_t[:, j * HEAD_DIM : (j + 1) * HEAD_DIM]]
        return jnp.concatenate(pieces, axis=1)
    return pl.pallas_call(
        pack_kernel,
        out_shape=jax.ShapeDtypeStruct((shard, 3 * PAD), bf16),
        name="pack_weights",
    )(qkv_weight, attn_t)


QB = 256
NEG = -1e30


def head_lanes(x, h):
    if h == 2:
        return x
    lane = lax.broadcasted_iota(jnp.int32, x.shape, 1)
    keep = (lane < HEAD_DIM) if h == 0 else (lane >= HEAD_DIM)
    return jnp.where(keep, x, jnp.zeros_like(x))


def in_terms(base, lane, at, x):
    hi = x.astype(bf16).astype(f32)
    rest = x - hi
    mid = rest.astype(bf16).astype(f32)
    out = jnp.where(lane == at + 1, mid, jnp.where(lane == at + 2, rest - mid, base))
    return jnp.where(lane == at, hi, out).astype(bf16)


def attn_fwd_kernel(q_ref, k_ref, v_ref, sq_ref, sk_ref, o_ref, lo_ref, x_ref):
    rows = q_ref.shape[1]
    keys = 2 * rows
    cols_k = sk_ref[0]
    ones = jnp.ones((keys, 128), bf16)
    part = lambda ref, c: ref[..., 128 * c : 128 * c + 128].reshape(keys, 128)
    kx = [jnp.concatenate([part(k_ref, c), cols_k], axis=1) for c in range(2)]
    vx = [jnp.concatenate([part(v_ref, c), ones], axis=1) for c in range(2)]
    lane = lax.broadcasted_iota(jnp.int32, (QB, 128), 1)
    low = lane < HEAD_DIM
    for qb in range(rows // QB):
        span = pl.ds(qb * QB, QB)
        cols_q = sq_ref[0, span, :]
        outs = []
        for h in range(HEADS_PER_BLOCK):
            c = h // 2
            qh = head_lanes(q_ref[0, span, 128 * c : 128 * c + 128], h)
            s = dot_nt(jnp.concatenate([qh, cols_q], axis=1), kx[c])
            top = jnp.max(s, axis=1, keepdims=True)
            o = dot_nn(jnp.exp(s - top).astype(bf16), vx[c])
            total = o[:, 128:]
            outs.append(o[:, :128] / total)
            lse = top + jnp.log(total[:, 0:1])
            x_ref[0, 0, h, span, :] = in_terms(cols_q.astype(f32), lane, 128 - 3, -lse)
        for c, o in enumerate((jnp.where(low, outs[0], outs[1]), outs[2])):
            hi = o.astype(bf16)
            o_ref[0, span, 128 * c : 128 * c + 128] = hi
            lo_ref[0, span, 128 * c : 128 * c + 128] = (o - hi.astype(f32)).astype(bf16)


def attn_fwd_call(q, k, v, cols_q, cols_k):
    _, rows, wide = q.shape
    tn = wide // PAD
    k4 = k.reshape(2, 2, rows, wide)
    v4 = v.reshape(2, 2, rows, wide)
    mine = pl.BlockSpec((1, rows, PAD), lambda m, t: (m, 0, t))
    all_keys = pl.BlockSpec((2, 1, rows, PAD), lambda m, t: (0, m, 0, t))
    return pl.pallas_call(
        attn_fwd_kernel,
        grid=(2, tn),
        in_specs=[
            mine,
            all_keys,
            all_keys,
            pl.BlockSpec((1, rows, 128), lambda m, t: (m, 0, 0)),
            pl.BlockSpec((1, 2 * rows, 128), lambda m, t: (m, 0, 0)),
        ],
        out_specs=[
            mine,
            mine,
            pl.BlockSpec((1, 1, HEADS_PER_BLOCK, rows, 128), lambda m, t: (m, t, 0, 0, 0)),
        ],
        out_shape=[
            jax.ShapeDtypeStruct((2, rows, wide), bf16),
            jax.ShapeDtypeStruct((2, rows, wide), bf16),
            jax.ShapeDtypeStruct((2, tn, HEADS_PER_BLOCK, rows, 128), bf16),
        ],
        compiler_params=params(LIMIT, 2),
        cost_estimate=cost(
            2 * tn * 3 * 2 * 2 * rows * 2 * rows * 256, 18 * MIB, 2 * tn * 3 * rows * 2 * rows
        ),
        name="attn_fwd",
    )(q, k4, v4, cols_q, cols_k)


def attn_bwd_kernel(
    tl_ref,
    q_ref,
    k_ref,
    v_ref,
    g_ref,
    o_ref,
    lo_ref,
    x_ref,
    sk_ref,
    cos_ref,
    sin_ref,
    norm_ref,
    wat_ref,
    dq_ref,
    own_ref,
    oth_ref,
    proj_ref,
    acc_ref,
):
    rows = q_ref.shape[1]
    keys = 2 * rows
    cols_k = sk_ref[0]
    lane = lax.broadcasted_iota(jnp.int32, (QB, 128), 1)
    low = lane < HEAD_DIM
    key_lane = lax.broadcasted_iota(jnp.int32, (keys, 128), 1)
    terms = jnp.where(key_lane < 3, 1.0, 0.0).astype(bf16)

    def unrotated(y, lanes, cos, sin):
        return y * cos - turn(y, (lanes & (HEAD_DIM - 1)) < HEAD_DIM // 2) * sin

    for c in range(2):
        ch = slice(128 * c, 128 * c + 128)
        kc = k_ref[..., ch].reshape(keys, 128)
        kt = kc.T
        kx = jnp.concatenate([kc, cols_k], axis=1)
        vx = jnp.concatenate([v_ref[..., ch].reshape(keys, 128), terms], axis=1)
        dk = jnp.zeros((keys, 128), f32)
        dv = jnp.zeros((keys, 128), f32)
        for qb in range(rows // QB):
            span = pl.ds(qb * QB, QB)
            qc = q_ref[0, span, ch]
            gc = g_ref[0, span, ch]
            prod = gc.astype(f32) * (o_ref[0, span, ch].astype(f32) + lo_ref[0, span, ch].astype(f32))
            dqs = []
            for h in (0, 1) if c == 0 else (2,):
                qh = head_lanes(qc, h)
                gh = head_lanes(gc, h)
                inner = jnp.sum(head_lanes(prod, h), axis=1, keepdims=True)
                gx = in_terms(jnp.zeros((QB, 128), f32), lane, 0, -inner)
                p = jnp.exp(dot_nt(kx, jnp.concatenate([qh, x_ref[0, 0, h, span, :]], axis=1)))
                ds = (p * dot_nt(vx, jnp.concatenate([gh, gx], axis=1))).astype(bf16)
                dv += dot_nn(p.astype(bf16), gh)
                dk += dot_nn(ds, qh)
                dqs.append(dot_nn(kt, ds).T * HEAD_DIM ** (-0.5))
            dq = jnp.where(low, dqs[0], dqs[1] if c == 0 else 0.0)
            dq_ref[0, 0, span, ch] = unrotated(dq, lane, cos_ref[span, :], sin_ref[span, :]).astype(bf16)
        dk = unrotated(dk, key_lane, cos_ref[...], sin_ref[...])
        for half, ref in enumerate((own_ref, oth_ref)):
            some = slice(half * rows, (half + 1) * rows)
            ref[0, 0, 0, :, ch] = dk[some].astype(bf16)
            ref[0, 1, 0, :, ch] = dv[some].astype(bf16)

    slot, m = pl.program_id(0), pl.program_id(1)
    for j in range(3):

        @pl.when(slot == 0)
        def _():
            cols = slice(j * PAD, (j + 1) * PAD)
            if j == 0:
                part = dot_tn(norm_ref[0, 0], dq_ref[0, 0])
            else:
                part = dot_tn(norm_ref[0, 0], own_ref[0, j - 1, 0])
                part += dot_tn(norm_ref[1, 0], oth_ref[0, j - 1, 0])

            @pl.when(m == 0)
            def _():
                acc_ref[:, cols] = part

            @pl.when(m == 1)
            def _():
                edge = (j + 1) * PAD - HEAD_DIM
                total = acc_ref[:, cols] + part
                proj_ref[:, j * PAD : edge] = total[:, : PAD - HEAD_DIM].astype(bf16)
                proj_ref[:, edge : edge + HEAD_DIM] = wat_ref[:, j * HEAD_DIM : (j + 1) * HEAD_DIM]


def attn_bwd_call(tlist, g, q, k, v, o, lo, x, cols_k, cos, sin, normed, wat):
    _, rows, wide = q.shape
    width = normed.shape[-1]
    one = pl.Buffered(1)
    nt = tlist.shape[0]
    k4 = k.reshape(2, 2, rows, wide)
    v4 = v.reshape(2, 2, rows, wide)
    mine = pl.BlockSpec((1, rows, PAD), lambda i, m, tl: (m, 0, tl[i]))
    all_keys = pl.BlockSpec((2, 1, rows, PAD), lambda i, m, tl: (0, m, 0, tl[i]))
    kv_out = pl.BlockSpec((1, 2, 1, rows, PAD), lambda i, m, tl: (i, 0, m, 0, 0))
    return pl.pallas_call(
        attn_bwd_kernel,
        grid_spec=pltpu.PrefetchScalarGridSpec(
            num_scalar_prefetch=1,
            grid=(nt, 2),
            in_specs=[
                mine,
                all_keys,
                all_keys,
                mine,
                mine,
                mine,
                pl.BlockSpec(
                    (1, 1, HEADS_PER_BLOCK, rows, 128), lambda i, m, tl: (m, tl[i], 0, 0, 0)
                ),
                pl.BlockSpec((1, 2 * rows, 128), lambda i, m, tl: (m, 0, 0)),
                whole((2 * rows, 128), pipeline_mode=one),
                whole((2 * rows, 128), pipeline_mode=one),
                pl.BlockSpec(
                    (2, 1, rows, width), lambda i, m, tl: (0, jnp.where(i == 0, m, 1), 0, 0)
                ),
                whole((width, PAD), pipeline_mode=one),
            ],
            out_specs=[
                pl.BlockSpec((1, 1, rows, PAD), lambda i, m, tl: (i, m, 0, 0)),
                kv_out,
                kv_out,
                whole((width, 3 * PAD), pipeline_mode=one),
            ],
            scratch_shapes=[pltpu.VMEM((width, 3 * PAD), f32)],
        ),
        out_shape=[
            jax.ShapeDtypeStruct((nt, 2, rows, PAD), bf16),
            jax.ShapeDtypeStruct((nt, 2, 2, rows, PAD), bf16),
            jax.ShapeDtypeStruct((nt, 2, 2, rows, PAD), bf16),
            jax.ShapeDtypeStruct((width, 3 * PAD), bf16),
        ],
        compiler_params=params(LIMIT, 2),
        cost_estimate=cost(
            2 * nt * 3 * 5 * 2 * rows * 2 * rows * 256, 5 * nt * MIB, 2 * nt * 3 * rows * 2 * rows
        ),
        name="attn_bwd",
    )(
        tlist,
        q,
        k4,
        v4,
        g,
        o,
        lo,
        x,
        cols_k,
        cos.reshape(2 * rows, 128),
        sin.reshape(2 * rows, 128),
        normed.reshape(2, 2, rows, width),
        wat,
    )


RB = 512
LAST_RB = 256


def dot_tn(a, b):
    return lax.dot_general(a, b, (((0,), (0,)), ((), ())), preferred_element_type=f32)


def normalise(h):
    mean = jnp.mean(h, axis=-1, keepdims=True)
    cent = h - mean
    var = jnp.mean(cent * cent, axis=-1, keepdims=True)
    rstd = lax.rsqrt(var + NORM_EPS)
    return cent * rstd, rstd


def block_kernel(
    flag_ref,
    mix_ref,
    wout_ref,
    hid_ref,
    vec_ref,
    cot_ref,
    mask_ref,
    ub_ref,
    ff_ref,
    out_ref,
    dh_ref,
    mg_ref,
    sum_ref,
    wff_ref,
    wat_ref,
    up_ref,
    dn_ref,
    x_ref,
    g_ref,
    bl_ref,
    mine_ref,
    act_ref,
    ul_ref,
    acts_ref,
    uls_ref,
    h1_ref,
    br_ref,
    d_ref,
    n_ref,
    sem,
):
    step = pl.program_id(0)
    steps = pl.num_programs(0)
    own = flag_ref[0]
    width = hid_ref.shape[1]
    tn = ff_ref.shape[0]
    ff = ub_ref.shape[2]
    here = pl.ds(pl.multiple_of(step * RB, RB), RB)

    def fetch(j):
        cols = pl.ds(pl.multiple_of(j * ff, ff), ff)
        return (
            pltpu.make_async_copy(ff_ref.at[j, :, 0:ff], up_ref.at[:, cols], sem.at[2 * j]),
            pltpu.make_async_copy(ff_ref.at[j, :, ff : 2 * ff], dn_ref.at[:, cols], sem.at[2 * j + 1]),
        )

    @pl.when(step == 0)
    def _():
        for j in range(tn):
            for copy in fetch(j):
                copy.start()

    gate1, gain2, shift2 = vec_ref[0, 0:1, :], vec_ref[0, 1:2, :], vec_ref[0, 2:3, :]
    gate2, dbias = vec_ref[0, 3:4, :], vec_ref[0, 4:5, :]
    acc = dot_nt(mix_ref[:, 0:PAD], wout_ref[0])
    for t in range(1, tn):
        acc += dot_nt(mix_ref[:, t * PAD : (t + 1) * PAD], wout_ref[t])
    br_ref[...] = acc
    h1 = hid_ref[...].astype(f32) + gate1 * acc
    h1_ref[...] = h1
    n, _ = normalise(h1)
    x = (n * gain2 + shift2).astype(bf16)
    x_ref[here, :] = x
    cot = cot_ref[...].astype(f32) * mask_ref[...]
    g = (cot * gate2).astype(bf16)
    g_ref[here, :] = g
    mine_ref[here, :] = mix_ref[:, pl.ds(pl.multiple_of(own * PAD, PAD), PAD)]

    def units(j, carry):
        @pl.when(step == 0)
        def _():
            for copy in fetch(j):
                copy.wait()

        cols = pl.ds(pl.multiple_of(j * ff, ff), ff)
        u = dot_nn(x_ref[here, :], up_ref[:, cols]) + ub_ref[lax.rem(own - j + tn, tn)]
        da = dot_nn(g_ref[here, :], dn_ref[:, cols])
        u2 = u * u
        th = jnp.tanh(GELU_C * u * (1.0 + 0.044715 * u2))
        half_up = 0.5 * (1.0 + th)
        slope = half_up + (0.5 * GELU_C) * u * (1.0 - th * th) * (1.0 + (3 * 0.044715) * u2)
        acts_ref[:, cols] = (u * half_up).astype(bf16)
        uls_ref[:, cols] = (da * slope).astype(bf16)
        return carry

    lax.fori_loop(0, tn, units, 0)
    mine = pl.ds(pl.multiple_of(own * ff, ff), ff)
    act_ref[here, :] = acts_ref[:, mine]
    ul_ref[here, :] = uls_ref[:, mine]
    for c in range(0, width, PAD):
        cols = slice(c, c + PAD)
        d_ref[:, cols] = dot_nt(acts_ref[...], dn_ref[cols, :])
        n_ref[:, cols] = dot_nt(uls_ref[...], up_ref[cols, :])

    down = d_ref[...] + dbias
    h1 = h1_ref[...]
    out_ref[...] = (h1 + gate2 * down).astype(bf16)
    n, rstd = normalise(h1)
    grad = n_ref[...]
    gn = grad * n
    e = grad * gain2
    en = gn * gain2
    dh = cot + rstd * (
        e - jnp.mean(e, axis=-1, keepdims=True) - n * jnp.mean(en, axis=-1, keepdims=True)
    )
    dh_ref[...] = dh
    bl = (dh * gate1).astype(bf16)
    bl_ref[here, :] = bl
    for t in range(tn):
        mg_ref[:, t * PAD : (t + 1) * PAD] = dot_nn(bl, wout_ref[t]).astype(bf16)

    @pl.when(lax.rem(step, steps // 2) == 0)
    def _():
        sum_ref[...] = jnp.zeros_like(sum_ref)

    parts = (cot * down, cot, grad, gn, dh * br_ref[...], uls_ref[:, mine].astype(f32))
    for r, part in enumerate(parts):
        sum_ref[0, r : r + 1, :] += jnp.sum(part, axis=0, keepdims=True)

    @pl.when(step == steps - 1)
    def _():
        def column(c, carry):
            cols = pl.ds(pl.multiple_of(c * PAD, PAD), PAD)
            wff_ref[:, cols] = dot_tn(x_ref[...], ul_ref[:, cols])
            far = pl.ds(pl.multiple_of(ff + c * PAD, PAD), PAD)
            wff_ref[:, far] = dot_tn(g_ref[...], act_ref[:, cols])
            return carry

        lax.fori_loop(0, ff // PAD, column, 0)
        wat_ref[...] = dot_tn(bl_ref[...], mine_ref[...]).astype(bf16)


def block_call(flags, mixed, w_out, hid, vec, cot, mask_col, w_ff, up_bias):
    rows, wide = mixed.shape
    width = hid.shape[1]
    tn, _, ff = w_ff.shape
    ff = ff // 2
    one = pl.Buffered(1)
    steps = rows // RB
    row = lambda w: pl.BlockSpec((RB, w), lambda i, o: (i, 0))
    vecs = pl.BlockSpec((1, 8, width), lambda i, o: (i // (steps // 2), 0, 0))
    tokens = lambda dtype, w, n=rows: pltpu.VMEM((n, w), dtype)
    return pl.pallas_call(
        block_kernel,
        grid_spec=pltpu.PrefetchScalarGridSpec(
            num_scalar_prefetch=1,
            grid=(steps,),
            in_specs=[
                row(wide),
                whole((tn, width, PAD), pipeline_mode=one),
                row(width),
                vecs,
                row(width),
                row(1),
                whole((tn, 1, ff), pipeline_mode=one),
                pl.BlockSpec(memory_space=pl.ANY),
            ],
            out_specs=[
                row(width),
                row(width),
                row(wide),
                vecs,
                whole((width, 2 * ff), pipeline_mode=one),
                whole((width, PAD), pipeline_mode=one),
            ],
            scratch_shapes=[
                tokens(bf16, tn * ff, width),
                tokens(bf16, tn * ff, width),
                tokens(bf16, width),
                tokens(bf16, width),
                tokens(bf16, width),
                tokens(bf16, PAD),
                tokens(bf16, ff),
                tokens(bf16, ff),
                tokens(bf16, tn * ff, RB),
                tokens(bf16, tn * ff, RB),
                tokens(f32, width, RB),
                tokens(f32, width, RB),
                tokens(f32, width, RB),
                tokens(f32, width, RB),
                pltpu.SemaphoreType.DMA((2 * tn,)),
            ],
        ),
        out_shape=[
            jax.ShapeDtypeStruct((rows, width), bf16),
            jax.ShapeDtypeStruct((rows, width), f32),
            jax.ShapeDtypeStruct((rows, wide), bf16),
            jax.ShapeDtypeStruct((2, 8, width), f32),
            jax.ShapeDtypeStruct((width, 2 * ff), f32),
            jax.ShapeDtypeStruct((width, PAD), bf16),
        ],
        compiler_params=params(LIMIT),
        cost_estimate=cost(
            4 * 2 * rows * width * ff * tn + 8 * rows * width * width, 32 * MIB, rows * ff * tn
        ),
        name="block_both",
    )(flags, mixed, w_out, hid, vec, cot, mask_col, up_bias, w_ff)


def table_kernel(flag_ref, seg_ref, cos_ref, sin_ref, sq_ref, sk_ref):
    rows = seg_ref.shape[3]
    lane = lax.broadcasted_iota(jnp.int32, (rows, 128), 1)
    fixed = lane >= 128 - 3
    pair = (lane & (HEAD_DIM // 2 - 1)).astype(f32)
    freq = jnp.exp(pair * (-2.0 * math.log(10000.0) / HEAD_DIM))
    sign = jnp.where((lane & (HEAD_DIM - 1)) < HEAD_DIM // 2, -1.0, 1.0)
    row = lax.broadcasted_iota(jnp.int32, (rows, 128), 0)
    for half in range(2):
        angle = (row + flag_ref[half]).astype(f32) * freq
        cos_ref[half] = jnp.cos(angle)
        sin_ref[half] = jnp.sin(angle) * sign
        for m in range(2):
            ids = jnp.broadcast_to(seg_ref[m, half].astype(f32), (128, rows)).T
            same = (ids == lane.astype(f32)) | fixed
            sk_ref[m, half] = jnp.where(same, 1.0, 0.0).astype(bf16)
            if half == 0:
                sq_ref[m] = jnp.where(same, 0.0, NEG).astype(bf16)


def table_call(starts, segments):
    _, _, _, rows = segments.shape
    cos, sin, cols_q, cols_k = pl.pallas_call(
        table_kernel,
        grid_spec=pltpu.PrefetchScalarGridSpec(
            num_scalar_prefetch=1,
            grid=(1,),
            in_specs=[whole(segments.shape)],
            out_specs=[
                whole((2, rows, 128)),
                whole((2, rows, 128)),
                whole((2, rows, 128)),
                whole((2, 2, rows, 128)),
            ],
        ),
        out_shape=[
            jax.ShapeDtypeStruct((2, rows, 128), f32),
            jax.ShapeDtypeStruct((2, rows, 128), f32),
            jax.ShapeDtypeStruct((2, rows, 128), bf16),
            jax.ShapeDtypeStruct((2, 2, rows, 128), bf16),
        ],
        compiler_params=params(LIMIT),
        cost_estimate=cost(100 * 2 * rows * 128, 3 * MIB),
        name="tables",
    )(starts, segments)
    return cos, sin, cols_q, cols_k.reshape(2, 2 * rows, 128)


def last_kernel(
    flag_ref,
    dq_ref,
    kv_ref,
    rv_ref,
    hid_ref,
    dh_ref,
    vec_ref,
    early_ref,
    *refs,
):
    out_ref, sum_ref, w_ref, d_ref, acc_ref = refs[-5:]
    first = pl.program_id(1) == 0
    own = flag_ref[0]
    tn = dq_ref.shape[0]

    @pl.when(first & (pl.program_id(0) == 0))
    def _():
        for t in range(tn):
            cols = pl.ds(3 * PAD * t, 3 * PAD)
            lay_weight(flag_ref, t, tn, refs[:-5], w_ref.at[:, cols], False)

    for t in range(tn):
        slot = lax.rem(t - own + tn, tn)
        at = 3 * PAD * t
        d_ref[:, at : at + PAD] = dq_ref[slot, 0]
        for j in range(2):
            at += PAD
            d = kv_ref[slot, j, 0].astype(f32) + rv_ref[slot, j, 0].astype(f32)
            d_ref[:, at : at + PAD] = d.astype(bf16)
    width = hid_ref.shape[2]
    for c in range(0, width, PAD):
        acc_ref[:, c : c + PAD] = dot_nt(d_ref[...], w_ref[c : c + PAD, :])
    acc = acc_ref[...]
    gain1 = vec_ref[0, 5:6, :]
    n, rstd = normalise(hid_ref[0].astype(f32))
    gn = acc * n
    e = acc * gain1
    en = gn * gain1
    out_ref[0] = dh_ref[0] + rstd * (
        e - jnp.mean(e, axis=-1, keepdims=True) - n * jnp.mean(en, axis=-1, keepdims=True)
    )

    @pl.when(first)
    def _():
        sum_ref[0, 0:2, :] = jnp.zeros((2, sum_ref.shape[2]), f32)
        sum_ref[0, 2:8, :] = early_ref[0, 0:6, :]

    sum_ref[0, 0:1, :] += jnp.sum(acc, axis=0, keepdims=True)
    sum_ref[0, 1:2, :] += jnp.sum(gn, axis=0, keepdims=True)


def last_call(flags, dq, kv, rv, weights, hid, dh, vec, early):
    _, rows, width = hid.shape
    tn = dq.shape[0]
    row = pl.BlockSpec((1, LAST_RB, width), lambda m, i, o: (m, i, 0))
    vecs = pl.BlockSpec((1, 8, width), lambda m, i, o: (m, 0, 0))
    q_spec = lambda n: pl.BlockSpec((n, 1, LAST_RB, PAD), lambda m, i, o: (0, m, i, 0))
    kv_spec = lambda n: pl.BlockSpec((n, 2, 1, LAST_RB, PAD), lambda m, i, o: (0, 0, m, i, 0))
    return pl.pallas_call(
        last_kernel,
        grid_spec=pltpu.PrefetchScalarGridSpec(
            num_scalar_prefetch=1,
            grid=(2, rows // LAST_RB),
            in_specs=[
                q_spec(tn),
                kv_spec(tn),
                kv_spec(tn),
                row,
                row,
                vecs,
                vecs,
                *[whole(w.shape, pipeline_mode=pl.Buffered(1)) for w in weights],
            ],
            out_specs=[row, vecs],
            scratch_shapes=[
                pltpu.VMEM((width, tn * 3 * PAD), bf16),
                pltpu.VMEM((LAST_RB, tn * 3 * PAD), bf16),
                pltpu.VMEM((LAST_RB, width), f32),
            ],
        ),
        out_shape=[
            jax.ShapeDtypeStruct((2, rows, width), f32),
            jax.ShapeDtypeStruct((2, 8, width), f32),
        ],
        compiler_params=params(LIMIT, 2),
        cost_estimate=cost(2 * 2 * rows * width * tn * 3 * PAD, 24 * MIB),
        name="first_norm_bwd",
    )(flags, dq, kv, rv, hid, dh, vec, early, *weights)


def split_terms(x):
    hi = x.astype(bf16)
    rest = x - hi.astype(f32)
    mid = rest.astype(bf16)
    return [hi, mid, (rest - mid.astype(f32)).astype(bf16)]


def finish_kernel(flag_ref, sums_ref, mod_ref, norm_ref, cond_ref, ada_ref, *refs):
    gada_ref, gadab_ref, gcond_ref, gn1_ref, gn2_ref, gdb_ref, gub_ref, all_ref = refs
    group, ada_cols, _ = ada_ref.shape
    width = sums_ref.shape[3]
    place = flag_ref[0]
    norm_one, norm_two = norm_ref[0:1, :], norm_ref[1:2, :]
    one = jnp.zeros((1, width), f32)
    small = [one, one, one, one]
    for f in range(group // 2):
        for m in range(2):
            s = 2 * f + m
            r = sums_ref[2 * f, m] + sums_ref[2 * f + 1, m]
            r = [r[i : i + 1, :] for i in range(8)]
            parts = (r[0], r[1] * norm_one, r[6], r[4], r[5] * norm_two, r[2])
            for i, part in enumerate(parts):
                all_ref[s : s + 1, i * width : (i + 1) * width] = part
            scale_one, scale_two, gate_two = (
                mod_ref[s : s + 1, i * width : (i + 1) * width] for i in (1, 4, 5)
            )
            terms = (r[1] * (1.0 + scale_one), r[5] * (1.0 + scale_two), r[3] * gate_two, r[7])
            small = [total + term for total, term in zip(small, terms)]

    def own_columns(x, count):
        total = x.shape[1]
        return pltpu.roll(x, lax.rem(total - place * count, total), 1)[:, :count]

    for ref, total in zip((gn1_ref, gn2_ref, gdb_ref, gub_ref), small):
        shard = ref.shape[1]
        ref[...] = own_columns(jnp.broadcast_to(total, (8, width)), shard)[0:1, :]
    mine = own_columns(all_ref[...], ada_cols)
    gadab_ref[...] = jnp.sum(mine, axis=0, keepdims=True)
    cond = cond_ref[...]
    terms = split_terms(mine)
    gada_ref[...] = dot_tn(terms[0], cond) + dot_tn(terms[1], cond) + dot_tn(terms[2], cond)
    total = jnp.zeros((8, cond.shape[1]), f32)
    seqs = all_ref[pl.ds(pl.multiple_of(flag_ref[1] * 8, 8), 8), :]
    for term in split_terms(seqs):
        for c in range(group):
            total += dot_nn(term[:, c * ada_cols : (c + 1) * ada_cols], ada_ref[c])
    for i in range(4):

        @pl.when(flag_ref[2] == i)
        def _():
            gcond_ref[...] = total[2 * i : 2 * i + 2]


def finish_call(flags, sums, mod_all, norms, cond, ada):
    group, ada_cols, cond_w = ada.shape
    shard = sums.shape[3] // group
    out = [(ada_cols, cond_w), (1, ada_cols), (2, cond_w)] + [(1, shard)] * 4
    return pl.pallas_call(
        finish_kernel,
        grid_spec=pltpu.PrefetchScalarGridSpec(
            num_scalar_prefetch=1,
            grid=(1,),
            in_specs=[whole(x.shape) for x in (sums, mod_all, norms, cond, ada)],
            out_specs=[whole(x) for x in out],
            scratch_shapes=[pltpu.VMEM(mod_all.shape, f32)],
        ),
        out_shape=[jax.ShapeDtypeStruct(x, f32) for x in out],
        compiler_params=params(LIMIT),
        cost_estimate=cost(1 << 20, 3 * MIB),
        name="finish",
    )(flags, sums, mod_all, norms, cond, ada)


def spread(x, axes):
    count = lax.axis_size(axes)
    many = jnp.broadcast_to(x[None], (count,) + x.shape)
    return lax.all_to_all(many, axes, split_axis=0, concat_axis=0, tiled=True)


def join_cores(part, other, rank):
    fs, tn, rows, width = part.shape
    both = jnp.stack([jnp.where(rank == 0, part, other), jnp.where(rank == 0, other, part)], axis=1)
    return both.transpose(2, 0, 1, 3, 4).reshape(1, tn, fs * 2 * rows, width)


def gather_rows(row):
    tn = lax.axis_size("tp")
    got = [row]
    for step in range(1, tn):
        got.append(lax.ppermute(row, "tp", [(i, (i + step) % tn) for i in range(tn)]))
    return jnp.stack(got).astype(f32)


def exchange_to_shard(grad):
    group = lax.axis_size(FC)
    parts = grad.reshape(group, -1, grad.shape[1])
    return lax.all_to_all(parts, FC, split_axis=0, concat_axis=0, tiled=True)


def on_device(
    hidden_in,
    cond_vec,
    segment_ids,
    pad_mask,
    out_cot,
    qkv_weight,
    attn_weight,
    up_weight,
    up_bias,
    down_weight,
    down_bias,
    ada_weight,
    ada_bias,
    attn_norm,
    mlp_norm,
):
    rank = lax.axis_index("ctx")
    own = lax.axis_index("tp")
    fs = lax.axis_size("fsdp")
    tn = lax.axis_size("tp")
    hid = hidden_in[:, 0]
    _, rows, width = hid.shape
    shard = qkv_weight.shape[1]
    heads_w = qkv_weight.shape[2]
    cond_w = cond_vec.shape[2]
    highest = lax.Precision.HIGHEST

    w_attn_shard = pack_weights(qkv_weight, attn_weight)
    ada_cols = ada_bias.shape[0]
    extra = [cond_vec[:, 0]]
    up_rows = gather_rows(jnp.pad(up_bias, (0, cond_w - shard)).reshape(1, cond_w)).astype(bf16)
    for x in (down_bias, attn_norm, mlp_norm, up_rows.reshape(-1), ada_bias):
        extra.append(jnp.pad(x, (0, -x.shape[0] % cond_w)).reshape(-1, cond_w))
    extra = jnp.concatenate(extra, axis=0)
    ada_rows = jnp.concatenate([ada_weight.T, extra], axis=0)
    ada_rows = jnp.pad(ada_rows, ((0, -ada_rows.shape[0] % 16), (0, 0)))
    w_ff = jnp.concatenate([up_weight, down_weight.T], axis=1)
    w_ff = lax.all_gather(w_ff, ("tp",) + FC, axis=0, tiled=True).reshape(tn, width, -1)
    ada_rows = spread(ada_rows, FC)
    along = lax.all_gather(w_attn_shard, "tp", axis=0, tiled=False)
    in_parts = fs == 4 and tn % 2 == 0 and shard % 16 == 0
    if in_parts:
        lower, upper = along[: tn // 2], along[tn // 2 :]
        x_lower = lax.ppermute(lower, "fsdp", ALONG_X)
        y_upper = lax.ppermute(upper, "fsdp", ALONG_Y)
        x_upper = lax.ppermute(upper, "fsdp", ALONG_X)
        y_lower = lax.ppermute(lower, "fsdp", ALONG_Y)

    ada_full = ada_rows[:, :ada_cols]
    small = ada_rows[:, ada_cols:]
    cond_all = small[:, :2].reshape(fs, 2, 2, cond_w)[:, 0]
    modulation_all = jnp.einsum(
        "smk,fck->smfc", cond_all, ada_full, preferred_element_type=f32
    ).reshape(fs, 2, -1)
    small = small.astype(f32)
    dnb_full = small[:, 2, :shard].reshape(-1)
    norm_one = small[:, 3, :shard].reshape(-1)
    norm_two = small[:, 4, :shard].reshape(-1)
    upb_full = small[:, 5 : 5 + tn, :shard].transpose(1, 0, 2).reshape(tn, 1, -1)
    adab_full = small[:, 5 + tn :].reshape(2 * fs, -1)[:, :ada_cols].reshape(-1)
    modulation_all = modulation_all + adab_full
    modulation = lax.dynamic_index_in_dim(modulation_all, lax.axis_index("fsdp"), 0, keepdims=False)
    shift_one, scale_one, gate_one, shift_two, scale_two, gate_two = jnp.split(modulation, 6, axis=1)
    gain_one = norm_one * (1.0 + scale_one)
    gain_two = norm_two * (1.0 + scale_two)
    zero = jnp.zeros_like(gain_one)
    vec = jnp.stack(
        [
            gate_one,
            gain_two,
            shift_two,
            gate_two,
            jnp.broadcast_to(dnb_full, gain_one.shape),
            gain_one,
            shift_one,
            zero,
        ],
        axis=1,
    )

    hid_other = lax.ppermute(hid, "ctx", SWAP)
    seg = segment_ids[:, 0]
    halves = jnp.where(rank == 0, seg.reshape(2, 2, 1, rows), seg.reshape(2, 2, 1, rows)[:, ::-1])
    starts = jnp.stack([rank * rows, (1 - rank) * rows]).astype(jnp.int32)
    cos, sin, cols_q, cols_k = table_call(starts, halves)
    mask = lax.dynamic_slice_in_dim(pad_mask[:, 0], rank * rows, rows, axis=1).astype(f32)
    cot = out_cot[:, 0]

    if in_parts:
        d_lower = lax.ppermute(x_lower, "fsdp", ALONG_Y)
        d_upper = lax.ppermute(y_upper, "fsdp", ALONG_X)
        w_attn = [along, x_lower, x_upper, y_lower, y_upper, d_lower, d_upper]
        w_attn = w_attn + [lax.ppermute(part, "ctx", SWAP) for part in w_attn]
    else:
        w_own = spread(along, "fsdp")
        w_own = join_cores(w_own, lax.ppermute(w_own, "ctx", SWAP), rank)
        w_attn = [w_own[:, :, : width // 2], w_own[:, :, width // 2 :]]
    sources = lax.axis_index("fsdp") ^ jnp.arange(4, dtype=jnp.int32)
    flags = jnp.concatenate(
        [own.reshape(1), jnp.zeros((1,), jnp.int32), 2 * sources + rank, 2 * sources + 1 - rank]
    ).astype(jnp.int32)
    q, k, v, w_out, normed_all = qkv_call(flags, tn, hid, hid_other, vec, w_attn, cos, sin)
    mixed, mixed_lo, score_cols = attn_fwd_call(q, k, v, cols_q, cols_k)

    own_index = own.reshape(1).astype(jnp.int32)
    flat = lambda x: x.reshape(2 * rows, -1)
    block_out, dh_one, mixed_grad, sums_two, ff_low, attn_low = block_call(
        flags,
        flat(mixed),
        w_out,
        flat(hid),
        vec,
        flat(cot),
        mask.reshape(-1, 1),
        w_ff,
        upb_full,
    )
    mixed_grad = mixed_grad.reshape(2, rows, -1)
    ff_low, mixed_grad = lax.optimization_barrier((ff_low, mixed_grad))
    ff_shard = lax.psum_scatter(ff_low, FC, scatter_dimension=0, tiled=True)

    order = lax.rem(own + jnp.arange(tn, dtype=jnp.int32), tn).astype(jnp.int32)
    dq, kv_own, kv_send, proj_low = attn_bwd_call(
        order, mixed_grad, q, k, v, mixed, mixed_lo, score_cols, cols_k, cos, sin, normed_all, attn_low
    )

    kv_send, proj_low = lax.optimization_barrier((kv_send, proj_low))
    kv_got = lax.ppermute(kv_send, "ctx", SWAP)
    proj_got = exchange_to_shard(proj_low)

    hidden_grad, sums_one = last_call(
        flags, dq, kv_own, kv_got, w_attn, hid, dh_one.reshape(hid.shape), vec, sums_two
    )

    all_sums = lax.all_gather(sums_one, FC, axis=0, tiled=False)
    all_sums, proj_got, ff_shard = lax.optimization_barrier((all_sums, proj_got, ff_shard))
    seq = lax.axis_index("fsdp")
    finish_flags = jnp.stack([lax.axis_index(FC), seq // 4, seq % 4]).astype(jnp.int32)
    grads = finish_call(
        finish_flags,
        all_sums,
        modulation_all.reshape(2 * fs, -1),
        jnp.stack([norm_one, norm_two]),
        cond_all.reshape(2 * fs, cond_w),
        ada_full,
    )
    grad_ada, grad_adabias, cond_grad, attnnorm, mlpnorm, downbias, upbias = grads
    attn_shard = jnp.sum(proj_got.astype(f32), axis=0)

    grad_qkv = jnp.stack([attn_shard[:, j * PAD : j * PAD + heads_w] for j in range(3)])
    grad_attn = jnp.concatenate(
        [attn_shard[:, j * PAD + heads_w : (j + 1) * PAD] for j in range(3)], axis=1
    ).T
    return (
        block_out.reshape(hidden_in.shape),
        hidden_grad[:, None],
        cond_grad[:, None],
        grad_qkv,
        grad_attn,
        ff_shard[:, : ff_shard.shape[1] // 2],
        upbias[0],
        ff_shard[:, ff_shard.shape[1] // 2 :].T,
        downbias[0],
        grad_ada.T,
        grad_adabias[0],
        attnnorm[0],
        mlpnorm[0],
    )


def solution(mesh):
    tokens = P(None, "fsdp", "ctx", None)
    per_seq = P(None, "fsdp", None)
    weights = (
        P(None, FC, "tp"),
        P("tp", FC),
        P(FC, "tp"),
        P(("tp",) + FC),
        P("tp", FC),
        P(FC),
        P(None, FC),
        P(FC),
        P(FC),
        P(FC),
    )
    return jax.shard_map(
        on_device,
        mesh=mesh,
        in_specs=(tokens, per_seq, per_seq, per_seq, tokens) + weights,
        out_specs=(tokens, tokens, per_seq) + weights,
        check_vma=False,
    )
```

```python
import functools
import math

import jax
import jax.numpy as jnp
from jax import lax
from jax.experimental import pallas as pl
from jax.experimental.pallas import tpu as pltpu
from jax.sharding import PartitionSpec as P

HEAD_DIM = 64
HEADS_PER_BLOCK = 3
PAD = 256
NORM_EPS = 1e-05
GELU_C = math.sqrt(2.0 / math.pi)
bf16 = jnp.bfloat16
f32 = jnp.float32
FC = ("fsdp", "ctx")
SWAP = [(0, 1), (1, 0)]
ALONG_X = [(0, 1), (1, 0), (2, 3), (3, 2)]
ALONG_Y = [(0, 2), (2, 0), (1, 3), (3, 1)]
MIB = 1 << 20
LIMIT = 60


def dot_nn(a, b):
    return lax.dot_general(a, b, (((1,), (0,)), ((), ())), preferred_element_type=f32)


def dot_nt(a, b):
    return lax.dot_general(a, b, (((1,), (1,)), ((), ())), preferred_element_type=f32)


def params(limit, axes=1):
    return pltpu.CompilerParams(
        dimension_semantics=("arbitrary",) * axes, vmem_limit_bytes=limit * MIB
    )


def cost(flops, nbytes, trans=0):
    return pl.CostEstimate(flops=flops, bytes_accessed=nbytes, transcendentals=trans)


def whole(shape, **kw):
    return pl.BlockSpec(shape, lambda *_: (0,) * len(shape), **kw)


def turn(x, first):
    return jnp.where(first, pltpu.roll(x, 96, 1), pltpu.roll(x, 32, 1))


def interleave(rank, own_ref, oth_ref, out_ref, col):
    count, shard = own_ref.shape[0], own_ref.shape[2]
    cols = slice(col, col + out_ref.shape[1])
    for c in range(2):

        @pl.when(rank == c)
        def _():
            for f in range(count):
                at = 2 * f * shard
                mine, theirs = at + c * shard, at + (1 - c) * shard
                out_ref[mine : mine + shard, :] = own_ref[f, 0, :, cols]
                out_ref[theirs : theirs + shard, :] = oth_ref[f, 0, :, cols]


def lay_weight(flag_ref, t, tn, refs, out_ref, held):
    half = tn // 2
    if len(refs) == 2:
        own_ref, oth_ref = refs if held else [ref.at[:, t : t + 1] for ref in refs]
        interleave(flag_ref[1], own_ref, oth_ref, out_ref, 0)
        return
    shard = refs[0].shape[1]

    def copy(src, row):
        out_ref[pl.ds(pl.multiple_of(row * shard, shard), shard), :] = src

    for core in range(2):
        parts = refs[7 * core : 7 * core + 7]
        for k in range(4):
            row = flag_ref[2 + 4 * core + k]
            if k == 0:
                copy(parts[0][0 if held else t], row)
            elif held:
                pl.when(t < half)(lambda: copy(parts[2 * k - 1][0], row))
                pl.when(t >= half)(lambda: copy(parts[2 * k][0], row))
            else:
                copy(parts[2 * k - 1 if t < half else 2 * k][t % half], row)


def weight_specs(weights, tn):
    width = weights[0].shape[-1]
    shard = weights[0].shape[-2]
    if len(weights) == 2:
        fs = weights[0].shape[0]
        return [pl.BlockSpec((fs, 1, shard, width), lambda t, r: (0, t, 0, 0))] * 2
    half = tn // 2
    at = [lambda t, r: (t, 0, 0)]
    at += [lambda t, r: (jnp.minimum(t, half - 1), 0, 0), lambda t, r: (jnp.maximum(t - half, 0), 0, 0)] * 3
    return [pl.BlockSpec((1, shard, width), index) for index in at * 2]


def qkv_kernel(flag_ref, hid_ref, other_ref, vec_ref, cos_ref, sin_ref, *refs):
    q_ref, k_ref, v_ref, wo_ref, x_ref, w_ref = refs[-6:]
    rows, width = x_ref.shape[1:]

    @pl.when(pl.program_id(0) == 0)
    def _():
        for half, ref in enumerate((hid_ref, other_ref)):
            for m in range(2):
                n, _ = normalise(ref[m].astype(f32))
                x_ref[2 * half + m] = (n * vec_ref[m, 5:6, :] + vec_ref[m, 6:7, :]).astype(bf16)

    lane = lax.broadcasted_iota(jnp.int32, (rows, 128), 1)
    first = (lane & (HEAD_DIM - 1)) < HEAD_DIM // 2
    low = lane < HEAD_DIM
    lay_weight(flag_ref, pl.program_id(0), pl.num_programs(0), refs[:-6], w_ref, True)
    for j in range(3):
        hole = (j + 1) * PAD - HEAD_DIM
        wo_ref[0, :, j * HEAD_DIM : (j + 1) * HEAD_DIM] = w_ref[:, hole : hole + HEAD_DIM]
    wo_ref[0, :, PAD - HEAD_DIM :] = jnp.zeros((width, HEAD_DIM), bf16)

    def rotated(y, half, ch):
        z = y[:, 128 * ch : 128 * ch + 128]
        return z * cos_ref[half] + turn(z, first) * sin_ref[half]

    for b in range(4):
        x = x_ref[b]
        y = dot_nn(x, w_ref[:, PAD : 2 * PAD])
        k_ref[b, :, 0:128] = rotated(y, b // 2, 0).astype(bf16)
        k_ref[b, :, 128:PAD] = rotated(y, b // 2, 1).astype(bf16)
        v_ref[b] = dot_nn(x, w_ref[:, 2 * PAD : 3 * PAD]).astype(bf16)
        if b < 2:
            y = dot_nn(x, w_ref[:, 0:PAD])
            scale = HEAD_DIM ** (-0.5)
            q_ref[b, :, 0:128] = rotated(y, 0, 0).astype(bf16) * scale
            q_ref[b, :, 128:PAD] = jnp.where(low, rotated(y, 0, 1), 0.0).astype(bf16) * scale


def qkv_call(flags, tn, hid, other, vec, weights, cos, sin):
    _, rows, width = hid.shape
    blocks = 4
    out = lambda n: pl.BlockSpec((n, rows, PAD), lambda t, r: (0, 0, t))
    one = pl.Buffered(1)
    return pl.pallas_call(
        qkv_kernel,
        grid_spec=pltpu.PrefetchScalarGridSpec(
            num_scalar_prefetch=1,
            grid=(tn,),
            in_specs=[
                whole((2, rows, width), pipeline_mode=one),
                whole((2, rows, width), pipeline_mode=one),
                whole((2, 8, width), pipeline_mode=one),
                whole((2, rows, 128), pipeline_mode=one),
                whole((2, rows, 128), pipeline_mode=one),
                *weight_specs(weights, tn),
            ],
            out_specs=[
                out(2),
                out(blocks),
                out(blocks),
                pl.BlockSpec((1, width, PAD), lambda t, r: (t, 0, 0)),
                whole((blocks, rows, width), pipeline_mode=one),
            ],
            scratch_shapes=[pltpu.VMEM((width, 3 * PAD), bf16)],
        ),
        out_shape=[
            jax.ShapeDtypeStruct((2, rows, tn * PAD), bf16),
            jax.ShapeDtypeStruct((blocks, rows, tn * PAD), bf16),
            jax.ShapeDtypeStruct((blocks, rows, tn * PAD), bf16),
            jax.ShapeDtypeStruct((tn, width, PAD), bf16),
            jax.ShapeDtypeStruct((blocks, rows, width), bf16),
        ],
        compiler_params=params(LIMIT),
        cost_estimate=cost(2 * blocks * rows * width * 640 * tn, 16 * MIB),
        name="qkv_rope",
    )(flags, hid, other, vec, cos, sin, *weights)


def pack_kernel(qkv_ref, attn_ref, a_ref):
    heads_w = qkv_ref.shape[2]
    for j in range(3):
        a_ref[:, j * PAD : j * PAD + heads_w] = qkv_ref[j]
        a_ref[:, j * PAD + heads_w : (j + 1) * PAD] = attn_ref[j * HEAD_DIM : (j + 1) * HEAD_DIM, :].T


def pack_weights(qkv_weight, attn_weight):
    shard = qkv_weight.shape[1]
    if shard % 16:
        attn_t = attn_weight.T
        pieces = []
        for j in range(3):
            pieces += [qkv_weight[j], attn_t[:, j * HEAD_DIM : (j + 1) * HEAD_DIM]]
        return jnp.concatenate(pieces, axis=1)
    return pl.pallas_call(
        pack_kernel,
        out_shape=jax.ShapeDtypeStruct((shard, 3 * PAD), bf16),
        name="pack_weights",
    )(qkv_weight, attn_weight)


QB = 256
NEG = -1e30


def head_lanes(x, h):
    if h == 2:
        return x
    lane = lax.broadcasted_iota(jnp.int32, x.shape, 1)
    keep = (lane < HEAD_DIM) if h == 0 else (lane >= HEAD_DIM)
    return jnp.where(keep, x, jnp.zeros_like(x))


def in_terms(base, lane, at, x):
    hi = x.astype(bf16).astype(f32)
    rest = x - hi
    mid = rest.astype(bf16).astype(f32)
    out = jnp.where(lane == at + 1, mid, jnp.where(lane == at + 2, rest - mid, base))
    return jnp.where(lane == at, hi, out).astype(bf16)


def attn_fwd_kernel(q_ref, k_ref, v_ref, sq_ref, sk_ref, o_ref, lo_ref, x_ref):
    rows = q_ref.shape[1]
    keys = 2 * rows
    cols_k = sk_ref[0]
    ones = jnp.ones((keys, 128), bf16)
    part = lambda ref, c: ref[..., 128 * c : 128 * c + 128].reshape(keys, 128)
    kx = [jnp.concatenate([part(k_ref, c), cols_k], axis=1) for c in range(2)]
    vx = [jnp.concatenate([part(v_ref, c), ones], axis=1) for c in range(2)]
    lane = lax.broadcasted_iota(jnp.int32, (QB, 128), 1)
    low = lane < HEAD_DIM
    for qb in range(rows // QB):
        span = pl.ds(qb * QB, QB)
        cols_q = sq_ref[0, span, :]
        outs = []
        for h in range(HEADS_PER_BLOCK):
            c = h // 2
            qh = head_lanes(q_ref[0, span, 128 * c : 128 * c + 128], h)
            s = dot_nt(jnp.concatenate([qh, cols_q], axis=1), kx[c])
            top = jnp.max(s, axis=1, keepdims=True)
            o = dot_nn(jnp.exp(s - top).astype(bf16), vx[c])
            total = o[:, 128:]
            outs.append(o[:, :128] / total)
            lse = top + jnp.log(total[:, 0:1])
            x_ref[0, 0, h, span, :] = in_terms(cols_q.astype(f32), lane, 128 - 3, -lse)
        for c, o in enumerate((jnp.where(low, outs[0], outs[1]), outs[2])):
            hi = o.astype(bf16)
            o_ref[0, span, 128 * c : 128 * c + 128] = hi
            lo_ref[0, span, 128 * c : 128 * c + 128] = (o - hi.astype(f32)).astype(bf16)


def attn_fwd_call(q, k, v, cols_q, cols_k):
    _, rows, wide = q.shape
    tn = wide // PAD
    k4 = k.reshape(2, 2, rows, wide)
    v4 = v.reshape(2, 2, rows, wide)
    mine = pl.BlockSpec((1, rows, PAD), lambda m, t: (m, 0, t))
    all_keys = pl.BlockSpec((2, 1, rows, PAD), lambda m, t: (0, m, 0, t))
    return pl.pallas_call(
        attn_fwd_kernel,
        grid=(2, tn),
        in_specs=[
            mine,
            all_keys,
            all_keys,
            pl.BlockSpec((1, rows, 128), lambda m, t: (m, 0, 0)),
            pl.BlockSpec((1, 2 * rows, 128), lambda m, t: (m, 0, 0)),
        ],
        out_specs=[
            mine,
            mine,
            pl.BlockSpec((1, 1, HEADS_PER_BLOCK, rows, 128), lambda m, t: (m, t, 0, 0, 0)),
        ],
        out_shape=[
            jax.ShapeDtypeStruct((2, rows, wide), bf16),
            jax.ShapeDtypeStruct((2, rows, wide), bf16),
            jax.ShapeDtypeStruct((2, tn, HEADS_PER_BLOCK, rows, 128), bf16),
        ],
        compiler_params=params(LIMIT, 2),
        cost_estimate=cost(
            2 * tn * 3 * 2 * 2 * rows * 2 * rows * 256, 18 * MIB, 2 * tn * 3 * rows * 2 * rows
        ),
        name="attn_fwd",
    )(q, k4, v4, cols_q, cols_k)


def attn_bwd_kernel(
    tl_ref,
    q_ref,
    k_ref,
    v_ref,
    g_ref,
    o_ref,
    lo_ref,
    x_ref,
    sk_ref,
    cos_ref,
    sin_ref,
    norm_ref,
    wat_ref,
    dq_ref,
    own_ref,
    oth_ref,
    proj_ref,
    acc_ref,
):
    rows = q_ref.shape[1]
    keys = 2 * rows
    cols_k = sk_ref[0]
    lane = lax.broadcasted_iota(jnp.int32, (QB, 128), 1)
    low = lane < HEAD_DIM
    key_lane = lax.broadcasted_iota(jnp.int32, (keys, 128), 1)
    terms = jnp.where(key_lane < 3, 1.0, 0.0).astype(bf16)

    def unrotated(y, lanes, cos, sin):
        return y * cos - turn(y, (lanes & (HEAD_DIM - 1)) < HEAD_DIM // 2) * sin

    for c in range(2):
        ch = slice(128 * c, 128 * c + 128)
        kc = k_ref[..., ch].reshape(keys, 128)
        kt = kc.T
        kx = jnp.concatenate([kc, cols_k], axis=1)
        vx = jnp.concatenate([v_ref[..., ch].reshape(keys, 128), terms], axis=1)
        dk = jnp.zeros((keys, 128), f32)
        dv = jnp.zeros((keys, 128), f32)
        for qb in range(rows // QB):
            span = pl.ds(qb * QB, QB)
            qc = q_ref[0, span, ch]
            gc = g_ref[0, span, ch]
            prod = gc.astype(f32) * (o_ref[0, span, ch].astype(f32) + lo_ref[0, span, ch].astype(f32))
            dqs = []
            for h in (0, 1) if c == 0 else (2,):
                qh = head_lanes(qc, h)
                gh = head_lanes(gc, h)
                inner = jnp.sum(head_lanes(prod, h), axis=1, keepdims=True)
                gx = in_terms(jnp.zeros((QB, 128), f32), lane, 0, -inner)
                p = jnp.exp(dot_nt(kx, jnp.concatenate([qh, x_ref[0, 0, h, span, :]], axis=1)))
                ds = (p * dot_nt(vx, jnp.concatenate([gh, gx], axis=1))).astype(bf16)
                dv += dot_nn(p.astype(bf16), gh)
                dk += dot_nn(ds, qh)
                dqs.append(dot_nn(kt, ds).T * HEAD_DIM ** (-0.5))
            dq = jnp.where(low, dqs[0], dqs[1] if c == 0 else 0.0)
            dq_ref[0, 0, span, ch] = unrotated(dq, lane, cos_ref[span, :], sin_ref[span, :]).astype(bf16)
        dk = unrotated(dk, key_lane, cos_ref[...], sin_ref[...])
        for half, ref in enumerate((own_ref, oth_ref)):
            some = slice(half * rows, (half + 1) * rows)
            ref[0, 0, 0, :, ch] = dk[some].astype(bf16)
            ref[0, 1, 0, :, ch] = dv[some].astype(bf16)

    slot, m = pl.program_id(0), pl.program_id(1)
    for j in range(3):

        @pl.when(slot == 0)
        def _():
            cols = slice(j * PAD, (j + 1) * PAD)
            if j == 0:
                part = dot_tn(norm_ref[0, 0], dq_ref[0, 0])
            else:
                part = dot_tn(norm_ref[0, 0], own_ref[0, j - 1, 0])
                part += dot_tn(norm_ref[1, 0], oth_ref[0, j - 1, 0])

            @pl.when(m == 0)
            def _():
                acc_ref[:, cols] = part

            @pl.when(m == 1)
            def _():
                edge = (j + 1) * PAD - HEAD_DIM
                total = acc_ref[:, cols] + part
                proj_ref[:, j * PAD : edge] = total[:, : PAD - HEAD_DIM].astype(bf16)
                proj_ref[:, edge : edge + HEAD_DIM] = wat_ref[:, j * HEAD_DIM : (j + 1) * HEAD_DIM]


def attn_bwd_call(tlist, g, q, k, v, o, lo, x, cols_k, cos, sin, normed, wat):
    _, rows, wide = q.shape
    width = normed.shape[-1]
    one = pl.Buffered(1)
    nt = tlist.shape[0]
    k4 = k.reshape(2, 2, rows, wide)
    v4 = v.reshape(2, 2, rows, wide)
    mine = pl.BlockSpec((1, rows, PAD), lambda i, m, tl: (m, 0, tl[i]))
    all_keys = pl.BlockSpec((2, 1, rows, PAD), lambda i, m, tl: (0, m, 0, tl[i]))
    kv_out = pl.BlockSpec((1, 2, 1, rows, PAD), lambda i, m, tl: (i, 0, m, 0, 0))
    return pl.pallas_call(
        attn_bwd_kernel,
        grid_spec=pltpu.PrefetchScalarGridSpec(
            num_scalar_prefetch=1,
            grid=(nt, 2),
            in_specs=[
                mine,
                all_keys,
                all_keys,
                mine,
                mine,
                mine,
                pl.BlockSpec(
                    (1, 1, HEADS_PER_BLOCK, rows, 128), lambda i, m, tl: (m, tl[i], 0, 0, 0)
                ),
                pl.BlockSpec((1, 2 * rows, 128), lambda i, m, tl: (m, 0, 0)),
                whole((2 * rows, 128), pipeline_mode=one),
                whole((2 * rows, 128), pipeline_mode=one),
                pl.BlockSpec(
                    (2, 1, rows, width), lambda i, m, tl: (0, jnp.where(i == 0, m, 1), 0, 0)
                ),
                whole((width, PAD), pipeline_mode=one),
            ],
            out_specs=[
                pl.BlockSpec((1, 1, rows, PAD), lambda i, m, tl: (i, m, 0, 0)),
                kv_out,
                kv_out,
                whole((width, 3 * PAD), pipeline_mode=one),
            ],
            scratch_shapes=[pltpu.VMEM((width, 3 * PAD), f32)],
        ),
        out_shape=[
            jax.ShapeDtypeStruct((nt, 2, rows, PAD), bf16),
            jax.ShapeDtypeStruct((nt, 2, 2, rows, PAD), bf16),
            jax.ShapeDtypeStruct((nt, 2, 2, rows, PAD), bf16),
            jax.ShapeDtypeStruct((width, 3 * PAD), bf16),
        ],
        compiler_params=params(LIMIT, 2),
        cost_estimate=cost(
            2 * nt * 3 * 5 * 2 * rows * 2 * rows * 256, 5 * nt * MIB, 2 * nt * 3 * rows * 2 * rows
        ),
        name="attn_bwd",
    )(
        tlist,
        q,
        k4,
        v4,
        g,
        o,
        lo,
        x,
        cols_k,
        cos.reshape(2 * rows, 128),
        sin.reshape(2 * rows, 128),
        normed.reshape(2, 2, rows, width),
        wat,
    )


RB = 512
LAST_RB = 256


def dot_tn(a, b):
    return lax.dot_general(a, b, (((0,), (0,)), ((), ())), preferred_element_type=f32)


def normalise(h):
    mean = jnp.mean(h, axis=-1, keepdims=True)
    cent = h - mean
    var = jnp.mean(cent * cent, axis=-1, keepdims=True)
    rstd = lax.rsqrt(var + NORM_EPS)
    return cent * rstd, rstd


def block_kernel(
    flag_ref,
    mix_ref,
    wout_ref,
    hid_ref,
    vec_ref,
    cot_ref,
    mask_ref,
    ub_ref,
    ff_ref,
    out_ref,
    dh_ref,
    mg_ref,
    sum_ref,
    wff_ref,
    wat_ref,
    up_ref,
    dn_ref,
    x_ref,
    g_ref,
    bl_ref,
    mine_ref,
    act_ref,
    ul_ref,
    acts_ref,
    uls_ref,
    h1_ref,
    br_ref,
    d_ref,
    n_ref,
    sem,
):
    step = pl.program_id(0)
    steps = pl.num_programs(0)
    own = flag_ref[0]
    width = hid_ref.shape[1]
    tn = ff_ref.shape[0]
    ff = ub_ref.shape[2]
    here = pl.ds(pl.multiple_of(step * RB, RB), RB)

    def fetch(j):
        cols = pl.ds(pl.multiple_of(j * ff, ff), ff)
        return (
            pltpu.make_async_copy(ff_ref.at[j, :, 0:ff], up_ref.at[:, cols], sem.at[2 * j]),
            pltpu.make_async_copy(ff_ref.at[j, :, ff : 2 * ff], dn_ref.at[:, cols], sem.at[2 * j + 1]),
        )

    @pl.when(step == 0)
    def _():
        for j in range(tn):
            for copy in fetch(j):
                copy.start()

    gate1, gain2, shift2 = vec_ref[0, 0:1, :], vec_ref[0, 1:2, :], vec_ref[0, 2:3, :]
    gate2, dbias = vec_ref[0, 3:4, :], vec_ref[0, 4:5, :]
    acc = dot_nt(mix_ref[:, 0:PAD], wout_ref[0])
    for t in range(1, tn):
        acc += dot_nt(mix_ref[:, t * PAD : (t + 1) * PAD], wout_ref[t])
    br_ref[...] = acc
    h1 = hid_ref[...].astype(f32) + gate1 * acc
    h1_ref[...] = h1
    n, _ = normalise(h1)
    x = (n * gain2 + shift2).astype(bf16)
    x_ref[here, :] = x
    cot = cot_ref[...].astype(f32) * mask_ref[...]
    g = (cot * gate2).astype(bf16)
    g_ref[here, :] = g
    mine_ref[here, :] = mix_ref[:, pl.ds(pl.multiple_of(own * PAD, PAD), PAD)]

    def units(j, carry):
        @pl.when(step == 0)
        def _():
            for copy in fetch(j):
                copy.wait()

        cols = pl.ds(pl.multiple_of(j * ff, ff), ff)
        u = dot_nn(x_ref[here, :], up_ref[:, cols]) + ub_ref[lax.rem(own - j + tn, tn)]
        da = dot_nn(g_ref[here, :], dn_ref[:, cols])
        u2 = u * u
        th = jnp.tanh(GELU_C * u * (1.0 + 0.044715 * u2))
        half_up = 0.5 * (1.0 + th)
        slope = half_up + (0.5 * GELU_C) * u * (1.0 - th * th) * (1.0 + (3 * 0.044715) * u2)
        acts_ref[:, cols] = (u * half_up).astype(bf16)
        uls_ref[:, cols] = (da * slope).astype(bf16)
        return carry

    lax.fori_loop(0, tn, units, 0)
    mine = pl.ds(pl.multiple_of(own * ff, ff), ff)
    act_ref[here, :] = acts_ref[:, mine]
    ul_ref[here, :] = uls_ref[:, mine]
    for c in range(0, width, PAD):
        cols = slice(c, c + PAD)
        d_ref[:, cols] = dot_nt(acts_ref[...], dn_ref[cols, :])
        n_ref[:, cols] = dot_nt(uls_ref[...], up_ref[cols, :])

    down = d_ref[...] + dbias
    h1 = h1_ref[...]
    out_ref[...] = (h1 + gate2 * down).astype(bf16)
    n, rstd = normalise(h1)
    grad = n_ref[...]
    gn = grad * n
    e = grad * gain2
    en = gn * gain2
    dh = cot + rstd * (
        e - jnp.mean(e, axis=-1, keepdims=True) - n * jnp.mean(en, axis=-1, keepdims=True)
    )
    dh_ref[...] = dh
    bl = (dh * gate1).astype(bf16)
    bl_ref[here, :] = bl
    for t in range(tn):
        mg_ref[:, t * PAD : (t + 1) * PAD] = dot_nn(bl, wout_ref[t]).astype(bf16)

    @pl.when(lax.rem(step, steps // 2) == 0)
    def _():
        sum_ref[...] = jnp.zeros_like(sum_ref)

    parts = (cot * down, cot, grad, gn, dh * br_ref[...], uls_ref[:, mine].astype(f32))
    for r, part in enumerate(parts):
        sum_ref[0, r : r + 1, :] += jnp.sum(part, axis=0, keepdims=True)

    @pl.when(step == steps - 1)
    def _():
        def column(c, carry):
            cols = pl.ds(pl.multiple_of(c * PAD, PAD), PAD)
            wff_ref[:, cols] = dot_tn(x_ref[...], ul_ref[:, cols])
            far = pl.ds(pl.multiple_of(ff + c * PAD, PAD), PAD)
            wff_ref[:, far] = dot_tn(g_ref[...], act_ref[:, cols])
            return carry

        lax.fori_loop(0, ff // PAD, column, 0)
        wat_ref[...] = dot_tn(bl_ref[...], mine_ref[...]).astype(bf16)


def block_call(flags, mixed, w_out, hid, vec, cot, mask_col, w_ff, up_bias):
    rows, wide = mixed.shape
    width = hid.shape[1]
    tn, _, ff = w_ff.shape
    ff = ff // 2
    one = pl.Buffered(1)
    steps = rows // RB
    row = lambda w: pl.BlockSpec((RB, w), lambda i, o: (i, 0))
    vecs = pl.BlockSpec((1, 8, width), lambda i, o: (i // (steps // 2), 0, 0))
    tokens = lambda dtype, w, n=rows: pltpu.VMEM((n, w), dtype)
    return pl.pallas_call(
        block_kernel,
        grid_spec=pltpu.PrefetchScalarGridSpec(
            num_scalar_prefetch=1,
            grid=(steps,),
            in_specs=[
                row(wide),
                whole((tn, width, PAD), pipeline_mode=one),
                row(width),
                vecs,
                row(width),
                row(1),
                whole((tn, 1, ff), pipeline_mode=one),
                pl.BlockSpec(memory_space=pl.ANY),
            ],
            out_specs=[
                row(width),
                row(width),
                row(wide),
                vecs,
                whole((width, 2 * ff), pipeline_mode=one),
                whole((width, PAD), pipeline_mode=one),
            ],
            scratch_shapes=[
                tokens(bf16, tn * ff, width),
                tokens(bf16, tn * ff, width),
                tokens(bf16, width),
                tokens(bf16, width),
                tokens(bf16, width),
                tokens(bf16, PAD),
                tokens(bf16, ff),
                tokens(bf16, ff),
                tokens(bf16, tn * ff, RB),
                tokens(bf16, tn * ff, RB),
                tokens(f32, width, RB),
                tokens(f32, width, RB),
                tokens(f32, width, RB),
                tokens(f32, width, RB),
                pltpu.SemaphoreType.DMA((2 * tn,)),
            ],
        ),
        out_shape=[
            jax.ShapeDtypeStruct((rows, width), bf16),
            jax.ShapeDtypeStruct((rows, width), f32),
            jax.ShapeDtypeStruct((rows, wide), bf16),
            jax.ShapeDtypeStruct((2, 8, width), f32),
            jax.ShapeDtypeStruct((width, 2 * ff), f32),
            jax.ShapeDtypeStruct((width, PAD), bf16),
        ],
        compiler_params=params(LIMIT),
        cost_estimate=cost(
            4 * 2 * rows * width * ff * tn + 8 * rows * width * width, 32 * MIB, rows * ff * tn
        ),
        name="block_both",
    )(flags, mixed, w_out, hid, vec, cot, mask_col, up_bias, w_ff)


def table_kernel(flag_ref, seg_ref, cos_ref, sin_ref, sq_ref, sk_ref):
    rows = seg_ref.shape[3]
    lane = lax.broadcasted_iota(jnp.int32, (rows, 128), 1)
    fixed = lane >= 128 - 3
    pair = (lane & (HEAD_DIM // 2 - 1)).astype(f32)
    freq = jnp.exp(pair * (-2.0 * math.log(10000.0) / HEAD_DIM))
    sign = jnp.where((lane & (HEAD_DIM - 1)) < HEAD_DIM // 2, -1.0, 1.0)
    row = lax.broadcasted_iota(jnp.int32, (rows, 128), 0)
    for half in range(2):
        angle = (row + flag_ref[half]).astype(f32) * freq
        cos_ref[half] = jnp.cos(angle)
        sin_ref[half] = jnp.sin(angle) * sign
        for m in range(2):
            ids = jnp.broadcast_to(seg_ref[m, half].astype(f32), (128, rows)).T
            same = (ids == lane.astype(f32)) | fixed
            sk_ref[m, half] = jnp.where(same, 1.0, 0.0).astype(bf16)
            if half == 0:
                sq_ref[m] = jnp.where(same, 0.0, NEG).astype(bf16)


def table_call(starts, segments):
    _, _, _, rows = segments.shape
    cos, sin, cols_q, cols_k = pl.pallas_call(
        table_kernel,
        grid_spec=pltpu.PrefetchScalarGridSpec(
            num_scalar_prefetch=1,
            grid=(1,),
            in_specs=[whole(segments.shape)],
            out_specs=[
                whole((2, rows, 128)),
                whole((2, rows, 128)),
                whole((2, rows, 128)),
                whole((2, 2, rows, 128)),
            ],
        ),
        out_shape=[
            jax.ShapeDtypeStruct((2, rows, 128), f32),
            jax.ShapeDtypeStruct((2, rows, 128), f32),
            jax.ShapeDtypeStruct((2, rows, 128), bf16),
            jax.ShapeDtypeStruct((2, 2, rows, 128), bf16),
        ],
        compiler_params=params(LIMIT),
        cost_estimate=cost(100 * 2 * rows * 128, 3 * MIB),
        name="tables",
    )(starts, segments)
    return cos, sin, cols_q, cols_k.reshape(2, 2 * rows, 128)


def last_kernel(
    flag_ref,
    dq_ref,
    kv_ref,
    rv_ref,
    hid_ref,
    dh_ref,
    vec_ref,
    early_ref,
    *refs,
):
    out_ref, sum_ref, w_ref, d_ref, acc_ref = refs[-5:]
    first = pl.program_id(1) == 0
    own = flag_ref[0]
    tn = dq_ref.shape[0]

    @pl.when(first & (pl.program_id(0) == 0))
    def _():
        for t in range(tn):
            cols = pl.ds(3 * PAD * t, 3 * PAD)
            lay_weight(flag_ref, t, tn, refs[:-5], w_ref.at[:, cols], False)

    for t in range(tn):
        slot = lax.rem(t - own + tn, tn)
        at = 3 * PAD * t
        d_ref[:, at : at + PAD] = dq_ref[slot, 0]
        for j in range(2):
            at += PAD
            d = kv_ref[slot, j, 0].astype(f32) + rv_ref[slot, j, 0].astype(f32)
            d_ref[:, at : at + PAD] = d.astype(bf16)
    width = hid_ref.shape[2]
    for c in range(0, width, PAD):
        acc_ref[:, c : c + PAD] = dot_nt(d_ref[...], w_ref[c : c + PAD, :])
    acc = acc_ref[...]
    gain1 = vec_ref[0, 5:6, :]
    n, rstd = normalise(hid_ref[0].astype(f32))
    gn = acc * n
    e = acc * gain1
    en = gn * gain1
    out_ref[0] = dh_ref[0] + rstd * (
        e - jnp.mean(e, axis=-1, keepdims=True) - n * jnp.mean(en, axis=-1, keepdims=True)
    )

    @pl.when(first)
    def _():
        sum_ref[0, 0:2, :] = jnp.zeros((2, sum_ref.shape[2]), f32)
        sum_ref[0, 2:8, :] = early_ref[0, 0:6, :]

    sum_ref[0, 0:1, :] += jnp.sum(acc, axis=0, keepdims=True)
    sum_ref[0, 1:2, :] += jnp.sum(gn, axis=0, keepdims=True)


def last_call(flags, dq, kv, rv, weights, hid, dh, vec, early):
    _, rows, width = hid.shape
    tn = dq.shape[0]
    row = pl.BlockSpec((1, LAST_RB, width), lambda m, i, o: (m, i, 0))
    vecs = pl.BlockSpec((1, 8, width), lambda m, i, o: (m, 0, 0))
    q_spec = lambda n: pl.BlockSpec((n, 1, LAST_RB, PAD), lambda m, i, o: (0, m, i, 0))
    kv_spec = lambda n: pl.BlockSpec((n, 2, 1, LAST_RB, PAD), lambda m, i, o: (0, 0, m, i, 0))
    return pl.pallas_call(
        last_kernel,
        grid_spec=pltpu.PrefetchScalarGridSpec(
            num_scalar_prefetch=1,
            grid=(2, rows // LAST_RB),
            in_specs=[
                q_spec(tn),
                kv_spec(tn),
                kv_spec(tn),
                row,
                row,
                vecs,
                vecs,
                *[whole(w.shape, pipeline_mode=pl.Buffered(1)) for w in weights],
            ],
            out_specs=[row, vecs],
            scratch_shapes=[
                pltpu.VMEM((width, tn * 3 * PAD), bf16),
                pltpu.VMEM((LAST_RB, tn * 3 * PAD), bf16),
                pltpu.VMEM((LAST_RB, width), f32),
            ],
        ),
        out_shape=[
            jax.ShapeDtypeStruct((2, rows, width), f32),
            jax.ShapeDtypeStruct((2, 8, width), f32),
        ],
        compiler_params=params(LIMIT, 2),
        cost_estimate=cost(2 * 2 * rows * width * tn * 3 * PAD, 24 * MIB),
        name="first_norm_bwd",
    )(flags, dq, kv, rv, hid, dh, vec, early, *weights)


def split_terms(x):
    hi = x.astype(bf16)
    rest = x - hi.astype(f32)
    mid = rest.astype(bf16)
    return [hi, mid, (rest - mid.astype(f32)).astype(bf16)]


def finish_kernel(flag_ref, sums_ref, mod_ref, norm_ref, cond_ref, ada_ref, *refs):
    gada_ref, gadab_ref, gcond_ref, gn1_ref, gn2_ref, gdb_ref, gub_ref, all_ref = refs
    group, ada_cols, _ = ada_ref.shape
    width = sums_ref.shape[3]
    place = flag_ref[0]
    norm_one, norm_two = norm_ref[0:1, :], norm_ref[1:2, :]
    one = jnp.zeros((1, width), f32)
    small = [one, one, one, one]
    for f in range(group // 2):
        for m in range(2):
            s = 2 * f + m
            r = sums_ref[2 * f, m] + sums_ref[2 * f + 1, m]
            r = [r[i : i + 1, :] for i in range(8)]
            parts = (r[0], r[1] * norm_one, r[6], r[4], r[5] * norm_two, r[2])
            for i, part in enumerate(parts):
                all_ref[s : s + 1, i * width : (i + 1) * width] = part
            scale_one, scale_two, gate_two = (
                mod_ref[s : s + 1, i * width : (i + 1) * width] for i in (1, 4, 5)
            )
            terms = (r[1] * (1.0 + scale_one), r[5] * (1.0 + scale_two), r[3] * gate_two, r[7])
            small = [total + term for total, term in zip(small, terms)]

    def own_columns(x, count):
        total = x.shape[1]
        return pltpu.roll(x, lax.rem(total - place * count, total), 1)[:, :count]

    for ref, total in zip((gn1_ref, gn2_ref, gdb_ref, gub_ref), small):
        shard = ref.shape[0]
        ref[...] = own_columns(jnp.broadcast_to(total, (8, width)), shard)[0]
    mine = own_columns(all_ref[...], ada_cols)
    gadab_ref[...] = jnp.sum(mine, axis=0)
    cond = cond_ref[...]
    terms = split_terms(mine)
    gada_ref[...] = dot_tn(terms[0], cond) + dot_tn(terms[1], cond) + dot_tn(terms[2], cond)
    total = jnp.zeros((8, cond.shape[1]), f32)
    seqs = all_ref[pl.ds(pl.multiple_of(flag_ref[1] * 8, 8), 8), :]
    for term in split_terms(seqs):
        for c in range(group):
            total += dot_nn(term[:, c * ada_cols : (c + 1) * ada_cols], ada_ref[c])
    for i in range(4):

        @pl.when(flag_ref[2] == i)
        def _():
            gcond_ref[...] = total[2 * i : 2 * i + 2]


def finish_call(flags, sums, mod_all, norms, cond, ada):
    group, ada_cols, cond_w = ada.shape
    shard = sums.shape[3] // group
    out = [(ada_cols, cond_w), (ada_cols,), (2, cond_w)] + [(shard,)] * 4
    return pl.pallas_call(
        finish_kernel,
        grid_spec=pltpu.PrefetchScalarGridSpec(
            num_scalar_prefetch=1,
            grid=(1,),
            in_specs=[whole(x.shape) for x in (sums, mod_all, norms, cond, ada)],
            out_specs=[whole(x) for x in out],
            scratch_shapes=[pltpu.VMEM(mod_all.shape, f32)],
        ),
        out_shape=[jax.ShapeDtypeStruct(x, f32) for x in out],
        compiler_params=params(LIMIT),
        cost_estimate=cost(1 << 20, 3 * MIB),
        name="finish",
    )(flags, sums, mod_all, norms, cond, ada)


def spread(x, axes):
    count = lax.axis_size(axes)
    many = jnp.broadcast_to(x[None], (count,) + x.shape)
    return lax.all_to_all(many, axes, split_axis=0, concat_axis=0, tiled=True)


def join_cores(part, other, rank):
    fs, tn, rows, width = part.shape
    both = jnp.stack([jnp.where(rank == 0, part, other), jnp.where(rank == 0, other, part)], axis=1)
    return both.transpose(2, 0, 1, 3, 4).reshape(1, tn, fs * 2 * rows, width)


def gather_rows(row):
    tn = lax.axis_size("tp")
    got = [row]
    for step in range(1, tn):
        got.append(lax.ppermute(row, "tp", [(i, (i + step) % tn) for i in range(tn)]))
    return jnp.stack(got).astype(f32)


def exchange_to_shard(grad):
    group = lax.axis_size(FC)
    parts = grad.reshape(group, -1, grad.shape[1])
    return lax.all_to_all(parts, FC, split_axis=0, concat_axis=0, tiled=True)


def on_device(
    hidden_in,
    cond_vec,
    segment_ids,
    pad_mask,
    out_cot,
    qkv_weight,
    attn_weight,
    up_weight,
    up_bias,
    down_weight,
    down_bias,
    ada_weight,
    ada_bias,
    attn_norm,
    mlp_norm,
):
    rank = lax.axis_index("ctx")
    own = lax.axis_index("tp")
    fs = lax.axis_size("fsdp")
    tn = lax.axis_size("tp")
    hid = hidden_in[:, 0]
    _, rows, width = hid.shape
    shard = qkv_weight.shape[1]
    heads_w = qkv_weight.shape[2]
    cond_w = cond_vec.shape[2]
    highest = lax.Precision.HIGHEST

    w_attn_shard = pack_weights(qkv_weight, attn_weight)
    ada_cols = ada_bias.shape[0]
    extra = [cond_vec[:, 0]]
    up_rows = gather_rows(jnp.pad(up_bias, (0, cond_w - shard)).reshape(1, cond_w)).astype(bf16)
    for x in (down_bias, attn_norm, mlp_norm, up_rows.reshape(-1), ada_bias):
        extra.append(jnp.pad(x, (0, -x.shape[0] % cond_w)).reshape(-1, cond_w))
    extra = jnp.concatenate(extra, axis=0)
    ada_rows = jnp.concatenate([ada_weight.T, extra], axis=0)
    ada_rows = jnp.pad(ada_rows, ((0, -ada_rows.shape[0] % 16), (0, 0)))
    w_ff = jnp.concatenate([up_weight, down_weight.T], axis=1)
    w_ff = lax.all_gather(w_ff, ("tp",) + FC, axis=0, tiled=True).reshape(tn, width, -1)
    ada_rows = spread(ada_rows, FC)
    along = lax.all_gather(w_attn_shard, "tp", axis=0, tiled=False)
    in_parts = fs == 4 and tn % 2 == 0 and shard % 16 == 0
    if in_parts:
        lower, upper = along[: tn // 2], along[tn // 2 :]
        x_lower = lax.ppermute(lower, "fsdp", ALONG_X)
        y_upper = lax.ppermute(upper, "fsdp", ALONG_Y)
        x_upper = lax.ppermute(upper, "fsdp", ALONG_X)
        y_lower = lax.ppermute(lower, "fsdp", ALONG_Y)

    ada_full = ada_rows[:, :ada_cols]
    small = ada_rows[:, ada_cols:]
    cond_all = small[:, :2].reshape(fs, 2, 2, cond_w)[:, 0]
    modulation_all = jnp.einsum(
        "smk,fck->smfc", cond_all, ada_full, preferred_element_type=f32
    ).reshape(fs, 2, -1)
    small = small.astype(f32)
    dnb_full = small[:, 2, :shard].reshape(-1)
    norm_one = small[:, 3, :shard].reshape(-1)
    norm_two = small[:, 4, :shard].reshape(-1)
    upb_full = small[:, 5 : 5 + tn, :shard].transpose(1, 0, 2).reshape(tn, 1, -1)
    adab_full = small[:, 5 + tn :].reshape(2 * fs, -1)[:, :ada_cols].reshape(-1)
    modulation_all = modulation_all + adab_full
    modulation = lax.dynamic_index_in_dim(modulation_all, lax.axis_index("fsdp"), 0, keepdims=False)
    shift_one, scale_one, gate_one, shift_two, scale_two, gate_two = jnp.split(modulation, 6, axis=1)
    gain_one = norm_one * (1.0 + scale_one)
    gain_two = norm_two * (1.0 + scale_two)
    zero = jnp.zeros_like(gain_one)
    vec = jnp.stack(
        [
            gate_one,
            gain_two,
            shift_two,
            gate_two,
            jnp.broadcast_to(dnb_full, gain_one.shape),
            gain_one,
            shift_one,
            zero,
        ],
        axis=1,
    )

    hid_other = lax.ppermute(hid, "ctx", SWAP)
    seg = segment_ids[:, 0]
    halves = jnp.where(rank == 0, seg.reshape(2, 2, 1, rows), seg.reshape(2, 2, 1, rows)[:, ::-1])
    starts = jnp.stack([rank * rows, (1 - rank) * rows]).astype(jnp.int32)
    cos, sin, cols_q, cols_k = table_call(starts, halves)
    mask = lax.dynamic_slice_in_dim(pad_mask[:, 0], rank * rows, rows, axis=1).astype(f32)
    cot = out_cot[:, 0]

    if in_parts:
        d_lower = lax.ppermute(x_lower, "fsdp", ALONG_Y)
        d_upper = lax.ppermute(y_upper, "fsdp", ALONG_X)
        w_attn = [along, x_lower, x_upper, y_lower, y_upper, d_lower, d_upper]
        w_attn = w_attn + [lax.ppermute(part, "ctx", SWAP) for part in w_attn]
    else:
        w_own = spread(along, "fsdp")
        w_own = join_cores(w_own, lax.ppermute(w_own, "ctx", SWAP), rank)
        w_attn = [w_own[:, :, : width // 2], w_own[:, :, width // 2 :]]
    sources = lax.axis_index("fsdp") ^ jnp.arange(4, dtype=jnp.int32)
    flags = jnp.concatenate(
        [own.reshape(1), jnp.zeros((1,), jnp.int32), 2 * sources + rank, 2 * sources + 1 - rank]
    ).astype(jnp.int32)
    q, k, v, w_out, normed_all = qkv_call(flags, tn, hid, hid_other, vec, w_attn, cos, sin)
    mixed, mixed_lo, score_cols = attn_fwd_call(q, k, v, cols_q, cols_k)

    own_index = own.reshape(1).astype(jnp.int32)
    flat = lambda x: x.reshape(2 * rows, -1)
    block_out, dh_one, mixed_grad, sums_two, ff_low, attn_low = block_call(
        flags,
        flat(mixed),
        w_out,
        flat(hid),
        vec,
        flat(cot),
        mask.reshape(-1, 1),
        w_ff,
        upb_full,
    )
    mixed_grad = mixed_grad.reshape(2, rows, -1)
    ff_low, mixed_grad = lax.optimization_barrier((ff_low, mixed_grad))
    ff_shard = lax.psum_scatter(ff_low, FC, scatter_dimension=0, tiled=True)

    order = lax.rem(own + jnp.arange(tn, dtype=jnp.int32), tn).astype(jnp.int32)
    dq, kv_own, kv_send, proj_low = attn_bwd_call(
        order, mixed_grad, q, k, v, mixed, mixed_lo, score_cols, cols_k, cos, sin, normed_all, attn_low
    )

    kv_send, proj_low = lax.optimization_barrier((kv_send, proj_low))
    kv_got = lax.ppermute(kv_send, "ctx", SWAP)
    proj_got = exchange_to_shard(proj_low)

    hidden_grad, sums_one = last_call(
        flags, dq, kv_own, kv_got, w_attn, hid, dh_one.reshape(hid.shape), vec, sums_two
    )

    all_sums = lax.all_gather(sums_one, FC, axis=0, tiled=False)
    all_sums, proj_got, ff_shard = lax.optimization_barrier((all_sums, proj_got, ff_shard))
    seq = lax.axis_index("fsdp")
    finish_flags = jnp.stack([lax.axis_index(FC), seq // 4, seq % 4]).astype(jnp.int32)
    grads = finish_call(
        finish_flags,
        all_sums,
        modulation_all.reshape(2 * fs, -1),
        jnp.stack([norm_one, norm_two]),
        cond_all.reshape(2 * fs, cond_w),
        ada_full,
    )
    grad_ada, grad_adabias, cond_grad, attnnorm, mlpnorm, downbias, upbias = grads
    attn_shard = jnp.sum(proj_got.astype(f32), axis=0)

    grad_qkv = jnp.stack([attn_shard[:, j * PAD : j * PAD + heads_w] for j in range(3)])
    grad_attn = jnp.concatenate(
        [attn_shard[:, j * PAD + heads_w : (j + 1) * PAD] for j in range(3)], axis=1
    ).T
    return (
        block_out.reshape(hidden_in.shape),
        hidden_grad[:, None],
        cond_grad[:, None],
        grad_qkv,
        grad_attn,
        ff_shard[:, : ff_shard.shape[1] // 2],
        upbias,
        ff_shard[:, ff_shard.shape[1] // 2 :].T,
        downbias,
        grad_ada.T,
        grad_adabias,
        attnnorm,
        mlpnorm,
    )


def solution(mesh):
    tokens = P(None, "fsdp", "ctx", None)
    per_seq = P(None, "fsdp", None)
    weights = (
        P(None, FC, "tp"),
        P("tp", FC),
        P(FC, "tp"),
        P(("tp",) + FC),
        P("tp", FC),
        P(FC),
        P(None, FC),
        P(FC),
        P(FC),
        P(FC),
    )
    return jax.shard_map(
        on_device,
        mesh=mesh,
        in_specs=(tokens, per_seq, per_seq, per_seq, tokens) + weights,
        out_specs=(tokens, tokens, per_seq) + weights,
        check_vma=False,
    )
```

```python
import functools
import math

import jax
import jax.numpy as jnp
from jax import lax
from jax.experimental import pallas as pl
from jax.experimental.pallas import tpu as pltpu
from jax.sharding import PartitionSpec as P

HEAD_DIM = 64
HEADS_PER_BLOCK = 3
PAD = 256
NORM_EPS = 1e-05
GELU_C = math.sqrt(2.0 / math.pi)
bf16 = jnp.bfloat16
f32 = jnp.float32
FC = ("fsdp", "ctx")
SWAP = [(0, 1), (1, 0)]
ALONG_X = [(0, 1), (1, 0), (2, 3), (3, 2)]
ALONG_Y = [(0, 2), (2, 0), (1, 3), (3, 1)]
MIB = 1 << 20
LIMIT = 60


def dot_nn(a, b):
    return lax.dot_general(a, b, (((1,), (0,)), ((), ())), preferred_element_type=f32)


def dot_nt(a, b):
    return lax.dot_general(a, b, (((1,), (1,)), ((), ())), preferred_element_type=f32)


def params(limit, axes=1):
    return pltpu.CompilerParams(
        dimension_semantics=("arbitrary",) * axes, vmem_limit_bytes=limit * MIB
    )


def cost(flops, nbytes, trans=0):
    return pl.CostEstimate(flops=flops, bytes_accessed=nbytes, transcendentals=trans)


def whole(shape, **kw):
    return pl.BlockSpec(shape, lambda *_: (0,) * len(shape), **kw)


def turn(x, first):
    return jnp.where(first, pltpu.roll(x, 96, 1), pltpu.roll(x, 32, 1))


def interleave(rank, own_ref, oth_ref, out_ref, col):
    count, shard = own_ref.shape[0], own_ref.shape[2]
    cols = slice(col, col + out_ref.shape[1])
    for c in range(2):

        @pl.when(rank == c)
        def _():
            for f in range(count):
                at = 2 * f * shard
                mine, theirs = at + c * shard, at + (1 - c) * shard
                out_ref[mine : mine + shard, :] = own_ref[f, 0, :, cols]
                out_ref[theirs : theirs + shard, :] = oth_ref[f, 0, :, cols]


def lay_weight(flag_ref, t, tn, refs, out_ref, held):
    half = tn // 2
    if len(refs) == 2:
        own_ref, oth_ref = refs if held else [ref.at[:, t : t + 1] for ref in refs]
        interleave(flag_ref[1], own_ref, oth_ref, out_ref, 0)
        return
    shard = refs[0].shape[1]

    def copy(src, row):
        out_ref[pl.ds(pl.multiple_of(row * shard, shard), shard), :] = src

    for core in range(2):
        parts = refs[7 * core : 7 * core + 7]
        for k in range(4):
            row = flag_ref[2 + 4 * core + k]
            if k == 0:
                copy(parts[0][0 if held else t], row)
            elif held:
                pl.when(t < half)(lambda: copy(parts[2 * k - 1][0], row))
                pl.when(t >= half)(lambda: copy(parts[2 * k][0], row))
            else:
                copy(parts[2 * k - 1 if t < half else 2 * k][t % half], row)


def weight_specs(weights, tn):
    width = weights[0].shape[-1]
    shard = weights[0].shape[-2]
    if len(weights) == 2:
        fs = weights[0].shape[0]
        return [pl.BlockSpec((fs, 1, shard, width), lambda t, r: (0, t, 0, 0))] * 2
    half = tn // 2
    at = [lambda t, r: (t, 0, 0)]
    at += [lambda t, r: (jnp.minimum(t, half - 1), 0, 0), lambda t, r: (jnp.maximum(t - half, 0), 0, 0)] * 3
    return [pl.BlockSpec((1, shard, width), index) for index in at * 2]


def qkv_kernel(flag_ref, hid_ref, other_ref, vec_ref, cos_ref, sin_ref, *refs):
    q_ref, k_ref, v_ref, wo_ref, x_ref, w_ref = refs[-6:]
    rows, width = x_ref.shape[1:]

    @pl.when(pl.program_id(0) == 0)
    def _():
        for half, ref in enumerate((hid_ref, other_ref)):
            for m in range(2):
                n, _ = normalise(ref[m].astype(f32))
                x_ref[2 * half + m] = (n * vec_ref[m, 5:6, :] + vec_ref[m, 6:7, :]).astype(bf16)

    lane = lax.broadcasted_iota(jnp.int32, (rows, 128), 1)
    first = (lane & (HEAD_DIM - 1)) < HEAD_DIM // 2
    low = lane < HEAD_DIM
    lay_weight(flag_ref, pl.program_id(0), pl.num_programs(0), refs[:-6], w_ref, True)
    for j in range(3):
        hole = (j + 1) * PAD - HEAD_DIM
        wo_ref[0, :, j * HEAD_DIM : (j + 1) * HEAD_DIM] = w_ref[:, hole : hole + HEAD_DIM]
    wo_ref[0, :, PAD - HEAD_DIM :] = jnp.zeros((width, HEAD_DIM), bf16)

    def rotated(y, half, ch):
        z = y[:, 128 * ch : 128 * ch + 128]
        return z * cos_ref[half] + turn(z, first) * sin_ref[half]

    for b in range(4):
        x = x_ref[b]
        y = dot_nn(x, w_ref[:, PAD : 2 * PAD])
        k_ref[b, :, 0:128] = rotated(y, b // 2, 0).astype(bf16)
        k_ref[b, :, 128:PAD] = rotated(y, b // 2, 1).astype(bf16)
        v_ref[b] = dot_nn(x, w_ref[:, 2 * PAD : 3 * PAD]).astype(bf16)
        if b < 2:
            y = dot_nn(x, w_ref[:, 0:PAD])
            scale = HEAD_DIM ** (-0.5)
            q_ref[b, :, 0:128] = rotated(y, 0, 0).astype(bf16) * scale
            q_ref[b, :, 128:PAD] = jnp.where(low, rotated(y, 0, 1), 0.0).astype(bf16) * scale


def qkv_call(flags, tn, hid, other, vec, weights, cos, sin):
    _, rows, width = hid.shape
    blocks = 4
    out = lambda n: pl.BlockSpec((n, rows, PAD), lambda t, r: (0, 0, t))
    one = pl.Buffered(1)
    return pl.pallas_call(
        qkv_kernel,
        grid_spec=pltpu.PrefetchScalarGridSpec(
            num_scalar_prefetch=1,
            grid=(tn,),
            in_specs=[
                whole((2, rows, width), pipeline_mode=one),
                whole((2, rows, width), pipeline_mode=one),
                whole((2, 8, width), pipeline_mode=one),
                whole((2, rows, 128), pipeline_mode=one),
                whole((2, rows, 128), pipeline_mode=one),
                *weight_specs(weights, tn),
            ],
            out_specs=[
                out(2),
                out(blocks),
                out(blocks),
                pl.BlockSpec((1, width, PAD), lambda t, r: (t, 0, 0)),
                whole((blocks, rows, width), pipeline_mode=one),
            ],
            scratch_shapes=[pltpu.VMEM((width, 3 * PAD), bf16)],
        ),
        out_shape=[
            jax.ShapeDtypeStruct((2, rows, tn * PAD), bf16),
            jax.ShapeDtypeStruct((blocks, rows, tn * PAD), bf16),
            jax.ShapeDtypeStruct((blocks, rows, tn * PAD), bf16),
            jax.ShapeDtypeStruct((tn, width, PAD), bf16),
            jax.ShapeDtypeStruct((blocks, rows, width), bf16),
        ],
        compiler_params=params(LIMIT),
        cost_estimate=cost(2 * blocks * rows * width * 640 * tn, 16 * MIB),
        name="qkv_rope",
    )(flags, hid, other, vec, cos, sin, *weights)


def pack_kernel(qkv_ref, attn_ref, a_ref):
    heads_w = qkv_ref.shape[2]
    for j in range(3):
        a_ref[:, j * PAD : j * PAD + heads_w] = qkv_ref[j]
        a_ref[:, j * PAD + heads_w : (j + 1) * PAD] = attn_ref[j * HEAD_DIM : (j + 1) * HEAD_DIM, :].T


def pack_weights(qkv_weight, attn_weight):
    shard = qkv_weight.shape[1]
    if shard % 16:
        attn_t = attn_weight.T
        pieces = []
        for j in range(3):
            pieces += [qkv_weight[j], attn_t[:, j * HEAD_DIM : (j + 1) * HEAD_DIM]]
        return jnp.concatenate(pieces, axis=1)
    return pl.pallas_call(
        pack_kernel,
        out_shape=jax.ShapeDtypeStruct((shard, 3 * PAD), bf16),
        name="pack_weights",
    )(qkv_weight, attn_weight)


QB = 256
NEG = -1e30


def head_lanes(x, h):
    if h == 2:
        return x
    lane = lax.broadcasted_iota(jnp.int32, x.shape, 1)
    keep = (lane < HEAD_DIM) if h == 0 else (lane >= HEAD_DIM)
    return jnp.where(keep, x, jnp.zeros_like(x))


def in_terms(base, lane, at, x):
    hi = x.astype(bf16).astype(f32)
    rest = x - hi
    mid = rest.astype(bf16).astype(f32)
    out = jnp.where(lane == at + 1, mid, jnp.where(lane == at + 2, rest - mid, base))
    return jnp.where(lane == at, hi, out).astype(bf16)


def attn_fwd_kernel(q_ref, k_ref, v_ref, sq_ref, sk_ref, o_ref, lo_ref, x_ref):
    rows = q_ref.shape[1]
    keys = 2 * rows
    cols_k = sk_ref[0]
    ones = jnp.ones((keys, 128), bf16)
    part = lambda ref, c: ref[..., 128 * c : 128 * c + 128].reshape(keys, 128)
    kx = [jnp.concatenate([part(k_ref, c), cols_k], axis=1) for c in range(2)]
    vx = [jnp.concatenate([part(v_ref, c), ones], axis=1) for c in range(2)]
    lane = lax.broadcasted_iota(jnp.int32, (QB, 128), 1)
    low = lane < HEAD_DIM
    for qb in range(rows // QB):
        span = pl.ds(qb * QB, QB)
        cols_q = sq_ref[0, span, :]
        outs = []
        for h in range(HEADS_PER_BLOCK):
            c = h // 2
            qh = head_lanes(q_ref[0, span, 128 * c : 128 * c + 128], h)
            s = dot_nt(jnp.concatenate([qh, cols_q], axis=1), kx[c])
            top = jnp.max(s, axis=1, keepdims=True)
            o = dot_nn(jnp.exp(s - top).astype(bf16), vx[c])
            total = o[:, 128:]
            outs.append(o[:, :128] / total)
            lse = top + jnp.log(total[:, 0:1])
            x_ref[0, 0, h, span, :] = in_terms(cols_q.astype(f32), lane, 128 - 3, -lse)
        for c, o in enumerate((jnp.where(low, outs[0], outs[1]), outs[2])):
            hi = o.astype(bf16)
            o_ref[0, span, 128 * c : 128 * c + 128] = hi
            lo_ref[0, span, 128 * c : 128 * c + 128] = (o - hi.astype(f32)).astype(bf16)


def attn_fwd_call(q, k, v, cols_q, cols_k):
    _, rows, wide = q.shape
    tn = wide // PAD
    k4 = k.reshape(2, 2, rows, wide)
    v4 = v.reshape(2, 2, rows, wide)
    mine = pl.BlockSpec((1, rows, PAD), lambda m, t: (m, 0, t))
    all_keys = pl.BlockSpec((2, 1, rows, PAD), lambda m, t: (0, m, 0, t))
    return pl.pallas_call(
        attn_fwd_kernel,
        grid=(2, tn),
        in_specs=[
            mine,
            all_keys,
            all_keys,
            pl.BlockSpec((1, rows, 128), lambda m, t: (m, 0, 0)),
            pl.BlockSpec((1, 2 * rows, 128), lambda m, t: (m, 0, 0)),
        ],
        out_specs=[
            mine,
            mine,
            pl.BlockSpec((1, 1, HEADS_PER_BLOCK, rows, 128), lambda m, t: (m, t, 0, 0, 0)),
        ],
        out_shape=[
            jax.ShapeDtypeStruct((2, rows, wide), bf16),
            jax.ShapeDtypeStruct((2, rows, wide), bf16),
            jax.ShapeDtypeStruct((2, tn, HEADS_PER_BLOCK, rows, 128), bf16),
        ],
        compiler_params=params(LIMIT, 2),
        cost_estimate=cost(
            2 * tn * 3 * 2 * 2 * rows * 2 * rows * 256, 18 * MIB, 2 * tn * 3 * rows * 2 * rows
        ),
        name="attn_fwd",
    )(q, k4, v4, cols_q, cols_k)


def attn_bwd_kernel(
    tl_ref,
    q_ref,
    k_ref,
    v_ref,
    g_ref,
    o_ref,
    lo_ref,
    x_ref,
    sk_ref,
    cos_ref,
    sin_ref,
    norm_ref,
    wat_ref,
    dq_ref,
    own_ref,
    oth_ref,
    proj_ref,
    acc_ref,
):
    rows = q_ref.shape[1]
    keys = 2 * rows
    cols_k = sk_ref[0]
    lane = lax.broadcasted_iota(jnp.int32, (QB, 128), 1)
    low = lane < HEAD_DIM
    key_lane = lax.broadcasted_iota(jnp.int32, (keys, 128), 1)
    terms = jnp.where(key_lane < 3, 1.0, 0.0).astype(bf16)

    def unrotated(y, lanes, cos, sin):
        return y * cos - turn(y, (lanes & (HEAD_DIM - 1)) < HEAD_DIM // 2) * sin

    for c in range(2):
        ch = slice(128 * c, 128 * c + 128)
        kc = k_ref[..., ch].reshape(keys, 128)
        kt = kc.T
        kx = jnp.concatenate([kc, cols_k], axis=1)
        vx = jnp.concatenate([v_ref[..., ch].reshape(keys, 128), terms], axis=1)
        dk = jnp.zeros((keys, 128), f32)
        dv = jnp.zeros((keys, 128), f32)
        for qb in range(rows // QB):
            span = pl.ds(qb * QB, QB)
            qc = q_ref[0, span, ch]
            gc = g_ref[0, span, ch]
            prod = gc.astype(f32) * (o_ref[0, span, ch].astype(f32) + lo_ref[0, span, ch].astype(f32))
            dqs = []
            for h in (0, 1) if c == 0 else (2,):
                qh = head_lanes(qc, h)
                gh = head_lanes(gc, h)
                inner = jnp.sum(head_lanes(prod, h), axis=1, keepdims=True)
                gx = in_terms(jnp.zeros((QB, 128), f32), lane, 0, -inner)
                p = jnp.exp(dot_nt(kx, jnp.concatenate([qh, x_ref[0, 0, h, span, :]], axis=1)))
                ds = (p * dot_nt(vx, jnp.concatenate([gh, gx], axis=1))).astype(bf16)
                dv += dot_nn(p.astype(bf16), gh)
                dk += dot_nn(ds, qh)
                dqs.append(dot_nn(kt, ds).T * HEAD_DIM ** (-0.5))
            dq = jnp.where(low, dqs[0], dqs[1] if c == 0 else 0.0)
            dq_ref[0, 0, span, ch] = unrotated(dq, lane, cos_ref[span, :], sin_ref[span, :]).astype(bf16)
        dk = unrotated(dk, key_lane, cos_ref[...], sin_ref[...])
        for half, ref in enumerate((own_ref, oth_ref)):
            some = slice(half * rows, (half + 1) * rows)
            ref[0, 0, 0, :, ch] = dk[some].astype(bf16)
            ref[0, 1, 0, :, ch] = dv[some].astype(bf16)

    slot, m = pl.program_id(0), pl.program_id(1)
    for j in range(3):

        @pl.when(slot == 0)
        def _():
            cols = slice(j * PAD, (j + 1) * PAD)
            if j == 0:
                part = dot_tn(norm_ref[0, 0], dq_ref[0, 0])
            else:
                part = dot_tn(norm_ref[0, 0], own_ref[0, j - 1, 0])
                part += dot_tn(norm_ref[1, 0], oth_ref[0, j - 1, 0])

            @pl.when(m == 0)
            def _():
                acc_ref[:, cols] = part

            @pl.when(m == 1)
            def _():
                edge = (j + 1) * PAD - HEAD_DIM
                total = acc_ref[:, cols] + part
                proj_ref[:, j * PAD : edge] = total[:, : PAD - HEAD_DIM].astype(bf16)
                proj_ref[:, edge : edge + HEAD_DIM] = wat_ref[:, j * HEAD_DIM : (j + 1) * HEAD_DIM]


def attn_bwd_call(tlist, g, q, k, v, o, lo, x, cols_k, cos, sin, normed, wat):
    _, rows, wide = q.shape
    width = normed.shape[-1]
    one = pl.Buffered(1)
    nt = tlist.shape[0]
    k4 = k.reshape(2, 2, rows, wide)
    v4 = v.reshape(2, 2, rows, wide)
    mine = pl.BlockSpec((1, rows, PAD), lambda i, m, tl: (m, 0, tl[i]))
    all_keys = pl.BlockSpec((2, 1, rows, PAD), lambda i, m, tl: (0, m, 0, tl[i]))
    kv_out = pl.BlockSpec((1, 2, 1, rows, PAD), lambda i, m, tl: (i, 0, m, 0, 0))
    return pl.pallas_call(
        attn_bwd_kernel,
        grid_spec=pltpu.PrefetchScalarGridSpec(
            num_scalar_prefetch=1,
            grid=(nt, 2),
            in_specs=[
                mine,
                all_keys,
                all_keys,
                mine,
                mine,
                mine,
                pl.BlockSpec(
                    (1, 1, HEADS_PER_BLOCK, rows, 128), lambda i, m, tl: (m, tl[i], 0, 0, 0)
                ),
                pl.BlockSpec((1, 2 * rows, 128), lambda i, m, tl: (m, 0, 0)),
                whole((2 * rows, 128), pipeline_mode=one),
                whole((2 * rows, 128), pipeline_mode=one),
                pl.BlockSpec(
                    (2, 1, rows, width), lambda i, m, tl: (0, jnp.where(i == 0, m, 1), 0, 0)
                ),
                whole((width, PAD), pipeline_mode=one),
            ],
            out_specs=[
                pl.BlockSpec((1, 1, rows, PAD), lambda i, m, tl: (i, m, 0, 0)),
                kv_out,
                kv_out,
                whole((width, 3 * PAD), pipeline_mode=one),
            ],
            scratch_shapes=[pltpu.VMEM((width, 3 * PAD), f32)],
        ),
        out_shape=[
            jax.ShapeDtypeStruct((nt, 2, rows, PAD), bf16),
            jax.ShapeDtypeStruct((nt, 2, 2, rows, PAD), bf16),
            jax.ShapeDtypeStruct((nt, 2, 2, rows, PAD), bf16),
            jax.ShapeDtypeStruct((width, 3 * PAD), bf16),
        ],
        compiler_params=params(LIMIT, 2),
        cost_estimate=cost(
            2 * nt * 3 * 5 * 2 * rows * 2 * rows * 256, 5 * nt * MIB, 2 * nt * 3 * rows * 2 * rows
        ),
        name="attn_bwd",
    )(
        tlist,
        q,
        k4,
        v4,
        g,
        o,
        lo,
        x,
        cols_k,
        cos.reshape(2 * rows, 128),
        sin.reshape(2 * rows, 128),
        normed.reshape(2, 2, rows, width),
        wat,
    )


RB = 512
LAST_RB = 256


def dot_tn(a, b):
    return lax.dot_general(a, b, (((0,), (0,)), ((), ())), preferred_element_type=f32)


def normalise(h):
    mean = jnp.mean(h, axis=-1, keepdims=True)
    cent = h - mean
    var = jnp.mean(cent * cent, axis=-1, keepdims=True)
    rstd = lax.rsqrt(var + NORM_EPS)
    return cent * rstd, rstd


def block_kernel(
    flag_ref,
    mix_ref,
    wout_ref,
    hid_ref,
    vec_ref,
    cot_ref,
    mask_ref,
    ub_ref,
    ff_ref,
    out_ref,
    dh_ref,
    mg_ref,
    sum_ref,
    wff_ref,
    wat_ref,
    up_ref,
    dn_ref,
    x_ref,
    g_ref,
    bl_ref,
    mine_ref,
    act_ref,
    ul_ref,
    acts_ref,
    uls_ref,
    h1_ref,
    br_ref,
    d_ref,
    n_ref,
    sem,
):
    step = pl.program_id(0)
    steps = pl.num_programs(0)
    own = flag_ref[0]
    width = hid_ref.shape[1]
    tn = ff_ref.shape[0]
    ff = ub_ref.shape[2]
    here = pl.ds(pl.multiple_of(step * RB, RB), RB)

    def fetch(j):
        cols = pl.ds(pl.multiple_of(j * ff, ff), ff)
        return (
            pltpu.make_async_copy(ff_ref.at[j, :, 0:ff], up_ref.at[:, cols], sem.at[2 * j]),
            pltpu.make_async_copy(ff_ref.at[j, :, ff : 2 * ff], dn_ref.at[:, cols], sem.at[2 * j + 1]),
        )

    @pl.when(step == 0)
    def _():
        for j in range(tn):
            for copy in fetch(j):
                copy.start()

    gate1, gain2, shift2 = vec_ref[0, 0:1, :], vec_ref[0, 1:2, :], vec_ref[0, 2:3, :]
    gate2, dbias = vec_ref[0, 3:4, :], vec_ref[0, 4:5, :]
    acc = dot_nt(mix_ref[:, 0:PAD], wout_ref[0])
    for t in range(1, tn):
        acc += dot_nt(mix_ref[:, t * PAD : (t + 1) * PAD], wout_ref[t])
    br_ref[...] = acc
    h1 = hid_ref[...].astype(f32) + gate1 * acc
    h1_ref[...] = h1
    n, _ = normalise(h1)
    x = (n * gain2 + shift2).astype(bf16)
    x_ref[here, :] = x
    cot = cot_ref[...].astype(f32) * mask_ref[...]
    g = (cot * gate2).astype(bf16)
    g_ref[here, :] = g
    mine_ref[here, :] = mix_ref[:, pl.ds(pl.multiple_of(own * PAD, PAD), PAD)]

    def units(j, carry):
        @pl.when(step == 0)
        def _():
            for copy in fetch(j):
                copy.wait()

        cols = pl.ds(pl.multiple_of(j * ff, ff), ff)
        u = dot_nn(x_ref[here, :], up_ref[:, cols]) + ub_ref[lax.rem(own - j + tn, tn)]
        da = dot_nn(g_ref[here, :], dn_ref[:, cols])
        u2 = u * u
        th = jnp.tanh(GELU_C * u * (1.0 + 0.044715 * u2))
        half_up = 0.5 * (1.0 + th)
        slope = half_up + (0.5 * GELU_C) * u * (1.0 - th * th) * (1.0 + (3 * 0.044715) * u2)
        acts_ref[:, cols] = (u * half_up).astype(bf16)
        uls_ref[:, cols] = (da * slope).astype(bf16)
        return carry

    lax.fori_loop(0, tn, units, 0)
    mine = pl.ds(pl.multiple_of(own * ff, ff), ff)
    act_ref[here, :] = acts_ref[:, mine]
    ul_ref[here, :] = uls_ref[:, mine]
    for c in range(0, width, PAD):
        cols = slice(c, c + PAD)
        d_ref[:, cols] = dot_nt(acts_ref[...], dn_ref[cols, :])
        n_ref[:, cols] = dot_nt(uls_ref[...], up_ref[cols, :])

    down = d_ref[...] + dbias
    h1 = h1_ref[...]
    out_ref[...] = (h1 + gate2 * down).astype(bf16)
    n, rstd = normalise(h1)
    grad = n_ref[...]
    gn = grad * n
    e = grad * gain2
    en = gn * gain2
    dh = cot + rstd * (
        e - jnp.mean(e, axis=-1, keepdims=True) - n * jnp.mean(en, axis=-1, keepdims=True)
    )
    dh_ref[...] = dh
    bl = (dh * gate1).astype(bf16)
    bl_ref[here, :] = bl
    for t in range(tn):
        mg_ref[:, t * PAD : (t + 1) * PAD] = dot_nn(bl, wout_ref[t]).astype(bf16)

    @pl.when(lax.rem(step, steps // 2) == 0)
    def _():
        sum_ref[...] = jnp.zeros_like(sum_ref)

    parts = (cot * down, cot, grad, gn, dh * br_ref[...], uls_ref[:, mine].astype(f32))
    for r, part in enumerate(parts):
        sum_ref[0, r : r + 1, :] += jnp.sum(part, axis=0, keepdims=True)

    @pl.when(step == steps - 1)
    def _():
        def column(c, carry):
            cols = pl.ds(pl.multiple_of(c * PAD, PAD), PAD)
            wff_ref[:, cols] = dot_tn(x_ref[...], ul_ref[:, cols])
            far = pl.ds(pl.multiple_of(ff + c * PAD, PAD), PAD)
            wff_ref[:, far] = dot_tn(g_ref[...], act_ref[:, cols])
            return carry

        lax.fori_loop(0, ff // PAD, column, 0)
        wat_ref[...] = dot_tn(bl_ref[...], mine_ref[...]).astype(bf16)


def block_call(flags, mixed, w_out, hid, vec, cot, mask_col, w_ff, up_bias):
    rows, wide = mixed.shape
    width = hid.shape[1]
    tn, _, ff = w_ff.shape
    ff = ff // 2
    one = pl.Buffered(1)
    steps = rows // RB
    row = lambda w: pl.BlockSpec((RB, w), lambda i, o: (i, 0))
    vecs = pl.BlockSpec((1, 8, width), lambda i, o: (i // (steps // 2), 0, 0))
    tokens = lambda dtype, w, n=rows: pltpu.VMEM((n, w), dtype)
    return pl.pallas_call(
        block_kernel,
        grid_spec=pltpu.PrefetchScalarGridSpec(
            num_scalar_prefetch=1,
            grid=(steps,),
            in_specs=[
                row(wide),
                whole((tn, width, PAD), pipeline_mode=one),
                row(width),
                vecs,
                row(width),
                row(1),
                whole((tn, 1, ff), pipeline_mode=one),
                pl.BlockSpec(memory_space=pl.ANY),
            ],
            out_specs=[
                row(width),
                row(width),
                row(wide),
                vecs,
                whole((width, 2 * ff), pipeline_mode=one),
                whole((width, PAD), pipeline_mode=one),
            ],
            scratch_shapes=[
                tokens(bf16, tn * ff, width),
                tokens(bf16, tn * ff, width),
                tokens(bf16, width),
                tokens(bf16, width),
                tokens(bf16, width),
                tokens(bf16, PAD),
                tokens(bf16, ff),
                tokens(bf16, ff),
                tokens(bf16, tn * ff, RB),
                tokens(bf16, tn * ff, RB),
                tokens(f32, width, RB),
                tokens(f32, width, RB),
                tokens(f32, width, RB),
                tokens(f32, width, RB),
                pltpu.SemaphoreType.DMA((2 * tn,)),
            ],
        ),
        out_shape=[
            jax.ShapeDtypeStruct((rows, width), bf16),
            jax.ShapeDtypeStruct((rows, width), f32),
            jax.ShapeDtypeStruct((rows, wide), bf16),
            jax.ShapeDtypeStruct((2, 8, width), f32),
            jax.ShapeDtypeStruct((width, 2 * ff), f32),
            jax.ShapeDtypeStruct((width, PAD), bf16),
        ],
        compiler_params=params(LIMIT),
        cost_estimate=cost(
            4 * 2 * rows * width * ff * tn + 8 * rows * width * width, 32 * MIB, rows * ff * tn
        ),
        name="block_both",
    )(flags, mixed, w_out, hid, vec, cot, mask_col, up_bias, w_ff)


def table_kernel(flag_ref, seg_ref, cos_ref, sin_ref, sq_ref, sk_ref):
    rows = seg_ref.shape[3]
    lane = lax.broadcasted_iota(jnp.int32, (rows, 128), 1)
    fixed = lane >= 128 - 3
    pair = (lane & (HEAD_DIM // 2 - 1)).astype(f32)
    freq = jnp.exp(pair * (-2.0 * math.log(10000.0) / HEAD_DIM))
    sign = jnp.where((lane & (HEAD_DIM - 1)) < HEAD_DIM // 2, -1.0, 1.0)
    row = lax.broadcasted_iota(jnp.int32, (rows, 128), 0)
    for half in range(2):
        angle = (row + flag_ref[half]).astype(f32) * freq
        cos_ref[half] = jnp.cos(angle)
        sin_ref[half] = jnp.sin(angle) * sign
        for m in range(2):
            ids = jnp.broadcast_to(seg_ref[m, half].astype(f32), (128, rows)).T
            same = (ids == lane.astype(f32)) | fixed
            sk_ref[m, half] = jnp.where(same, 1.0, 0.0).astype(bf16)
            if half == 0:
                sq_ref[m] = jnp.where(same, 0.0, NEG).astype(bf16)


def table_call(starts, segments):
    _, _, _, rows = segments.shape
    cos, sin, cols_q, cols_k = pl.pallas_call(
        table_kernel,
        grid_spec=pltpu.PrefetchScalarGridSpec(
            num_scalar_prefetch=1,
            grid=(1,),
            in_specs=[whole(segments.shape)],
            out_specs=[
                whole((2, rows, 128)),
                whole((2, rows, 128)),
                whole((2, rows, 128)),
                whole((2, 2, rows, 128)),
            ],
        ),
        out_shape=[
            jax.ShapeDtypeStruct((2, rows, 128), f32),
            jax.ShapeDtypeStruct((2, rows, 128), f32),
            jax.ShapeDtypeStruct((2, rows, 128), bf16),
            jax.ShapeDtypeStruct((2, 2, rows, 128), bf16),
        ],
        compiler_params=params(LIMIT),
        cost_estimate=cost(100 * 2 * rows * 128, 3 * MIB),
        name="tables",
    )(starts, segments)
    return cos, sin, cols_q, cols_k.reshape(2, 2 * rows, 128)


def last_kernel(
    flag_ref,
    dq_ref,
    kv_ref,
    rv_ref,
    hid_ref,
    dh_ref,
    vec_ref,
    early_ref,
    *refs,
):
    out_ref, sum_ref, w_ref, d_ref, acc_ref = refs[-5:]
    first = pl.program_id(1) == 0
    own = flag_ref[0]
    tn = dq_ref.shape[0]

    @pl.when(first & (pl.program_id(0) == 0))
    def _():
        for t in range(tn):
            cols = pl.ds(3 * PAD * t, 3 * PAD)
            lay_weight(flag_ref, t, tn, refs[:-5], w_ref.at[:, cols], False)

    for t in range(tn):
        slot = lax.rem(t - own + tn, tn)
        at = 3 * PAD * t
        d_ref[:, at : at + PAD] = dq_ref[slot, 0]
        for j in range(2):
            at += PAD
            d = kv_ref[slot, j, 0].astype(f32) + rv_ref[slot, j, 0].astype(f32)
            d_ref[:, at : at + PAD] = d.astype(bf16)
    width = hid_ref.shape[2]
    for c in range(0, width, PAD):
        acc_ref[:, c : c + PAD] = dot_nt(d_ref[...], w_ref[c : c + PAD, :])
    acc = acc_ref[...]
    gain1 = vec_ref[0, 5:6, :]
    n, rstd = normalise(hid_ref[0].astype(f32))
    gn = acc * n
    e = acc * gain1
    en = gn * gain1
    out_ref[0] = dh_ref[0] + rstd * (
        e - jnp.mean(e, axis=-1, keepdims=True) - n * jnp.mean(en, axis=-1, keepdims=True)
    )

    @pl.when(first)
    def _():
        sum_ref[0, 0:2, :] = jnp.zeros((2, sum_ref.shape[2]), f32)
        sum_ref[0, 2:8, :] = early_ref[0, 0:6, :]

    sum_ref[0, 0:1, :] += jnp.sum(acc, axis=0, keepdims=True)
    sum_ref[0, 1:2, :] += jnp.sum(gn, axis=0, keepdims=True)


def last_call(flags, dq, kv, rv, weights, hid, dh, vec, early):
    _, rows, width = hid.shape
    tn = dq.shape[0]
    row = pl.BlockSpec((1, LAST_RB, width), lambda m, i, o: (m, i, 0))
    vecs = pl.BlockSpec((1, 8, width), lambda m, i, o: (m, 0, 0))
    q_spec = lambda n: pl.BlockSpec((n, 1, LAST_RB, PAD), lambda m, i, o: (0, m, i, 0))
    kv_spec = lambda n: pl.BlockSpec((n, 2, 1, LAST_RB, PAD), lambda m, i, o: (0, 0, m, i, 0))
    return pl.pallas_call(
        last_kernel,
        grid_spec=pltpu.PrefetchScalarGridSpec(
            num_scalar_prefetch=1,
            grid=(2, rows // LAST_RB),
            in_specs=[
                q_spec(tn),
                kv_spec(tn),
                kv_spec(tn),
                row,
                row,
                vecs,
                vecs,
                *[whole(w.shape, pipeline_mode=pl.Buffered(1)) for w in weights],
            ],
            out_specs=[row, vecs],
            scratch_shapes=[
                pltpu.VMEM((width, tn * 3 * PAD), bf16),
                pltpu.VMEM((LAST_RB, tn * 3 * PAD), bf16),
                pltpu.VMEM((LAST_RB, width), f32),
            ],
        ),
        out_shape=[
            jax.ShapeDtypeStruct((2, rows, width), f32),
            jax.ShapeDtypeStruct((2, 8, width), f32),
        ],
        compiler_params=params(LIMIT, 2),
        cost_estimate=cost(2 * 2 * rows * width * tn * 3 * PAD, 24 * MIB),
        name="first_norm_bwd",
    )(flags, dq, kv, rv, hid, dh, vec, early, *weights)


def split_terms(x):
    hi = x.astype(bf16)
    rest = x - hi.astype(f32)
    mid = rest.astype(bf16)
    return [hi, mid, (rest - mid.astype(f32)).astype(bf16)]


def finish_kernel(flag_ref, sums_ref, mod_ref, norm_ref, cond_ref, ada_ref, *refs):
    gada_ref, gadab_ref, gcond_ref, gn1_ref, gn2_ref, gdb_ref, gub_ref, all_ref = refs
    group, ada_cols, _ = ada_ref.shape
    width = sums_ref.shape[2]
    place = flag_ref[0]
    norm_one, norm_two = norm_ref[0:1, :], norm_ref[1:2, :]
    one = jnp.zeros((1, width), f32)
    small = [one, one, one, one]
    for f in range(group // 2):
        for m in range(2):
            s = 2 * f + m
            r = sums_ref[4 * f + m] + sums_ref[4 * f + 2 + m]
            r = [r[i : i + 1, :] for i in range(8)]
            parts = (r[0], r[1] * norm_one, r[6], r[4], r[5] * norm_two, r[2])
            for i, part in enumerate(parts):
                all_ref[s : s + 1, i * width : (i + 1) * width] = part
            scale_one, scale_two, gate_two = (
                mod_ref[s : s + 1, i * width : (i + 1) * width] for i in (1, 4, 5)
            )
            terms = (r[1] * (1.0 + scale_one), r[5] * (1.0 + scale_two), r[3] * gate_two, r[7])
            small = [total + term for total, term in zip(small, terms)]

    def own_columns(x, count):
        total = x.shape[1]
        return pltpu.roll(x, lax.rem(total - place * count, total), 1)[:, :count]

    for ref, total in zip((gn1_ref, gn2_ref, gdb_ref, gub_ref), small):
        shard = ref.shape[0]
        ref[...] = own_columns(jnp.broadcast_to(total, (8, width)), shard)[0]
    mine = own_columns(all_ref[...], ada_cols)
    gadab_ref[...] = jnp.sum(mine, axis=0)
    cond = cond_ref[...]
    terms = split_terms(mine)
    gada_ref[...] = dot_tn(terms[0], cond) + dot_tn(terms[1], cond) + dot_tn(terms[2], cond)
    total = jnp.zeros((8, cond.shape[1]), f32)
    seqs = all_ref[pl.ds(pl.multiple_of(flag_ref[1] * 8, 8), 8), :]
    for term in split_terms(seqs):
        for c in range(group):
            total += dot_nn(term[:, c * ada_cols : (c + 1) * ada_cols], ada_ref[c])
    for i in range(4):

        @pl.when(flag_ref[2] == i)
        def _():
            gcond_ref[...] = total[2 * i : 2 * i + 2]


def finish_call(flags, sums, mod_all, norms, cond, ada):
    group, ada_cols, cond_w = ada.shape
    shard = sums.shape[2] // group
    out = [(ada_cols, cond_w), (ada_cols,), (2, cond_w)] + [(shard,)] * 4
    return pl.pallas_call(
        finish_kernel,
        grid_spec=pltpu.PrefetchScalarGridSpec(
            num_scalar_prefetch=1,
            grid=(1,),
            in_specs=[whole(x.shape) for x in (sums, mod_all, norms, cond, ada)],
            out_specs=[whole(x) for x in out],
            scratch_shapes=[pltpu.VMEM(mod_all.shape, f32)],
        ),
        out_shape=[jax.ShapeDtypeStruct(x, f32) for x in out],
        compiler_params=params(LIMIT),
        cost_estimate=cost(1 << 20, 3 * MIB),
        name="finish",
    )(flags, sums, mod_all, norms, cond, ada)


def spread(x, axes):
    count = lax.axis_size(axes)
    many = jnp.broadcast_to(x[None], (count,) + x.shape)
    return lax.all_to_all(many, axes, split_axis=0, concat_axis=0, tiled=True)


def join_cores(part, other, rank):
    fs, tn, rows, width = part.shape
    both = jnp.stack([jnp.where(rank == 0, part, other), jnp.where(rank == 0, other, part)], axis=1)
    return both.transpose(2, 0, 1, 3, 4).reshape(1, tn, fs * 2 * rows, width)


def gather_rows(row):
    tn = lax.axis_size("tp")
    got = [row]
    for step in range(1, tn):
        got.append(lax.ppermute(row, "tp", [(i, (i + step) % tn) for i in range(tn)]))
    return jnp.stack(got).astype(f32)


def exchange_to_shard(grad):
    group = lax.axis_size(FC)
    parts = grad.reshape(group, -1, grad.shape[1])
    return lax.all_to_all(parts, FC, split_axis=0, concat_axis=0, tiled=True)


def on_device(
    hidden_in,
    cond_vec,
    segment_ids,
    pad_mask,
    out_cot,
    qkv_weight,
    attn_weight,
    up_weight,
    up_bias,
    down_weight,
    down_bias,
    ada_weight,
    ada_bias,
    attn_norm,
    mlp_norm,
):
    rank = lax.axis_index("ctx")
    own = lax.axis_index("tp")
    fs = lax.axis_size("fsdp")
    tn = lax.axis_size("tp")
    hid = hidden_in[:, 0]
    _, rows, width = hid.shape
    shard = qkv_weight.shape[1]
    heads_w = qkv_weight.shape[2]
    cond_w = cond_vec.shape[2]
    highest = lax.Precision.HIGHEST

    w_attn_shard = pack_weights(qkv_weight, attn_weight)
    ada_cols = ada_bias.shape[0]
    extra = [cond_vec[:, 0]]
    up_rows = gather_rows(jnp.pad(up_bias, (0, cond_w - shard)).reshape(1, cond_w)).astype(bf16)
    for x in (down_bias, attn_norm, mlp_norm, up_rows.reshape(-1), ada_bias):
        extra.append(jnp.pad(x, (0, -x.shape[0] % cond_w)).reshape(-1, cond_w))
    extra = jnp.concatenate(extra, axis=0)
    ada_rows = jnp.concatenate([ada_weight.T, extra], axis=0)
    ada_rows = jnp.pad(ada_rows, ((0, -ada_rows.shape[0] % 16), (0, 0)))
    w_ff = jnp.concatenate([up_weight, down_weight.T], axis=1)
    w_ff = lax.all_gather(w_ff, ("tp",) + FC, axis=0, tiled=True).reshape(tn, width, -1)
    ada_rows = spread(ada_rows, FC)
    along = lax.all_gather(w_attn_shard, "tp", axis=0, tiled=False)
    in_parts = fs == 4 and tn % 2 == 0 and shard % 16 == 0
    if in_parts:
        lower, upper = along[: tn // 2], along[tn // 2 :]
        x_lower = lax.ppermute(lower, "fsdp", ALONG_X)
        y_upper = lax.ppermute(upper, "fsdp", ALONG_Y)
        x_upper = lax.ppermute(upper, "fsdp", ALONG_X)
        y_lower = lax.ppermute(lower, "fsdp", ALONG_Y)

    ada_full = ada_rows[:, :ada_cols]
    small = ada_rows[:, ada_cols:]
    cond_all = small[:, :2].reshape(fs, 2, 2, cond_w)[:, 0]
    modulation_all = jnp.einsum(
        "smk,fck->smfc", cond_all, ada_full, preferred_element_type=f32
    ).reshape(fs, 2, -1)
    small = small.astype(f32)
    dnb_full = small[:, 2, :shard].reshape(-1)
    norm_one = small[:, 3, :shard].reshape(-1)
    norm_two = small[:, 4, :shard].reshape(-1)
    upb_full = small[:, 5 : 5 + tn, :shard].transpose(1, 0, 2).reshape(tn, 1, -1)
    adab_full = small[:, 5 + tn :].reshape(2 * fs, -1)[:, :ada_cols].reshape(-1)
    modulation_all = modulation_all + adab_full
    modulation = lax.dynamic_index_in_dim(modulation_all, lax.axis_index("fsdp"), 0, keepdims=False)
    shift_one, scale_one, gate_one, shift_two, scale_two, gate_two = jnp.split(modulation, 6, axis=1)
    gain_one = norm_one * (1.0 + scale_one)
    gain_two = norm_two * (1.0 + scale_two)
    zero = jnp.zeros_like(gain_one)
    vec = jnp.stack(
        [
            gate_one,
            gain_two,
            shift_two,
            gate_two,
            jnp.broadcast_to(dnb_full, gain_one.shape),
            gain_one,
            shift_one,
            zero,
        ],
        axis=1,
    )

    hid_other = lax.ppermute(hid, "ctx", SWAP)
    seg = segment_ids[:, 0]
    halves = jnp.where(rank == 0, seg.reshape(2, 2, 1, rows), seg.reshape(2, 2, 1, rows)[:, ::-1])
    starts = jnp.stack([rank * rows, (1 - rank) * rows]).astype(jnp.int32)
    cos, sin, cols_q, cols_k = table_call(starts, halves)
    mask = lax.dynamic_slice_in_dim(pad_mask[:, 0], rank * rows, rows, axis=1).astype(f32)
    cot = out_cot[:, 0]

    if in_parts:
        d_lower = lax.ppermute(x_lower, "fsdp", ALONG_Y)
        d_upper = lax.ppermute(y_upper, "fsdp", ALONG_X)
        w_attn = [along, x_lower, x_upper, y_lower, y_upper, d_lower, d_upper]
        w_attn = w_attn + [lax.ppermute(part, "ctx", SWAP) for part in w_attn]
    else:
        w_own = spread(along, "fsdp")
        w_own = join_cores(w_own, lax.ppermute(w_own, "ctx", SWAP), rank)
        w_attn = [w_own[:, :, : width // 2], w_own[:, :, width // 2 :]]
    sources = lax.axis_index("fsdp") ^ jnp.arange(4, dtype=jnp.int32)
    flags = jnp.concatenate(
        [own.reshape(1), jnp.zeros((1,), jnp.int32), 2 * sources + rank, 2 * sources + 1 - rank]
    ).astype(jnp.int32)
    q, k, v, w_out, normed_all = qkv_call(flags, tn, hid, hid_other, vec, w_attn, cos, sin)
    mixed, mixed_lo, score_cols = attn_fwd_call(q, k, v, cols_q, cols_k)

    own_index = own.reshape(1).astype(jnp.int32)
    flat = lambda x: x.reshape(2 * rows, -1)
    block_out, dh_one, mixed_grad, sums_two, ff_low, attn_low = block_call(
        flags,
        flat(mixed),
        w_out,
        flat(hid),
        vec,
        flat(cot),
        mask.reshape(-1, 1),
        w_ff,
        upb_full,
    )
    mixed_grad = mixed_grad.reshape(2, rows, -1)
    ff_low, mixed_grad = lax.optimization_barrier((ff_low, mixed_grad))
    ff_shard = lax.psum_scatter(ff_low, FC, scatter_dimension=0, tiled=True)

    order = lax.rem(own + jnp.arange(tn, dtype=jnp.int32), tn).astype(jnp.int32)
    dq, kv_own, kv_send, proj_low = attn_bwd_call(
        order, mixed_grad, q, k, v, mixed, mixed_lo, score_cols, cols_k, cos, sin, normed_all, attn_low
    )

    kv_send, proj_low = lax.optimization_barrier((kv_send, proj_low))
    kv_got = lax.ppermute(kv_send, "ctx", SWAP)
    proj_got = exchange_to_shard(proj_low)

    hidden_grad, sums_one = last_call(
        flags, dq, kv_own, kv_got, w_attn, hid, dh_one.reshape(hid.shape), vec, sums_two
    )

    all_sums = lax.all_gather(sums_one, FC, axis=0, tiled=True)
    all_sums, proj_got, ff_shard = lax.optimization_barrier((all_sums, proj_got, ff_shard))
    seq = lax.axis_index("fsdp")
    finish_flags = jnp.stack([lax.axis_index(FC), seq // 4, seq % 4]).astype(jnp.int32)
    grads = finish_call(
        finish_flags,
        all_sums,
        modulation_all.reshape(2 * fs, -1),
        jnp.stack([norm_one, norm_two]),
        cond_all.reshape(2 * fs, cond_w),
        ada_full,
    )
    grad_ada, grad_adabias, cond_grad, attnnorm, mlpnorm, downbias, upbias = grads
    attn_shard = jnp.sum(proj_got.astype(f32), axis=0)

    grad_qkv = jnp.stack([attn_shard[:, j * PAD : j * PAD + heads_w] for j in range(3)])
    grad_attn = jnp.concatenate(
        [attn_shard[:, j * PAD + heads_w : (j + 1) * PAD] for j in range(3)], axis=1
    ).T
    return (
        block_out.reshape(hidden_in.shape),
        hidden_grad[:, None],
        cond_grad[:, None],
        grad_qkv,
        grad_attn,
        ff_shard[:, : ff_shard.shape[1] // 2],
        upbias,
        ff_shard[:, ff_shard.shape[1] // 2 :].T,
        downbias,
        grad_ada.T,
        grad_adabias,
        attnnorm,
        mlpnorm,
    )


def solution(mesh):
    tokens = P(None, "fsdp", "ctx", None)
    per_seq = P(None, "fsdp", None)
    weights = (
        P(None, FC, "tp"),
        P("tp", FC),
        P(FC, "tp"),
        P(("tp",) + FC),
        P("tp", FC),
        P(FC),
        P(None, FC),
        P(FC),
        P(FC),
        P(FC),
    )
    return jax.shard_map(
        on_device,
        mesh=mesh,
        in_specs=(tokens, per_seq, per_seq, per_seq, tokens) + weights,
        out_specs=(tokens, tokens, per_seq) + weights,
        check_vma=False,
    )
```
